32 devices in a mesh: wide: 8 (over z, x), narrow: 4 (over y, core).
Axes of the slice: x: 2, y: 2, z: 4, core: 2. Of those that a mesh axis runs over, the one named last changes fastest.
Arguments:
- patches: bfloat16 [8192, 768], P(('wide', 'narrow')), may hold values from -6 to 6
- cotangent: float32 [8192, 768], P(('wide', 'narrow')), may hold values from -6 to 6
- mask_index: int32 [16, 450], P('wide'), may hold values from 0 to 511, as said below
- mask_count: int32 [16], P('wide'), may hold values from 100 to 450, as said below
- weights: float32 [2, 12, 768, 768], P(None, None, 'wide', 'narrow')
- first_moment: float32 [2, 12, 768, 768], P(None, None, 'wide', 'narrow'), may hold values from -0.0004272461 to 0.0004272461
- second_moment: float32 [2, 12, 768, 768], P(None, None, 'wide', 'narrow'), may hold values from 3.532127e-11 to 5.651403e-10
- small_params: float32 [5, 768], P(None, 'wide')
- small_first: float32 [5, 768], P(None, 'wide'), may hold values from -0.0012207031 to 0.0012207031
- small_second: float32 [5, 768], P(None, 'wide'), may hold values from 3.1789144e-10 to 5.086263e-09
Outputs:
- block_output: float32 [8192, 768], P(('wide', 'narrow'))
- input_grad: float32 [8192, 768], P(('wide', 'narrow'))
- new_weights: float32 [2, 12, 768, 768], P(None, None, 'wide', 'narrow')
- new_first: float32 [2, 12, 768, 768], P(None, None, 'wide', 'narrow')
- new_second: float32 [2, 12, 768, 768], P(None, None, 'wide', 'narrow')
- new_small: float32 [5, 768], P(None, 'wide')
- new_small_first: float32 [5, 768], P(None, 'wide')
- new_small_second: float32 [5, 768], P(None, 'wide')
- grad_norm: float32 [], replicated
The draws below stay inside these ranges and needn't reach their ends.
Inputs may be any that keep to these rules, and one draw needn't show every extreme that they name: `mask_index`: row c lists 450 distinct patch positions of clip c; its first mask_count[c] entries are the masked patches, the rest are not masked. `mask_count`: some clip has exactly 450 masked patches and another exactly 100.
All inputs are finite; a program needn't handle non-finite values.
Results may differ from the reference program's by a relative error of at most 0.02.
Values may be sent and summed in bfloat16 or wider, within the bound.
A program may use at most 192 MiB of HBM per device.

```python
import math
import jax
import jax.numpy as jnp
from jax import lax

D = 768
HEADS = 12
HD = 64
LAYERS = 2
SEQ = 512
CLIPS_DEV = 2
MAXM = 450
MINM = 100
STEP = 10
CLIPS = 16
TOKENS = 8192
SMALL = 5
N_WIDE = 8


def mask_lists(key):
    base = jax.random.fold_in(key, 17)
    order_keys = jax.random.split(jax.random.fold_in(base, 1), CLIPS)
    orders = jax.vmap(lambda one_key: jax.random.permutation(one_key, SEQ))(order_keys)
    index_rows = orders[:, :MAXM].astype(jnp.int32)
    counts = jax.random.randint(jax.random.fold_in(base, 2), (CLIPS,), MINM, MAXM + 1)
    top_clip = jax.random.randint(jax.random.fold_in(base, 3), (), 0, CLIPS)
    low_clip = (top_clip + 1 + jax.random.randint(jax.random.fold_in(base, 4), (), 0, CLIPS - 1)) % CLIPS
    clip_ids = jnp.arange(CLIPS)
    counts = jnp.where(clip_ids == top_clip, MAXM, jnp.where(clip_ids == low_clip, MINM, counts))
    return (index_rows, counts.astype(jnp.int32))


def draw_mask_index(key, part):
    return mask_lists(key)[0]


def draw_mask_count(key, part):
    return mask_lists(key)[1]


def draw_weights(key, part):
    values = jax.random.normal(jax.random.fold_in(key, 5), (LAYERS, 12, D, D), jnp.float32) * D ** (-0.5)
    slot_scale = jnp.where(jnp.arange(12) == 3, 4.0, 1.0).astype(jnp.float32)
    return values * slot_scale[None, :, None, None]


def draw_small_params(key, part):
    gains = jax.random.uniform(jax.random.fold_in(key, 6), (2 * LAYERS, D), jnp.float32, 0.6, 1.4)
    embed = jnp.clip(jax.random.normal(jax.random.fold_in(key, 7), (1, D), jnp.float32), -4.0, 4.0)
    return jnp.concatenate([gains, embed], axis=0)


def block_levels(own_key, dims, shards, low, top_value):
    def one(position, shards_of):
        heights = jax.random.uniform(jax.random.fold_in(jax.random.fold_in(own_key, 6), position), (shards_of,), jnp.float32, low / len(shards), top_value / len(shards))
        return jnp.repeat(jnp.exp(heights), dims[position] // shards_of).reshape((-1,) + (1,) * (len(dims) - position - 1))

    loudness = one(*shards[0])
    for cut in shards[1:]:
        loudness = loudness * one(*cut)
    return loudness


def gaussian(rng, shape, scale, most, pieces=(), kind=jnp.bfloat16):
    entries = jax.random.normal(rng, shape, jnp.float32) * scale
    if len(pieces) > 0:
        entries = block_levels(rng, shape, pieces, -0.22, 0.18) * entries
    return jnp.clip(entries, min=-most, max=most).astype(kind)


def setup_inputs(seed: int = 0) -> dict:
    key_list = jax.random.split(jax.random.key(seed), 11)
    patches = gaussian(key_list[0], (TOKENS, D), 1.0, 6.0, ((0, 32),))
    cotangent = gaussian(key_list[1], (TOKENS, D), 1.0, 6.0, ((0, 32),), jnp.float32)
    mask_index = draw_mask_index(jax.random.fold_in(key_list[10], 71), 0)
    mask_count = draw_mask_count(jax.random.fold_in(key_list[10], 71), 0)
    weights = draw_weights(jax.random.fold_in(key_list[10], 71), 0)
    first_moment = gaussian(key_list[5], (LAYERS, 12, D, D), (0.111 * (LAYERS * 12 * D * D) ** -0.5), 0.0004272461, ((2, 8), (3, 4)), jnp.float32)
    second_moment = jnp.clip(jnp.exp(math.log(5.65140323427471e-10) - 2.7725887 * jax.random.uniform(key_list[6], (LAYERS, 12, D, D), jnp.float32) ** block_levels(key_list[6], (LAYERS, 12, D, D), ((2, 8), (3, 4)), -0.2, 0.2)), 3.532127021421694e-11, 5.65140323427471e-10)
    small_params = draw_small_params(jax.random.fold_in(key_list[10], 71), 0)
    small_first = gaussian(key_list[8], (SMALL, D), (0.333 * (LAYERS * 12 * D * D) ** -0.5), 0.0012207031, ((1, 8),), jnp.float32)
    small_second = jnp.clip(jnp.exp(math.log(5.08626296635839e-09) - 2.7725887 * jax.random.uniform(key_list[9], (SMALL, D), jnp.float32) ** block_levels(key_list[9], (SMALL, D), ((1, 8),), -0.2, 0.2)), 3.178914353973994e-10, 5.08626296635839e-09)
    return dict(patches=patches, cotangent=cotangent, mask_index=mask_index, mask_count=mask_count, weights=weights, first_moment=first_moment, second_moment=second_moment, small_params=small_params, small_first=small_first, small_second=small_second)


@jax.custom_vjp
def low(v):
    return lax.optimization_barrier(v.astype(jnp.bfloat16)).astype(jnp.float32)

@jax.custom_vjp
def low_back(v):
    return v

def low_keep(v):
    return (low(v), None)

def low_pass(kept, grad):
    return (grad,)

def back_keep(v):
    return (v, None)

def back_low(kept, grad):
    return (low(grad),)
low.defvjp(low_keep, low_pass)
low_back.defvjp(back_keep, back_low)
EPS_NORM = 1e-06
BETA_ONE = 0.9
BETA_TWO = 0.999
EPS_ADAM = 1e-08
DECAY_RATE = 0.05
RATE_SMALL = 0.6
CLIP_MAX = 1.0

def matmul(left, right):
    return jnp.dot(left, right, precision=lax.Precision.HIGHEST, preferred_element_type=jnp.float32)

def layer_norm(values, gain):
    centre = values - lax.optimization_barrier(jnp.mean(values, axis=-1, keepdims=True))
    spread = lax.optimization_barrier(jnp.mean(centre * centre, axis=-1, keepdims=True))
    return centre * lax.rsqrt(spread + EPS_NORM) * gain

def attend(queries, key_rows, value_rows):
    scores = jnp.einsum('cqhd,ckhd->chqk', queries, key_rows, precision=lax.Precision.HIGHEST) * HD ** (-0.5)
    scores = low_back(scores)
    probs = jax.nn.softmax(scores, axis=-1)
    return jnp.einsum('chqk,ckhd->cqhd', low(probs), value_rows, precision=lax.Precision.HIGHEST)

def layer(stream, weight, gain_one, gain_two):
    all_rows = stream.shape[0]
    clip_count = all_rows // SEQ

    def heads(values):
        return values.reshape(clip_count, SEQ, HEADS, HD)
    normed = low(layer_norm(stream, gain_one))
    queries = low(low_back(matmul(normed, weight[0])))
    key_rows = low(low_back(matmul(normed, weight[1])))
    value_rows = low(low_back(matmul(normed, weight[2])))
    mixture = low(low_back(attend(heads(queries), heads(key_rows), heads(value_rows)).reshape(all_rows, D)))
    resid_one = stream + low_back(matmul(mixture, weight[3].T))
    normed_two = low(layer_norm(resid_one, gain_two))
    upward = low_back(jnp.concatenate([matmul(normed_two, weight[4 + block]) for block in range(4)], axis=1))
    hidden = low(jax.nn.gelu(upward, approximate=False))
    down = matmul(hidden[:, 0:D], weight[8].T)
    for block in range(1, 4):
        down = down + matmul(hidden[:, block * D:(block + 1) * D], weight[8 + block].T)
    return resid_one + low_back(down)

def forward(weight_in, small_in, patch_rows, flags):
    matrices = low(weight_in)
    gains = low(small_in)
    stream = patch_rows * (1.0 - flags) + flags * gains[2 * LAYERS][None, :]
    for layer_idx in range(LAYERS):
        stream = layer(stream, matrices[layer_idx], gains[2 * layer_idx], gains[2 * layer_idx + 1])
    return stream

def mask_flags(index_rows, count_rows):
    positions = jnp.arange(SEQ, dtype=jnp.int32)
    slots = jnp.arange(index_rows.shape[1], dtype=jnp.int32)
    live = slots[None, :] < count_rows[:, None]
    hits = (index_rows[:, :, None] == positions[None, None, :]) & live[:, :, None]
    return jnp.any(hits, axis=1).astype(jnp.float32).reshape(-1)

def adam_step(weight_in, moment_one, moment_two, gradient, step_rate, decay_rate):
    moment_one = BETA_ONE * moment_one + (1.0 - BETA_ONE) * gradient
    moment_two = BETA_TWO * moment_two + (1.0 - BETA_TWO) * gradient * gradient
    first_hat = moment_one / (1.0 - BETA_ONE ** STEP)
    second_hat = moment_two / (1.0 - BETA_TWO ** STEP)
    updated = weight_in - step_rate * (first_hat / (jnp.sqrt(second_hat) + EPS_ADAM) + decay_rate * weight_in)
    return (updated, moment_one, moment_two)

def reference(patches, cotangent, mask_index, mask_count, weights, first_moment, second_moment, small_params, small_first, small_second):
    rows_group = CLIPS_DEV * SEQ
    patch_groups = patches.astype(jnp.float32).reshape(N_WIDE, rows_group, D)
    cot_groups = cotangent.reshape(N_WIDE, rows_group, D)
    index_groups = mask_index.reshape(N_WIDE, CLIPS_DEV, MAXM)
    count_groups = mask_count.reshape(N_WIDE, CLIPS_DEV)

    def one_group(carry, parts):
        patch_rows, cot_rows, index_rows, count_rows = parts
        flags = mask_flags(index_rows, count_rows)[:, None]

        def run(weight_in, small_in, rows_in):
            return forward(weight_in, small_in, rows_in, flags)
        result, pullback = jax.vjp(run, weights, small_params, patch_rows)
        grad_weight, grad_small, grad_patch = pullback(cot_rows)
        return ((carry[0] + grad_weight, carry[1] + grad_small), (result, grad_patch))
    start = (jnp.zeros_like(weights), jnp.zeros_like(small_params))
    sums, outputs = lax.scan(one_group, start, (patch_groups, cot_groups, index_groups, count_groups))
    grad_matrix, grad_small = sums
    block_output = outputs[0].reshape(-1, D)
    input_grad = outputs[1].reshape(-1, D)
    grad_norm = jnp.sqrt(jnp.sum(grad_matrix * grad_matrix) + jnp.sum(grad_small * grad_small))
    factor = jnp.minimum(1.0, CLIP_MAX / grad_norm)
    new_weights, new_first, new_second = adam_step(weights, first_moment, second_moment, grad_matrix * factor, D ** (-0.5), DECAY_RATE)
    new_small, new_small_first, new_small_second = adam_step(small_params, small_first, small_second, grad_small * factor, RATE_SMALL, 0.0)
    return (block_output, input_grad, new_weights, new_first, new_second, new_small, new_small_first, new_small_second, grad_norm)
```

```python
import functools

import jax
import jax.numpy as jnp
from jax import lax
from jax.experimental import pallas as pl
from jax.experimental.pallas import tpu as pltpu
from jax.sharding import PartitionSpec as P

D = 768
HD = 64
LAYERS = 2
SEQ = 512
STEP = 10

EPS_NORM = 1e-06
BETA_ONE = 0.9
BETA_TWO = 0.999
EPS_ADAM = 1e-08
DECAY_RATE = 0.05
RATE_SMALL = 0.6
CLIP_MAX = 1.0

MESH = pl.DeviceIdType.MESH
F32 = jnp.float32
BF16 = jnp.bfloat16

PAIRS = 12
PER = 6
NZ, NX = 4, 2
ROWS = 96
HALF = 48
COL = 192
WIDE = 2 * COL
SCALE = HD ** (-0.5)
TM = 256
TR = 64
HEADS_Y = COL // HD

LEAD_ONE, LEAD_TWO, LEAD_THREE = 5, 3, 1
LAG_TWO, LAG_THREE, LAG_LAST = 1, 2, 3


def mm(a, b):
    return lax.dot_general(a, b, (((1,), (0,)), ((), ())), preferred_element_type=F32)


def mm_nt(a, b):
    return lax.dot_general(a, b, (((1,), (1,)), ((), ())), preferred_element_type=F32)


def mm_tn(a, b):
    return lax.dot_general(a, b, (((0,), (0,)), ((), ())), preferred_element_type=F32)


def loop(count, body):
    def wrapped(i, carry):
        body(i)
        return carry

    lax.fori_loop(0, count, wrapped, 0)


def rows_at(i, size):
    return pl.ds(pl.multiple_of(i * size, size), size)


def step_kernel(
    wloc, patch, cot, mask_index, mask_count, small,
    out_block, out_igrad, out_grad, out_small, out_norm,
    G, S, R1, NRM, NRM2, QK, V, MIX, GP, HID, GR, ACC, XS, XR, BK, TA, TB, GU, GM, DQK, DV,
    FL, GAIN, GPIECE, SG, SR, NB, RB0Y, RB0X, RB1, RB2,
    ag_s, ag_r, rs_s, rs_r, ex_s, ex_r, in_s, in_r, lc_s, gn_s, gn_r, fs_s, fs_r, nm_s, nm_r,
):
    wide = lax.axis_index("wide")
    narrow = lax.axis_index("narrow")
    z, x = wide // NX, wide % NX
    y, c = narrow // 2, narrow % 2

    dev_core = (wide, 2 * y + 1 - c)
    dev_x = (z * NX + 1 - x, narrow)
    dev_y = (wide, 2 * (1 - y) + c)

    def z_to(k):
        return (z + k) % NZ

    def z_from(k):
        return (z + NZ - k) % NZ

    def dev_z(k):
        return (z_to(k) * NX + x, narrow)

    barrier = pltpu.get_barrier_semaphore()
    for dev in [dev_core, dev_x, dev_y] + [dev_z(k) for k in range(1, NZ)]:
        pl.semaphore_signal(barrier, inc=1, device_id=dev, device_id_type=MESH)
    pl.semaphore_wait(barrier, 3 + NZ - 1)

    def remote(src, dst, send, recv, dev):
        return pltpu.make_async_remote_copy(
            src_ref=src, dst_ref=dst, send_sem=send, recv_sem=recv, device_id=dev, device_id_type=MESH
        )

    def lazy(*what):
        return lambda: remote(*what)

    ALL = slice(None)
    partners = {
        "x": [(3, dev_x, 1 - x, 1 - x)],
        "y": [(4, dev_y, 1 - y, 1 - y)],
        "z": [(k - 1, dev_z(k), z_to(k), z_from(k)) for k in range(1, NZ)],
    }
    own = {"x": x, "y": y, "z": z}

    def block(p, h, where):
        return G.at[p, where["y"], where["z"], where["x"], h]

    def gather_order(z_first, h):
        a, b = ("x", "y") if h == 0 else ("y", "x")
        return ("z", a, b) if z_first else (a, "z", b)

    def gather_copies(p, h, order, phase):
        axis = order[phase]
        have = {q: (ALL if q in order[:phase] else own[q]) for q in own}
        src = block(p, h, have)
        sends, recvs = [], []
        for slot, dev, _, frm in partners[axis]:
            sends.append(lazy(src, src, ag_s.at[p, h, slot], ag_r.at[p, h, slot], dev))
            got = block(p, h, {**have, axis: frm})
            recvs.append(lazy(got, got, ag_s.at[p, h, slot], ag_r.at[p, h, slot], dev))
        return sends, recvs

    def by_kind(slot_index, action):
        z_second = (slot_index % 3) == 2

        @pl.when(jnp.logical_not(z_second))
        def _():
            action(True)

        @pl.when(z_second)
        def _():
            action(False)

    def gather_issue(p, phase):
        def action(z_first):
            for h in range(2):
                order = gather_order(z_first, h)
                if phase > 0:
                    for r in gather_copies(p, h, order, phase - 1)[1]:
                        r().wait_recv()
                if phase < 3:
                    for s in gather_copies(p, h, order, phase)[0]:
                        s().start()

        by_kind(p % PER, action)

    def gather_sent(p):
        def action(z_first):
            for h in range(2):
                for phase in range(3):
                    for s in gather_copies(p, h, gather_order(z_first, h), phase)[0]:
                        s().wait_send()

        by_kind(p % PER, action)

    for p in range(PAIRS):
        for h in range(2):
            G[p, y, z, x, h] = wloc[p, h]

    half = TM * c
    BKh = BK.at[pl.ds(pl.multiple_of(half, TM), TM)]
    GRh = GR.at[pl.ds(pl.multiple_of(half, TM), TM)]
    other = TM * (1 - c)
    BKo = BK.at[pl.ds(pl.multiple_of(other, TM), TM)]
    GRo = GR.at[pl.ds(pl.multiple_of(other, TM), TM)]
    patch_out = remote(patch, BKh, in_s.at[0], in_r.at[0], dev_core)
    patch_in = remote(patch, BKo, in_s.at[0], in_r.at[0], dev_core)
    cot_out = remote(cot, GRh, in_s.at[1], in_r.at[1], dev_core)
    cot_in = remote(cot, GRo, in_s.at[1], in_r.at[1], dev_core)
    patch_own = pltpu.make_async_copy(patch, BKh, lc_s.at[0])
    cot_own = pltpu.make_async_copy(cot, GRh, lc_s.at[1])
    patch_own.start()
    cot_own.start()
    patch_out.start()
    GPIECE[z, x] = jnp.zeros((8, 128), F32)
    GPIECE[z, x, 0:5, 0:ROWS] = small[...].astype(BF16).astype(F32)
    gain_z = [
        (
            remote(GPIECE.at[z, x], GPIECE.at[z, x], gn_s.at[k - 1], gn_r.at[k - 1], dev_z(k)),
            remote(GPIECE.at[z_from(k), x], GPIECE.at[z_from(k), x], gn_s.at[k - 1], gn_r.at[k - 1], dev_z(k)),
        )
        for k in range(1, NZ)
    ]
    gain_x = (
        remote(GPIECE.at[:, x], GPIECE.at[:, x], gn_s.at[3], gn_r.at[3], dev_x),
        remote(GPIECE.at[:, 1 - x], GPIECE.at[:, 1 - x], gn_s.at[3], gn_r.at[3], dev_x),
    )
    for s, _ in gain_z:
        s.start()
    for p in range(LEAD_ONE):
        gather_issue(p, 0)
    cot_out.start()

    index_row = mask_index[pl.ds(y, 1), :]
    count = mask_count[y]
    spot = lax.broadcasted_iota(jnp.int32, (SEQ, index_row.shape[1]), 0)
    live = lax.broadcasted_iota(jnp.int32, (1, index_row.shape[1]), 1) < count
    hits = jnp.where(jnp.logical_and(spot == index_row, live), 1.0, 0.0)
    FL[...] = jnp.max(hits, axis=1, keepdims=True)

    for _, r in gain_z:
        r.wait_recv()
    gain_x[0].start()
    gain_x[1].wait_recv()
    lane = lax.broadcasted_iota(jnp.int32, (128, D), 0)
    feature = lax.broadcasted_iota(jnp.int32, (128, D), 1)
    gains = jnp.zeros((8, D), F32)
    for zz in range(NZ):
        for xx in range(NX):
            place = jnp.logical_and(feature - ROWS * (zz * NX + xx) == lane, lane < ROWS)
            gains = gains + mm(GPIECE[zz, xx].astype(BF16), jnp.where(place, 1.0, 0.0).astype(BF16))
    GAIN[...] = gains

    patch_own.wait()
    patch_in.wait_recv()
    embed = GAIN[4:5, :]

    def mask_tile(i):
        rows = rows_at(i, TR)
        flag = FL[rows, :]
        S[0, rows, :] = BK[rows, :].astype(F32) * (1.0 - flag) + flag * embed

    loop(SEQ // TR, mask_tile)

    def norm_parts(values):
        centre = values - jnp.mean(values, axis=-1, keepdims=True)
        spread = jnp.mean(centre * centre, axis=-1, keepdims=True)
        return centre, lax.rsqrt(spread + EPS_NORM)

    def norm_into(dst, src, gain_row):
        gain = GAIN[pl.ds(gain_row, 1), :]

        def tile(i):
            rows = rows_at(i, TR)
            centre, inv = norm_parts(src[rows, :])
            dst[rows, :] = (centre * inv * gain).astype(BF16)

        loop(SEQ // TR, tile)

    def matrix(p, yy):
        return G[p, yy].reshape(D, WIDE)

    def exchange(e, make, take):
        par = e % 2

        def copies(i, par):
            rows = rows_at(i, TM)
            return remote(XS.at[rows], XR.at[par, rows], ex_s.at[i], ex_r.at[par, i], dev_core)

        def give(i):
            XS[rows_at(i, TM), :] = make(i).astype(BF16)
            copies(i, par).start()

        loop(SEQ // TM, give)

        def receive(i):
            copies(i, par).wait_recv()

            def tile(j):
                rows = pl.ds(pl.multiple_of(i * TM + j * TR, TR), TR)
                take(rows, XS[rows, :].astype(F32) + XR[par, rows, :].astype(F32))

            loop(TM // TR, tile)

        loop(SEQ // TM, receive)
        loop(SEQ // TM, lambda i: copies(i, par).wait_send())

    def attend(l, yy):
        def tile(i):
            rows = rows_at(i, TM)
            outs = []
            for hd in range(HEADS_Y):
                lo = hd * HD
                q = QK[l, yy, rows, lo : lo + HD]
                k = QK[l, yy, :, COL + lo : COL + lo + HD]
                v = V[l, yy, :, lo : lo + HD]
                s = mm_nt(q, k) * SCALE
                e = jnp.exp(s - jnp.max(s, axis=1, keepdims=True))
                probs = e / jnp.sum(e, axis=1, keepdims=True)
                outs.append(mm(probs.astype(BF16), v))
            MIX[l, yy, rows, :] = jnp.concatenate(outs, axis=1).astype(BF16)

        loop(SEQ // TM, tile)

    def attend_back(l, yy):
        for hd in range(HEADS_Y):
            lo = hd * HD
            k = QK[l, yy, :, COL + lo : COL + lo + HD]
            v = V[l, yy, :, lo : lo + HD]

            def tile(i, carry):
                dk, dv = carry
                rows = rows_at(i, TM)
                q = QK[l, yy, rows, lo : lo + HD]
                dm = GM[yy, rows, lo : lo + HD]
                s = mm_nt(k, q) * SCALE
                e = jnp.exp(s - jnp.max(s, axis=0, keepdims=True))
                probs = e / jnp.sum(e, axis=0, keepdims=True)
                dp = mm_nt(v, dm)
                ds = probs * (dp - jnp.sum(probs * dp, axis=0, keepdims=True))
                ds = ds.astype(BF16)
                dv = dv + mm(probs.astype(BF16), dm)
                dk = dk + mm(ds, q)
                dq = mm_tn(ds, k) * SCALE
                DQK[yy, rows, lo : lo + HD] = dq.astype(BF16)
                return dk, dv

            zero = jnp.zeros((SEQ, HD), F32)
            dk, dv = lax.fori_loop(0, SEQ // TM, tile, (zero, zero))
            DQK[yy, :, COL + lo : COL + lo + HD] = (dk * SCALE).astype(BF16)
            DV[yy, :, lo : lo + HD] = dv.astype(BF16)

    def forward_slot(slot, l):
        p = l * PER + slot
        if slot == 0:
            norm_into(NRM.at[l], S.at[l], 2 * l)

            def project(yy):
                def tile(i):
                    rows = rows_at(i, TM)
                    QK[l, yy, rows, :] = mm(NRM[l, rows, :], matrix(p, yy)).astype(BF16)

                loop(SEQ // TM, tile)

            loop(2, project)
        elif slot == 1:

            def project_v(yy):
                def tile(i):
                    rows = rows_at(i, TM)
                    V[l, yy, rows, :] = mm(NRM[l, rows, :], matrix(p, yy)[:, :COL]).astype(BF16)

                loop(SEQ // TM, tile)
                attend(l, yy)

            loop(2, project_v)

            def make(i):
                rows = rows_at(i, TM)
                total = mm_nt(MIX[l, 0, rows, :], matrix(p, 0)[:, COL:])
                return total + mm_nt(MIX[l, 1, rows, :], matrix(p, 1)[:, COL:])

            def take(rows, total):
                R1[l, rows, :] = S[l, rows, :] + total

            exchange(0, make, take)
        elif slot in (2, 3):
            u = slot - 2
            if u == 0:
                norm_into(NRM2.at[l], R1.at[l], 2 * l + 1)

            def project_up(yy):
                def tile(i):
                    rows = rows_at(i, TM)
                    ACC[rows, 0:WIDE] = mm(NRM2[l, rows, :], matrix(p, yy))

                loop(SEQ // TM, tile)

                def gelu(i):
                    rows = rows_at(i, TR)
                    v = ACC[rows, 0:WIDE]
                    cdf = 0.5 * (1.0 + lax.erf(v * (2.0 ** -0.5)))
                    HID[l, u, yy, rows, :] = (v * cdf).astype(BF16)
                    pdf = jnp.exp(-0.5 * v * v) * 0.3989422804014327
                    GP[l, u, yy, rows, :] = (cdf + v * pdf).astype(BF16)

                loop(SEQ // TR, gelu)

            loop(2, project_up)
        elif slot == 4:

            def down(i):
                rows = rows_at(i, TM)
                total = mm_nt(HID[l, 0, 0, rows, :], matrix(p, 0))
                ACC[rows, :] = total + mm_nt(HID[l, 0, 1, rows, :], matrix(p, 1))

            loop(SEQ // TM, down)
        else:

            def make(i):
                rows = rows_at(i, TM)
                total = ACC[rows, :] + mm_nt(HID[l, 1, 0, rows, :], matrix(p, 0))
                return total + mm_nt(HID[l, 1, 1, rows, :], matrix(p, 1))

            def take(rows, total):
                value = R1[l, rows, :] + total

                @pl.when(l == 0)
                def _():
                    S[1, rows, :] = value

                @pl.when(l == 1)
                def _():
                    ACC[rows, :] = value

            exchange(1, make, take)

    def forward_tick(t):
        for lead, phase in ((LEAD_ONE, 0), (LEAD_TWO, 1), (LEAD_THREE, 2)):

            @pl.when(jnp.logical_and(t + lead >= (LEAD_ONE if phase == 0 else 0), t + lead < PAIRS))
            def _():
                gather_issue(t + lead, phase)

        @pl.when(t >= 0)
        def _():
            gather_issue(t, 3)
            for slot in range(PER):

                @pl.when(t % PER == slot)
                def _():
                    forward_slot(slot, t // PER)

    lead_in = LEAD_TWO

    loop(PAIRS + lead_in, lambda i: forward_tick(i - lead_in))

    block_copy = pltpu.make_async_copy(ACC.at[pl.ds(pl.multiple_of(half, TM), TM)], out_block, lc_s.at[2])
    block_copy.start()
    loop(PAIRS, gather_sent)
    for s, _ in gain_z:
        s.wait_send()
    gain_x[0].wait_send()
    patch_out.wait_send()
    block_copy.wait()

    def scatter_copies(p, h, z_first, phase):
        order = gather_order(z_first, h)[::-1]
        axis = order[phase]
        have = {q: (own[q] if q in order[:phase] else ALL) for q in own}
        sends, recvs = [], []
        for slot, dev, to, _ in partners[axis]:
            src = block(p, h, {**have, axis: to})
            if phase == 0:
                dst = (RB0Y if h == 0 else RB0X).at[p]
            elif phase == 1:
                dst = RB1.at[p, h, pl.ds(2 * slot, 2)] if axis == "z" else RB1.at[p, h, pl.ds(0, NZ)]
            else:
                dst = RB2.at[p, h, slot] if axis == "z" else RB2.at[p, h, 0]
            sends.append(lazy(src, dst, rs_s.at[p, h, slot], rs_r.at[p, h, slot], dev))
            recvs.append((dst, lazy(dst, dst, rs_s.at[p, h, slot], rs_r.at[p, h, slot], dev)))
        return sends, recvs, {**have, axis: own[axis]}

    def scatter_issue(p, phase):
        def action(z_first):
            for h in range(2):
                if phase > 0:
                    _, recvs, where = scatter_copies(p, h, z_first, phase - 1)
                    for _, r in recvs:
                        r().wait_recv()
                    view = block(p, h, where)
                    total = view[...].astype(F32)
                    for dst, _ in recvs:
                        total = total + dst[...].astype(F32)
                    if phase < 3:
                        view[...] = total.astype(BF16)
                    else:
                        out_grad[p, h] = total
                        NB[0] += fold(total * total)
                if phase < 3:
                    for s in scatter_copies(p, h, z_first, phase)[0]:
                        s().start()

        by_kind(p % PER, action)

    def fold(sq):
        sq = jnp.sum(sq.reshape(HALF // 8, 8, WIDE), axis=0)
        return sq[:, 0:128] + sq[:, 128:256] + sq[:, 256:384]

    def scatter_sent(p):
        def action(z_first):
            for h in range(2):
                for phase in range(3):
                    for s in scatter_copies(p, h, z_first, phase)[0]:
                        s().wait_send()

        by_kind(p % PER, action)

    NB[0] = jnp.zeros((8, 128), F32)
    SG[...] = jnp.zeros_like(SG)

    def transpose_into(dst, src):
        def tile(i):
            rows = rows_at(i, 128)
            dst[:, rows] = jnp.transpose(src[rows, :])

        loop(SEQ // 128, tile)

    def put_grad(p, yy, left, right):
        def tile(i):
            G[p, yy, i] = mm(left[rows_at(i, D // NZ), :], right).reshape(NX, 2, HALF, WIDE).astype(BF16)

        loop(NZ, tile)

    def back_exchange(e, make, src, gain_row):
        gain = GAIN[pl.ds(gain_row, 1), :]
        def take(rows, dn):
            centre, inv = norm_parts(src[rows, :])
            xhat = centre * inv
            dh = dn * gain
            dv = inv * (
                dh
                - jnp.mean(dh, axis=-1, keepdims=True)
                - xhat * jnp.mean(dh * xhat, axis=-1, keepdims=True)
            )
            GR[rows, :] += dv
            SG[pl.ds(gain_row, 1), :] += jnp.sum(dn * xhat, axis=0, keepdims=True)

        exchange(e, make, take)

    def cast_rows(dst, src):
        def tile(i):
            rows = rows_at(i, TR)
            dst[rows, :] = src[rows, :].astype(BF16)

        loop(SEQ // TR, tile)

    def backward_slot(s, l):
        slot = (4, 2, 5, 3, 1, 0)[s]
        p = l * PER + slot
        if slot in (4, 5):
            u = slot - 4
            if u == 0:
                cast_rows(BK, GR)
                transpose_into(TA, BK)
                transpose_into(TB, NRM2.at[l])

            def down_back(yy):
                def tile(i):
                    rows = rows_at(i, TM)
                    gh = mm(BK[rows, :], matrix(p, yy))
                    GU[yy, rows, :] = (gh * GP[l, u, yy, rows, :].astype(F32)).astype(BF16)

                loop(SEQ // TM, tile)
                put_grad(p, yy, TA, HID[l, u, yy])

            loop(2, down_back)
        elif slot in (2, 3):
            u = slot - 2
            if u == 0:

                def part(i):
                    rows = rows_at(i, TM)
                    total = mm_nt(GU[0, rows, :], matrix(p, 0))
                    ACC[rows, :] = total + mm_nt(GU[1, rows, :], matrix(p, 1))

                loop(SEQ // TM, part)
            else:

                def make(i):
                    rows = rows_at(i, TM)
                    total = ACC[rows, :] + mm_nt(GU[0, rows, :], matrix(p, 0))
                    return total + mm_nt(GU[1, rows, :], matrix(p, 1))

                back_exchange(0, make, R1.at[l], 2 * l + 1)
            loop(2, lambda yy: put_grad(p, yy, TB, GU[yy]))
        elif slot == 1:
            cast_rows(BK, GR)
            transpose_into(TA, BK)
            transpose_into(TB, NRM.at[l])

            def attn_back(yy):
                def tile(i):
                    rows = rows_at(i, TM)
                    GM[yy, rows, :] = mm(BK[rows, :], matrix(p, yy)[:, COL:]).astype(BF16)

                loop(SEQ // TM, tile)
                attend_back(l, yy)

            loop(2, attn_back)

            def part(i):
                rows = rows_at(i, TM)
                total = mm_nt(DV[0, rows, :], matrix(p, 0)[:, :COL])
                ACC[rows, :] = total + mm_nt(DV[1, rows, :], matrix(p, 1)[:, :COL])

            loop(SEQ // TM, part)

            def grads(yy):
                def tile(i):
                    rows = rows_at(i, D // NZ)
                    gv = mm(TB[rows, :], DV[yy])
                    go = mm(TA[rows, :], MIX[l, yy])
                    both = jnp.concatenate([gv, go], axis=1)
                    G[p, yy, i] = both.reshape(NX, 2, HALF, WIDE).astype(BF16)

                loop(NZ, tile)

            loop(2, grads)
        else:

            def make(i):
                rows = rows_at(i, TM)
                total = ACC[rows, :] + mm_nt(DQK[0, rows, :], matrix(p, 0))
                return total + mm_nt(DQK[1, rows, :], matrix(p, 1))

            back_exchange(1, make, S.at[l], 2 * l)
            loop(2, lambda yy: put_grad(p, yy, TB, DQK[yy]))
        return p

    def position(i):
        s = i % PER
        slot = jnp.where(s == 0, 4, jnp.where(s == 1, 2, jnp.where(s == 2, 5, jnp.where(s == 3, 3, 5 - s))))
        return (LAYERS - 1 - i // PER) * PER + slot

    cot_own.wait()
    cot_in.wait_recv()
    cot_out.wait_send()

    def backward_tick(t):
        @pl.when(t < PAIRS)
        def _():
            for s in range(PER):

                @pl.when(t % PER == s)
                def _():
                    backward_slot(s, LAYERS - 1 - t // PER)

            scatter_issue(position(t), 0)

        for lag, phase in ((LAG_TWO, 1), (LAG_THREE, 2), (LAG_LAST, 3)):

            @pl.when(jnp.logical_and(t - lag >= 0, t - lag < PAIRS))
            def _():
                scatter_issue(position(t - lag), phase)

    loop(PAIRS, backward_tick)

    def finish_tile(i):
        rows = rows_at(i, TR)
        flag = FL[rows, :]
        value = GR[rows, :]
        SG[4:5, :] += jnp.sum(value * flag, axis=0, keepdims=True)
        GR[rows, :] = value * (1.0 - flag)

    loop(SEQ // TR, finish_tile)
    igrad_copy = pltpu.make_async_copy(GRh, out_igrad, lc_s.at[3])
    igrad_copy.start()

    SR[0, z] = SG[...]
    sg_z = [
        (
            remote(SR.at[0, z], SR.at[0, z], fs_s.at[k - 1], fs_r.at[k - 1], dev_z(k)),
            remote(SR.at[0, z_from(k)], SR.at[0, z_from(k)], fs_s.at[k - 1], fs_r.at[k - 1], dev_z(k)),
        )
        for k in range(1, NZ)
    ]
    for s, _ in sg_z:
        s.start()
    for _, r in sg_z:
        r.wait_recv()
    SR[1, 0] = SR[0, 0] + SR[0, 1] + SR[0, 2] + SR[0, 3]
    sg_x = remote(SR.at[1, 0], SR.at[1, 1], fs_s.at[3], fs_r.at[3], dev_x)
    sg_x.start()

    loop(LAG_LAST, lambda i: backward_tick(PAIRS + i))

    sg_x.wait_recv()
    SR[1, 2] = SR[1, 0] + SR[1, 1]
    sg_y = remote(SR.at[1, 2], SR.at[1, 3], fs_s.at[4], fs_r.at[4], dev_y)
    sg_y.start()

    own_square = jnp.sum(jnp.sum(NB[0], axis=1, keepdims=True), axis=0, keepdims=True)
    NB[1 + z] = jnp.broadcast_to(own_square, (8, 128))
    nm_z = [
        (
            remote(NB.at[1 + z], NB.at[1 + z], nm_s.at[k - 1], nm_r.at[k - 1], dev_z(k)),
            remote(NB.at[1 + z_from(k)], NB.at[1 + z_from(k)], nm_s.at[k - 1], nm_r.at[k - 1], dev_z(k)),
        )
        for k in range(1, NZ)
    ]
    for s, _ in nm_z:
        s.start()
    sg_y.wait_recv()
    total_small = SR[1, 2] + SR[1, 3]
    out_small[...] = total_small
    small_square = jnp.sum(jnp.sum(total_small * total_small, axis=1, keepdims=True), axis=0, keepdims=True)
    for _, r in nm_z:
        r.wait_recv()
    NB[5] = NB[1] + NB[2] + NB[3] + NB[4]
    nm_x = remote(NB.at[5], NB.at[6], nm_s.at[3], nm_r.at[3], dev_x)
    nm_x.start()
    nm_x.wait_recv()
    NB[7] = NB[5] + NB[6]
    nm_y = remote(NB.at[7], NB.at[8], nm_s.at[4], nm_r.at[4], dev_y)
    nm_y.start()
    nm_y.wait_recv()
    NB[9] = NB[7] + NB[8]
    nm_c = remote(NB.at[9], NB.at[10], nm_s.at[5], nm_r.at[5], dev_core)
    nm_c.start()
    nm_c.wait_recv()
    out_norm[...] = jnp.sqrt(NB[9] + NB[10] + small_square)

    for s, _ in sg_z + nm_z:
        s.wait_send()
    for s in (sg_x, sg_y, nm_x, nm_y, nm_c):
        s.wait_send()
    loop(PAIRS, scatter_sent)
    igrad_copy.wait()


def big_step(wloc, patches, cotangent, mask_index, mask_count, small):
    vm = pl.BlockSpec(memory_space=pltpu.VMEM)
    hb = pl.BlockSpec(memory_space=pl.ANY)
    sm = pl.BlockSpec(memory_space=pltpu.SMEM)
    dma = pltpu.SemaphoreType.DMA
    V = pltpu.VMEM
    scratch = [
        V((PAIRS, 2, NZ, NX, 2, HALF, WIDE), BF16),
        V((2, SEQ, D), F32),
        V((2, SEQ, D), F32),
        V((2, SEQ, D), BF16),
        V((2, SEQ, D), BF16),
        V((2, 2, SEQ, WIDE), BF16),
        V((2, 2, SEQ, COL), BF16),
        V((2, 2, SEQ, COL), BF16),
        V((2, 2, 2, SEQ, WIDE), BF16),
        V((2, 2, 2, SEQ, WIDE), BF16),
        V((SEQ, D), F32),
        V((SEQ, D), F32),
        V((SEQ, D), BF16),
        V((2, SEQ, D), BF16),
        V((SEQ, D), BF16),
        V((D, SEQ), BF16),
        V((D, SEQ), BF16),
        V((2, SEQ, WIDE), BF16),
        V((2, SEQ, COL), BF16),
        V((2, SEQ, WIDE), BF16),
        V((2, SEQ, COL), BF16),
        V((SEQ, 1), F32),
        V((8, D), F32),
        V((NZ, NX, 8, 128), F32),
        V((8, D), F32),
        V((2, 4, 8, D), F32),
        V((11, 8, 128), F32),
        V((PAIRS, NZ, NX, HALF, WIDE), BF16),
        V((PAIRS, 2, NZ, HALF, WIDE), BF16),
        V((PAIRS, 2, 6, HALF, WIDE), BF16),
        V((PAIRS, 2, 3, HALF, WIDE), BF16),
        dma((PAIRS, 2, 5)), dma((PAIRS, 2, 5)),
        dma((PAIRS, 2, 5)), dma((PAIRS, 2, 5)),
        dma((2,)), dma((2, 2)),
        dma((2,)), dma((2,)), dma((4,)),
        dma((4,)), dma((4,)),
        dma((5,)), dma((5,)),
        dma((6,)), dma((6,)),
    ]
    return pl.pallas_call(
        step_kernel,
        out_shape=(
            jax.ShapeDtypeStruct((TM, D), F32),
            jax.ShapeDtypeStruct((TM, D), F32),
            jax.ShapeDtypeStruct((PAIRS, 2, HALF, WIDE), F32),
            jax.ShapeDtypeStruct((8, D), F32),
            jax.ShapeDtypeStruct((8, 128), F32),
        ),
        in_specs=[vm, hb, hb, vm, sm, vm],
        out_specs=(hb, hb, vm, vm, vm),
        scratch_shapes=scratch,
        compiler_params=pltpu.CompilerParams(
            collective_id=0, has_side_effects=True, vmem_limit_bytes=62 << 20
        ),
        name="train_step",
    )(wloc, patches, cotangent, mask_index, mask_count, small)


def adam_values(weight_in, moment_one, moment_two, gradient, step_rate, decay_rate):
    moment_one = BETA_ONE * moment_one + (1.0 - BETA_ONE) * gradient
    moment_two = BETA_TWO * moment_two + (1.0 - BETA_TWO) * gradient * gradient
    first_hat = moment_one / (1.0 - BETA_ONE**STEP)
    second_hat = moment_two / (1.0 - BETA_TWO**STEP)
    updated = weight_in - step_rate * (
        first_hat / (jnp.sqrt(second_hat) + EPS_ADAM) + decay_rate * weight_in
    )
    return (updated, moment_one, moment_two)


def adam_kernel(norm, grad, w, m, v, nw, nm, nv):
    factor = jnp.minimum(1.0, CLIP_MAX / norm[0:1, 0:1])
    g = grad[0].reshape(ROWS, WIDE) * factor
    for j in range(2):
        nw[j], nm[j], nv[j] = adam_values(w[j], m[j], v[j], g[:, j * COL : (j + 1) * COL], D ** (-0.5), DECAY_RATE)


def adam_matrices(norm, grad, weights, first, second):
    shape = weights.shape
    flat = (LAYERS * 12, ROWS, COL)
    blk = pl.BlockSpec((2, ROWS, COL), lambda i: (i, 0, 0))
    outs = pl.pallas_call(
        adam_kernel,
        grid=(PAIRS,),
        out_shape=tuple(jax.ShapeDtypeStruct(flat, F32) for _ in range(3)),
        in_specs=[
            pl.BlockSpec((8, 128), lambda i: (0, 0)),
            pl.BlockSpec((1, 2, HALF, WIDE), lambda i: (i, 0, 0, 0)),
            blk, blk, blk,
        ],
        out_specs=(blk, blk, blk),
        name="adam",
    )(norm, grad, weights.reshape(flat), first.reshape(flat), second.reshape(flat))
    return tuple(o.reshape(shape) for o in outs)


def shards(patches, cotangent, mask_index, mask_count, weights, first_moment, second_moment,
           small_params, small_first, small_second):
    owned_rows = weights.shape[2]
    low = weights.astype(BF16).reshape(PAIRS, 2, ROWS, COL)
    wloc = jnp.concatenate([low[:, 0], low[:, 1]], axis=-1).reshape(PAIRS, 2, HALF, WIDE)
    block_output, input_grad, grad_own, small_total, norm = big_step(
        wloc, patches, cotangent, mask_index, mask_count, small_params
    )
    new_weights, new_first, new_second = adam_matrices(norm, grad_own, weights, first_moment, second_moment)
    grad_norm = norm[0, 0]
    factor = jnp.minimum(1.0, CLIP_MAX / grad_norm)
    first_col = lax.axis_index("wide") * owned_rows
    small_own = lax.dynamic_slice_in_dim(small_total, first_col, owned_rows, 1)[0:5]
    new_small, new_small_first, new_small_second = adam_values(
        small_params, small_first, small_second, small_own * factor, RATE_SMALL, 0.0
    )
    return (block_output, input_grad, new_weights, new_first, new_second,
            new_small, new_small_first, new_small_second, grad_norm)


def layer_norm(values, gain):
    centre = values - jnp.mean(values, axis=-1, keepdims=True)
    spread = jnp.mean(centre * centre, axis=-1, keepdims=True)
    return centre * lax.rsqrt(spread + EPS_NORM) * gain


def exact_gelu(values):
    return jax.nn.gelu(values, approximate=False)


def gather_rows(share):
    return lax.all_gather(share, "narrow", axis=0, tiled=True)


def gather_grads(share):
    return lax.all_gather(share, "narrow", axis=0, tiled=True)


def branch_total(term, row_count):
    return lax.psum_scatter(
        term(jnp.int32(0), row_count * lax.axis_size("narrow")).astype(jnp.bfloat16),
        "narrow",
        scatter_dimension=0,
        tiled=True,
    ).astype(jnp.float32)


def input_total(term, row_count):
    return lax.psum_scatter(
        term(jnp.int32(0), row_count * lax.axis_size("narrow")).astype(jnp.bfloat16),
        "narrow",
        scatter_dimension=0,
        tiled=True,
    ).astype(jnp.float32)


def heads_of(values, clip_count):
    return values.reshape(clip_count, SEQ, values.shape[1] // HD, HD)


def attend_clip(parts):
    queries, key_rows, value_rows = parts
    scores = jnp.einsum(
        "qhd,khd->hqk", queries, key_rows, preferred_element_type=jnp.float32
    ) * HD ** (-0.5)
    probs = jax.nn.softmax(scores, axis=-1)
    return jnp.einsum(
        "hqk,khd->qhd", probs.astype(jnp.bfloat16), value_rows, preferred_element_type=jnp.float32
    ).astype(jnp.bfloat16)


def attend_back_clip(parts):
    queries, key_rows, value_rows, grad_mix = parts
    scale = HD ** (-0.5)
    scores = (
        jnp.einsum("qhd,khd->hqk", queries, key_rows, preferred_element_type=jnp.float32) * scale
    )
    probs = jax.nn.softmax(scores, axis=-1)
    grad_values = jnp.einsum(
        "hqk,qhd->khd", probs.astype(jnp.bfloat16), grad_mix, preferred_element_type=jnp.float32
    ).astype(jnp.bfloat16)
    grad_probs = jnp.einsum(
        "qhd,khd->hqk", grad_mix, value_rows, preferred_element_type=jnp.float32
    )
    grad_scores = probs * (grad_probs - jnp.sum(probs * grad_probs, axis=-1, keepdims=True))
    grad_scores = grad_scores.astype(jnp.bfloat16)
    grad_queries = (
        jnp.einsum("hqk,khd->qhd", grad_scores, key_rows, preferred_element_type=jnp.float32)
        * scale
    ).astype(jnp.bfloat16)
    grad_keys = (
        jnp.einsum("hqk,qhd->khd", grad_scores, queries, preferred_element_type=jnp.float32) * scale
    ).astype(jnp.bfloat16)
    return (grad_queries, grad_keys, grad_values)


def forward_layer(stream, weight, gain_one, gain_two):
    row_count = stream.shape[0]
    normed = gather_rows(layer_norm(stream, gain_one).astype(jnp.bfloat16))
    all_rows = normed.shape[0]
    clip_count = all_rows // SEQ
    project = jnp.einsum(
        "rd,sde->sre", normed, weight[0:3], preferred_element_type=jnp.float32
    ).astype(jnp.bfloat16)
    mixture = lax.map(
        attend_clip,
        (
            heads_of(project[0], clip_count),
            heads_of(project[1], clip_count),
            heads_of(project[2], clip_count),
        ),
    )
    mixture = mixture.reshape(all_rows, -1)

    def attn_term(first_row, row_num):
        return lax.dot_general(
            mixture, weight[3], (((1,), (1,)), ((), ())), preferred_element_type=jnp.float32
        )

    resid_one = stream + branch_total(attn_term, row_count)
    normed_two = gather_rows(layer_norm(resid_one, gain_two).astype(jnp.bfloat16))
    upward = jnp.einsum("rd,jde->jre", normed_two, weight[4:8], preferred_element_type=jnp.float32)
    hidden = exact_gelu(upward).astype(jnp.bfloat16)

    def mlp_term(first_row, row_num):
        return jnp.einsum("jre,jde->rd", hidden, weight[8:12], preferred_element_type=jnp.float32)

    result = resid_one + branch_total(mlp_term, row_count)
    return (result, (stream, normed, project, mixture, resid_one, normed_two, upward, hidden))


def backward_layer(grad_out, saved, weight, gain_one, gain_two):
    stream, normed, project, mixture, resid_one, normed_two, upward, hidden = saved
    row_count = stream.shape[0]
    all_rows = normed.shape[0]
    clip_count = all_rows // SEQ
    back_mlp = gather_grads(grad_out.astype(jnp.bfloat16))
    grad_down = jnp.einsum("rd,jre->jde", back_mlp, hidden, preferred_element_type=jnp.float32)
    grad_hidden = jnp.einsum(
        "rd,jde->jre", back_mlp, weight[8:12], preferred_element_type=jnp.float32
    )
    gelu_out, gelu_back = jax.vjp(exact_gelu, upward)
    grad_upward = gelu_back(grad_hidden)[0].astype(jnp.bfloat16)
    grad_up = jnp.einsum("rd,jre->jde", normed_two, grad_upward, preferred_element_type=jnp.float32)

    def up_term(first_row, row_num):
        return jnp.einsum(
            "jre,jde->rd", grad_upward, weight[4:8], preferred_element_type=jnp.float32
        )

    grad_normed_two = input_total(up_term, row_count)
    norm_out, norm_back = jax.vjp(layer_norm, resid_one, gain_two)
    part_stream, grad_gain_two = norm_back(grad_normed_two)
    grad_resid = grad_out + part_stream
    back_attn = gather_grads(grad_resid.astype(jnp.bfloat16))
    grad_out_proj = lax.dot_general(
        back_attn, mixture, (((0,), (0,)), ((), ())), preferred_element_type=jnp.float32
    )
    grad_mixture = jnp.dot(back_attn, weight[3], preferred_element_type=jnp.float32).astype(
        jnp.bfloat16
    )
    grad_heads = lax.map(
        attend_back_clip,
        (
            heads_of(project[0], clip_count),
            heads_of(project[1], clip_count),
            heads_of(project[2], clip_count),
            heads_of(grad_mixture, clip_count),
        ),
    )
    grad_project = jnp.stack([piece.reshape(all_rows, -1) for piece in grad_heads])
    grad_qkv = jnp.einsum("rd,sre->sde", normed, grad_project, preferred_element_type=jnp.float32)

    def qkv_term(first_row, row_num):
        return jnp.einsum(
            "sre,sde->rd", grad_project, weight[0:3], preferred_element_type=jnp.float32
        )

    grad_normed = input_total(qkv_term, row_count)
    norm_out_one, norm_back_one = jax.vjp(layer_norm, stream, gain_one)
    part_in, grad_gain_one = norm_back_one(grad_normed)
    grad_matrix = jnp.concatenate([grad_qkv, grad_out_proj[None], grad_up, grad_down], axis=0)
    return (grad_resid + part_in, grad_matrix, grad_gain_one, grad_gain_two)


def masked_rows(mask_index, mask_count, row_count):
    positions = lax.iota(jnp.int32, SEQ)
    slots = lax.iota(jnp.int32, mask_index.shape[1])
    live = slots[None, :] < mask_count[:, None]
    hits = (mask_index[:, :, None] == positions[None, None, :]) & live[:, :, None]
    flag_all = jnp.any(hits, axis=1).astype(jnp.float32).reshape(-1)
    return lax.dynamic_slice_in_dim(flag_all, lax.axis_index("narrow") * row_count, row_count, 0)


def shards_general(
    patches,
    cotangent,
    mask_index,
    mask_count,
    weights,
    first_moment,
    second_moment,
    small_params,
    small_first,
    small_second,
):
    row_count = patches.shape[0]
    narrow_size = lax.axis_size("narrow")
    owned_rows = weights.shape[2]
    matrices, small_low = (
        lax.all_gather(weights.astype(jnp.bfloat16), "wide", axis=2, tiled=True),
        lax.all_gather(small_params.astype(jnp.bfloat16), "wide", axis=1, tiled=True),
    )
    gains = small_low.astype(jnp.float32)
    flags = masked_rows(mask_index, mask_count, row_count)[:, None]
    stream = patches.astype(jnp.float32) * (1.0 - flags) + flags * gains[2 * LAYERS][None, :]
    saved_all = []
    for layer_idx in range(LAYERS):
        stream, saved = forward_layer(
            stream, matrices[layer_idx], gains[2 * layer_idx], gains[2 * layer_idx + 1]
        )
        saved_all.append(saved)
    grad_stream = cotangent
    grad_mats = [None] * LAYERS
    grad_gains = [None] * (2 * LAYERS)
    for layer_idx in reversed(range(LAYERS)):
        (
            grad_stream,
            grad_mats[layer_idx],
            grad_gains[2 * layer_idx],
            grad_gains[2 * layer_idx + 1],
        ) = backward_layer(
            grad_stream,
            saved_all[layer_idx],
            matrices[layer_idx],
            gains[2 * layer_idx],
            gains[2 * layer_idx + 1],
        )
    input_grad = grad_stream * (1.0 - flags)
    grad_embed = jnp.sum(grad_stream * flags, axis=0)
    grad_small = jnp.stack(grad_gains + [grad_embed])
    grad_matrix = jnp.stack(grad_mats)
    first_col = lax.axis_index("wide") * owned_rows
    small_total = lax.psum(grad_small, ("wide", "narrow"))
    small_own = lax.dynamic_slice_in_dim(small_total, first_col, owned_rows, 1)
    matrix_total = lax.psum(grad_matrix, "wide")
    matrix_own = lax.dynamic_slice_in_dim(matrix_total, first_col, owned_rows, 2)
    local_square = jnp.sum(matrix_own * matrix_own) + jnp.sum(small_own * small_own) / narrow_size
    grad_norm = jnp.sqrt(lax.psum(local_square, ("wide", "narrow")))
    factor = jnp.minimum(1.0, CLIP_MAX / grad_norm)
    new_weights, new_first, new_second = adam_values(
        weights, first_moment, second_moment, matrix_own * factor, D ** (-0.5), DECAY_RATE
    )
    new_small, new_small_first, new_small_second = adam_values(
        small_params, small_first, small_second, small_own * factor, RATE_SMALL, 0.0
    )
    return (
        stream,
        input_grad,
        new_weights,
        new_first,
        new_second,
        new_small,
        new_small_first,
        new_small_second,
        grad_norm,
    )


def solution(mesh):
    in_specs = (
        P(("wide", "narrow"), None),
        P(("wide", "narrow"), None),
        P("wide", None),
        P("wide"),
        P(None, None, "wide", "narrow"),
        P(None, None, "wide", "narrow"),
        P(None, None, "wide", "narrow"),
        P(None, "wide"),
        P(None, "wide"),
        P(None, "wide"),
    )
    out_specs = (
        P(("wide", "narrow"), None),
        P(("wide", "narrow"), None),
        P(None, None, "wide", "narrow"),
        P(None, None, "wide", "narrow"),
        P(None, None, "wide", "narrow"),
        P(None, "wide"),
        P(None, "wide"),
        P(None, "wide"),
        P(),
    )
    fits = mesh.shape["wide"] == NZ * NX and mesh.shape["narrow"] == 4
    step = shards if fits else shards_general
    return jax.shard_map(step, mesh=mesh, in_specs=in_specs, out_specs=out_specs, check_vma=False)
```

```python
import functools

import jax
import jax.numpy as jnp
from jax import lax
from jax.experimental import pallas as pl
from jax.experimental.pallas import tpu as pltpu
from jax.sharding import PartitionSpec as P

D = 768
HD = 64
LAYERS = 2
SEQ = 512
STEP = 10

EPS_NORM = 1e-06
BETA_ONE = 0.9
BETA_TWO = 0.999
EPS_ADAM = 1e-08
DECAY_RATE = 0.05
RATE_SMALL = 0.6
CLIP_MAX = 1.0

MESH = pl.DeviceIdType.MESH
F32 = jnp.float32
BF16 = jnp.bfloat16

PAIRS = 12
ADAM_STEPS = 2
PER = 6
NZ, NX = 4, 2
ROWS = 96
PARTS = 3
PART = ROWS // PARTS
COL = 192
WIDE = 2 * COL
SCALE = HD ** (-0.5)
TM = 256
TR = 64
HEADS_Y = COL // HD

BACK_ORDER = (4, 5, 2, 3, 1, 0)
LEAD_ONE, LEAD_TWO, LEAD_THREE = 4, 3, 2
LAG_TWO, LAG_THREE, LAG_LAST = 2, 4, 6


def mm(a, b):
    return lax.dot_general(a, b, (((1,), (0,)), ((), ())), preferred_element_type=F32)


def mm_nt(a, b):
    return lax.dot_general(a, b, (((1,), (1,)), ((), ())), preferred_element_type=F32)


def mm_tn(a, b):
    return lax.dot_general(a, b, (((0,), (0,)), ((), ())), preferred_element_type=F32)


def loop(count, body):
    def wrapped(i, carry):
        body(i)
        return carry

    lax.fori_loop(0, count, wrapped, 0)


def rows_at(i, size):
    return pl.ds(pl.multiple_of(i * size, size), size)


def step_kernel(
    weights, patch, cot, mask_index, mask_count, small,
    out_block, out_igrad, out_grad, out_small, out_norm,
    G, WF, S, R1, NRM, NRM2, QK, V, MIX, GP, HID, GR, ACC, XS, XR, BK, TA, TB, GU, GM, DQK, DV,
    FL, GAIN, GPIECE, SG, SR, NB, NZC, NXY, RB0Y, RB0X, RB1, RB1Z, RB2, RB2X,
    wf_s, ag_s, ag_r, rs_s, rs_r, ex_s, ex_r, in_s, in_r, lc_s, gn_s, gn_r, fs_s, fs_r, nm_s, nm_r,
):
    wide = lax.axis_index("wide")
    narrow = lax.axis_index("narrow")
    z, x = wide // NX, wide % NX
    y, c = narrow // 2, narrow % 2

    dev_core = (wide, 2 * y + 1 - c)
    dev_x = (z * NX + 1 - x, narrow)
    dev_y = (wide, 2 * (1 - y) + c)

    def z_to(k):
        return (z + k) % NZ

    def z_from(k):
        return (z + NZ - k) % NZ

    def dev_z(k):
        return (z_to(k) * NX + x, narrow)

    dev_xy = (z * NX + 1 - x, 2 * (1 - y) + c)

    def dev_zc(k):
        return (z_to(k) * NX + x, 2 * y + 1 - c)

    def load_pair(p):
        return pltpu.make_async_copy(weights.at[pl.ds(2 * p, 2)], WF.at[p % LEAD_ONE], wf_s.at[p % LEAD_ONE])

    for p in range(LEAD_ONE):
        load_pair(p).start()

    greeted = [dev_core, dev_x, dev_y, dev_xy] + [dev(k) for k in range(1, NZ) for dev in (dev_z, dev_zc)]
    barrier = pltpu.get_barrier_semaphore()
    for dev in greeted:
        pl.semaphore_signal(barrier, inc=1, device_id=dev, device_id_type=MESH)
    pl.semaphore_wait(barrier, len(greeted))

    def remote(src, dst, send, recv, dev):
        return pltpu.make_async_remote_copy(
            src_ref=src, dst_ref=dst, send_sem=send, recv_sem=recv, device_id=dev, device_id_type=MESH
        )

    def lazy(*what):
        return lambda: remote(*what)

    ALL = slice(None)
    partners = {
        "x": [(3, dev_x, 1 - x, 1 - x)],
        "y": [(4, dev_y, 1 - y, 1 - y)],
        "z": [(k - 1, dev_z(k), z_to(k), z_from(k)) for k in range(1, NZ)],
    }
    own = {"x": x, "y": y, "z": z}

    def block(p, h, where):
        return G.at[p, where["y"], where["z"], where["x"], h]

    def gather_order(even, h):
        if h == 0:
            return ("z", "x", "y")
        if h == 1:
            return ("z", "y", "x")
        return ("x", "z", "y") if even else ("y", "z", "x")

    def gather_copies(p, h, order, phase):
        axis = order[phase]
        have = {q: (ALL if q in order[:phase] else own[q]) for q in own}
        src = block(p, h, have)
        sends, recvs = [], []
        for slot, dev, _, frm in partners[axis]:
            sends.append(lazy(src, src, ag_s.at[p, h, slot], ag_r.at[p, h, slot], dev))
            got = block(p, h, {**have, axis: frm})
            recvs.append(lazy(got, got, ag_s.at[p, h, slot], ag_r.at[p, h, slot], dev))
        return sends, recvs

    def by_kind(p, action):
        @pl.when(p % 2 == 0)
        def _():
            action(True)

        @pl.when(p % 2 == 1)
        def _():
            action(False)

    def gather_issue(p, phase):
        def action(even):
            for h in range(PARTS):
                order = gather_order(even, h)
                if phase > 0:
                    for r in gather_copies(p, h, order, phase - 1)[1]:
                        r().wait_recv()
                if phase < 3:
                    for s in gather_copies(p, h, order, phase)[0]:
                        s().start()

        by_kind(p, action)

    def gather_sent(p):
        def action(even):
            for h in range(PARTS):
                for phase in range(3):
                    for s in gather_copies(p, h, gather_order(even, h), phase)[0]:
                        s().wait_send()

        by_kind(p, action)

    def pack(p):
        load_pair(p).wait()
        slot = p % LEAD_ONE
        both = jnp.concatenate([WF[slot, 0].astype(BF16), WF[slot, 1].astype(BF16)], axis=1)
        G[p, y, z, x] = both.reshape(PARTS, PART, WIDE)

        @pl.when(p + LEAD_ONE < PAIRS)
        def _():
            load_pair(p + LEAD_ONE).start()

    half = TM * c
    BKh = BK.at[pl.ds(pl.multiple_of(half, TM), TM)]
    GRh = GR.at[pl.ds(pl.multiple_of(half, TM), TM)]
    other = TM * (1 - c)
    BKo = BK.at[pl.ds(pl.multiple_of(other, TM), TM)]
    GRo = GR.at[pl.ds(pl.multiple_of(other, TM), TM)]
    patch_out = remote(patch, BKh, in_s.at[0], in_r.at[0], dev_core)
    patch_in = remote(patch, BKo, in_s.at[0], in_r.at[0], dev_core)
    cot_out = remote(cot, GRh, in_s.at[1], in_r.at[1], dev_core)
    cot_in = remote(cot, GRo, in_s.at[1], in_r.at[1], dev_core)
    patch_own = pltpu.make_async_copy(patch, BKh, lc_s.at[0])
    cot_own = pltpu.make_async_copy(cot, GRh, lc_s.at[1])
    patch_own.start()
    cot_own.start()
    patch_out.start()
    GPIECE[z, x] = jnp.zeros((8, 128), F32)
    GPIECE[z, x, 0:5, 0:ROWS] = small[...].astype(BF16).astype(F32)
    gain_z = [
        (
            remote(GPIECE.at[z, x], GPIECE.at[z, x], gn_s.at[k - 1], gn_r.at[k - 1], dev_z(k)),
            remote(GPIECE.at[z_from(k), x], GPIECE.at[z_from(k), x], gn_s.at[k - 1], gn_r.at[k - 1], dev_z(k)),
        )
        for k in range(1, NZ)
    ]
    gain_x = (
        remote(GPIECE.at[:, x], GPIECE.at[:, x], gn_s.at[3], gn_r.at[3], dev_x),
        remote(GPIECE.at[:, 1 - x], GPIECE.at[:, 1 - x], gn_s.at[3], gn_r.at[3], dev_x),
    )
    for s, _ in gain_z:
        s.start()
    def begin(p):
        pack(p)
        gather_issue(p, 0)

    loop(LEAD_ONE, begin)
    cot_out.start()
    loop(PAIRS - LEAD_ONE, lambda i: pack(i + LEAD_ONE))

    index_row = mask_index[pl.ds(y, 1), :]
    count = mask_count[y]
    spot = lax.broadcasted_iota(jnp.int32, (SEQ, index_row.shape[1]), 0)
    live = lax.broadcasted_iota(jnp.int32, (1, index_row.shape[1]), 1) < count
    hits = jnp.where(jnp.logical_and(spot == index_row, live), 1.0, 0.0)
    FL[...] = jnp.max(hits, axis=1, keepdims=True)

    for _, r in gain_z:
        r.wait_recv()
    gain_x[0].start()
    gain_x[1].wait_recv()
    lane = lax.broadcasted_iota(jnp.int32, (128, D), 0)
    feature = lax.broadcasted_iota(jnp.int32, (128, D), 1)
    gains = jnp.zeros((8, D), F32)
    for zz in range(NZ):
        for xx in range(NX):
            place = jnp.logical_and(feature - ROWS * (zz * NX + xx) == lane, lane < ROWS)
            gains = gains + mm(GPIECE[zz, xx].astype(BF16), jnp.where(place, 1.0, 0.0).astype(BF16))
    GAIN[...] = gains

    patch_own.wait()
    patch_in.wait_recv()
    embed = GAIN[4:5, :]

    def mask_tile(i):
        rows = rows_at(i, TR)
        flag = FL[rows, :]
        S[0, rows, :] = BK[rows, :].astype(F32) * (1.0 - flag) + flag * embed

    loop(SEQ // TR, mask_tile)

    def norm_parts(values):
        centre = values - jnp.mean(values, axis=-1, keepdims=True)
        spread = jnp.mean(centre * centre, axis=-1, keepdims=True)
        return centre, lax.rsqrt(spread + EPS_NORM)

    def norm_into(dst, src, gain_row):
        gain = GAIN[pl.ds(gain_row, 1), :]

        def tile(i):
            rows = rows_at(i, TR)
            centre, inv = norm_parts(src[rows, :])
            dst[rows, :] = (centre * inv * gain).astype(BF16)

        loop(SEQ // TR, tile)

    def matrix(p, yy):
        return G[p, yy].reshape(D, WIDE)

    def exchange_copy(e, i):
        rows = rows_at(i, TM)
        return remote(XS.at[rows], XR.at[e, rows], ex_s.at[i], ex_r.at[e, i], dev_core)

    def give(e, value):
        XS[...] = value.astype(BF16)
        loop(SEQ // TM, lambda i: exchange_copy(e, i).start())

    def receive(e, take):
        def chunk(i):
            exchange_copy(e, i).wait_recv()

            def tile(j):
                rows = pl.ds(pl.multiple_of(i * TM + j * TR, TR), TR)
                take(rows, XS[rows, :].astype(F32) + XR[e, rows, :].astype(F32))

            loop(TM // TR, tile)

        loop(SEQ // TM, chunk)
        loop(SEQ // TM, lambda i: exchange_copy(e, i).wait_send())

    def attend(l, yy):
        def tile(i):
            rows = rows_at(i, TM)
            outs = []
            for hd in range(HEADS_Y):
                lo = hd * HD
                q = QK[l, yy, rows, lo : lo + HD]
                k = QK[l, yy, :, COL + lo : COL + lo + HD]
                v = V[l, yy, :, lo : lo + HD]
                s = mm_nt(q, k) * SCALE
                e = jnp.exp(s - jnp.max(s, axis=1, keepdims=True))
                probs = e / jnp.sum(e, axis=1, keepdims=True)
                outs.append(mm(probs.astype(BF16), v))
            MIX[l, yy, rows, :] = jnp.concatenate(outs, axis=1).astype(BF16)

        loop(SEQ // TM, tile)

    def attend_back(l, yy):
        for hd in range(HEADS_Y):
            lo = hd * HD
            k = QK[l, yy, :, COL + lo : COL + lo + HD]
            v = V[l, yy, :, lo : lo + HD]

            def tile(i, carry):
                dk, dv = carry
                rows = rows_at(i, TM)
                q = QK[l, yy, rows, lo : lo + HD]
                dm = GM[yy, rows, lo : lo + HD]
                s = mm_nt(k, q) * SCALE
                e = jnp.exp(s - jnp.max(s, axis=0, keepdims=True))
                probs = e / jnp.sum(e, axis=0, keepdims=True)
                dp = mm_nt(v, dm)
                ds = probs * (dp - jnp.sum(probs * dp, axis=0, keepdims=True))
                ds = ds.astype(BF16)
                dv = dv + mm(probs.astype(BF16), dm)
                dk = dk + mm(ds, q)
                dq = mm_tn(ds, k) * SCALE
                DQK[yy, rows, lo : lo + HD] = dq.astype(BF16)
                return dk, dv

            zero = jnp.zeros((SEQ, HD), F32)
            dk, dv = lax.fori_loop(0, SEQ // TM, tile, (zero, zero))
            DQK[yy, :, COL + lo : COL + lo + HD] = (dk * SCALE).astype(BF16)
            DV[yy, :, lo : lo + HD] = dv.astype(BF16)

    def up_part(l, u, yy, p):
        ACC[:, 0:WIDE] = mm(NRM2[l], matrix(p, yy))

        def gelu(i):
            rows = rows_at(i, TR)
            v = ACC[rows, 0:WIDE]
            cdf = 0.5 * (1.0 + lax.erf(v * (2.0 ** -0.5)))
            HID[l, u, yy, rows, :] = (v * cdf).astype(BF16)
            pdf = jnp.exp(-0.5 * v * v) * 0.3989422804014327
            GP[l, u, yy, rows, :] = (cdf + v * pdf).astype(BF16)

        loop(SEQ // TR, gelu)

    def forward_slot(slot, step, l):
        p = l * PER + slot
        if slot == 0:
            if step == 0:
                norm_into(NRM.at[l], S.at[l], 2 * l)
            else:

                def project(yy):
                    QK[l, yy] = mm(NRM[l], matrix(p, yy)).astype(BF16)

                loop(2, project)
        elif slot == 1:
            if step == 0:

                def project_v(yy):
                    V[l, yy] = mm(NRM[l], matrix(p, yy)[:, :COL]).astype(BF16)

                loop(2, project_v)
                attend(l, 0)
            else:
                attend(l, 1)
                total = mm_nt(MIX[l, 0], matrix(p, 0)[:, COL:])
                give(0, total + mm_nt(MIX[l, 1], matrix(p, 1)[:, COL:]))
        elif slot in (2, 3):
            if slot == 2 and step == 0:

                def take(rows, total):
                    R1[l, rows, :] = S[l, rows, :] + total

                receive(0, take)
                norm_into(NRM2.at[l], R1.at[l], 2 * l + 1)
            up_part(l, slot - 2, step, p)
        elif slot == 4:
            if step == 0:
                ACC[...] = mm_nt(HID[l, 0, 0], matrix(p, 0)) + mm_nt(HID[l, 0, 1], matrix(p, 1))
        elif step == 0:
            total = ACC[...] + mm_nt(HID[l, 1, 0], matrix(p, 0))
            give(1, total + mm_nt(HID[l, 1, 1], matrix(p, 1)))
        else:

            def take(rows, total):
                value = R1[l, rows, :] + total

                @pl.when(l == 0)
                def _():
                    S[1, rows, :] = value

                @pl.when(l == 1)
                def _():
                    ACC[rows, :] = value

            receive(1, take)

            @pl.when(l == 1)
            def _():
                block_copy.start()

    block_copy = pltpu.make_async_copy(ACC.at[pl.ds(pl.multiple_of(half, TM), TM)], out_block, lc_s.at[2])

    def scatter_copies(p, h, even, phase):
        order = gather_order(even, h)[::-1]
        axis = order[phase]
        have = {q: (own[q] if q in order[:phase] else ALL) for q in own}
        sends, recvs = [], []
        for slot, dev, to, _ in partners[axis]:
            src = block(p, h, {**have, axis: to})
            if phase == 0:
                dst = (RB0Y if axis == "y" else RB0X).at[p if h < 2 else PAIRS + p // 2]
            elif phase == 1:
                dst = RB1Z.at[p, slot] if axis == "z" else RB1.at[p, h]
            else:
                dst = RB2.at[p, h, slot] if axis == "z" else RB2X.at[p]
            sends.append(lazy(src, dst, rs_s.at[p, h, slot], rs_r.at[p, h, slot], dev))
            recvs.append((dst, lazy(dst, dst, rs_s.at[p, h, slot], rs_r.at[p, h, slot], dev)))
        return sends, recvs, {**have, axis: own[axis]}

    def scatter_issue(p, phase):
        def action(even):
            for h in range(PARTS):
                if phase > 0:
                    _, recvs, where = scatter_copies(p, h, even, phase - 1)
                    for _, r in recvs:
                        r().wait_recv()
                    view = block(p, h, where)
                    total = view[...].astype(F32)
                    for dst, _ in recvs:
                        total = total + dst[...].astype(F32)
                    if phase < 3:
                        view[...] = total.astype(BF16)
                    else:
                        out_grad[p, h] = total
                        NB[...] += fold(total * total)
                if phase < 3:
                    for s in scatter_copies(p, h, even, phase)[0]:
                        s().start()

        by_kind(p, action)

    def fold(sq):
        sq = jnp.sum(sq.reshape(PART // 8, 8, WIDE), axis=0)
        return sq[:, 0:128] + sq[:, 128:256] + sq[:, 256:384]

    def scatter_sent(p):
        def action(even):
            for h in range(PARTS):
                for phase in range(3):
                    for s in scatter_copies(p, h, even, phase)[0]:
                        s().wait_send()

        by_kind(p, action)

    NB[...] = jnp.zeros((8, 128), F32)
    SG[...] = jnp.zeros_like(SG)

    def transpose_into(dst, src):
        def tile(i):
            rows = rows_at(i, 128)
            dst[:, rows] = jnp.transpose(src[rows, :])

        loop(SEQ // 128, tile)

    def put_grad(p, yy, left, right):
        G[p, yy] = mm(left[...], right).astype(BF16).reshape(NZ, NX, PARTS, PART, WIDE)

    def norm_back(e, src, gain_row):
        gain = GAIN[pl.ds(gain_row, 1), :]
        def take(rows, dn):
            centre, inv = norm_parts(src[rows, :])
            xhat = centre * inv
            dh = dn * gain
            dv = inv * (
                dh
                - jnp.mean(dh, axis=-1, keepdims=True)
                - xhat * jnp.mean(dh * xhat, axis=-1, keepdims=True)
            )
            GR[rows, :] += dv
            SG[pl.ds(gain_row, 1), :] += jnp.sum(dn * xhat, axis=0, keepdims=True)

        receive(e, take)

    def cast_rows(dst, src):
        def tile(i):
            rows = rows_at(i, TR)
            dst[rows, :] = src[rows, :].astype(BF16)

        loop(SEQ // TR, tile)

    def both(action):
        loop(2, action)

    def backward_slot(s, step, l):
        slot = BACK_ORDER[s]
        p = l * PER + slot
        if step == 0:
            gather_sent(p)
        if slot in (4, 5):
            u = slot - 4
            if slot == 4 and step == 0:

                @pl.when(l == 1)
                def _():
                    cot_own.wait()
                    cot_in.wait_recv()
                    cot_out.wait_send()

                cast_rows(BK, GR)
                transpose_into(TA, BK)
                transpose_into(TB, NRM2.at[l])
            gh = mm(BK[...], matrix(p, step))
            GU[u, step] = (gh * GP[l, u, step].astype(F32)).astype(BF16)
            put_grad(p, step, TA, HID[l, u, step])
        elif slot == 2:
            if step == 0:

                @pl.when(l == 1)
                def _():
                    block_copy.wait()

                ACC[...] = mm_nt(GU[0, 0], matrix(p, 0)) + mm_nt(GU[0, 1], matrix(p, 1))
            else:
                both(lambda yy: put_grad(p, yy, TB, GU[0, yy]))
        elif slot == 3:
            if step == 0:
                total = ACC[...] + mm_nt(GU[1, 0], matrix(p, 0))
                give(0, total + mm_nt(GU[1, 1], matrix(p, 1)))
            else:
                both(lambda yy: put_grad(p, yy, TB, GU[1, yy]))
                norm_back(0, R1.at[l], 2 * l + 1)
        elif slot == 1:
            if step == 0:
                cast_rows(BK, GR)
                transpose_into(TA, BK)
                transpose_into(TB, NRM.at[l])

                def grad_mix(yy):
                    GM[yy] = mm(BK[...], matrix(p, yy)[:, COL:]).astype(BF16)

                both(grad_mix)
                attend_back(l, 0)
            else:
                attend_back(l, 1)
                ACC[...] = mm_nt(DV[0], matrix(p, 0)[:, :COL]) + mm_nt(DV[1], matrix(p, 1)[:, :COL])

                def grads(yy):
                    gv = mm(TB[...], DV[yy])
                    go = mm(TA[...], MIX[l, yy])
                    pair = jnp.concatenate([gv, go], axis=1).astype(BF16)
                    G[p, yy] = pair.reshape(NZ, NX, PARTS, PART, WIDE)

                both(grads)
        else:
            if step == 0:
                total = ACC[...] + mm_nt(DQK[0], matrix(p, 0))
                give(1, total + mm_nt(DQK[1], matrix(p, 1)))
            else:
                both(lambda yy: put_grad(p, yy, TB, DQK[yy]))
                norm_back(1, S.at[l], 2 * l)

    def position(i):
        s = i % PER
        slot = jnp.where(s < 2, s + 4, jnp.where(s < 4, s, 5 - s))
        return (LAYERS - 1 - i // PER) * PER + slot

    def within(t, action, phase, first=0):
        @pl.when(jnp.logical_and(t >= first, t < PAIRS))
        def _():
            action(t, phase)

    def by_slot(t, action):
        for slot in range(PER):

            @pl.when(t % PER == slot)
            def _():
                action(slot)

    def scatter_at(t, phase):
        scatter_issue(position(t), phase)

    def forward_tick(t, q):
        for step in range(2):

            @pl.when(q == step)
            def _():
                if step == 0:
                    within(t + LEAD_ONE, gather_issue, 0, LEAD_ONE)
                    within(t + LEAD_TWO, gather_issue, 1)
                    within(t + LEAD_THREE, gather_issue, 2)
                    within(t, gather_issue, 3)

                @pl.when(t >= 0)
                def _():
                    by_slot(t, lambda slot: forward_slot(slot, step, t // PER))

    def backward_tick(t, q):
        for step in range(2):

            @pl.when(q == step)
            def _():
                @pl.when(t < PAIRS)
                def _():
                    by_slot(t, lambda s: backward_slot(s, step, LAYERS - 1 - t // PER))

                if step == 0:
                    pl.when(t == PAIRS)(rows_done)
                    pl.when(t == PAIRS + LAG_TWO)(small_sums)

                if step == 0:
                    within(t - LAG_TWO, scatter_at, 1)
                    within(t - LAG_LAST, scatter_at, 3)
                else:
                    within(t, scatter_at, 0)
                    within(t - LAG_THREE, scatter_at, 2)

    igrad_copy = pltpu.make_async_copy(GRh, out_igrad, lc_s.at[3])
    place = 2 * y + x
    around = ((2 * y + 1 - x, dev_x), (2 * (1 - y) + x, dev_y), (2 * (1 - y) + 1 - x, dev_xy))

    def small_z(k):
        got = SR.at[z_from(k), 0]
        return (
            remote(SR.at[z, 0], SR.at[z, 0], fs_s.at[k - 1], fs_r.at[k - 1], dev_z(k)),
            remote(got, got, fs_s.at[k - 1], fs_r.at[k - 1], dev_z(k)),
        )

    def small_xy(k):
        there, dev = around[k]
        return (
            remote(SR.at[place, 1], SR.at[place, 1], fs_s.at[3 + k], fs_r.at[3 + k], dev),
            remote(SR.at[there, 1], SR.at[there, 1], fs_s.at[3 + k], fs_r.at[3 + k], dev),
        )

    def rows_done():
        def finish_tile(i):
            rows = rows_at(i, TR)
            flag = FL[rows, :]
            value = GR[rows, :]
            SG[4:5, :] += jnp.sum(value * flag, axis=0, keepdims=True)
            GR[rows, :] = value * (1.0 - flag)

        loop(SEQ // TR, finish_tile)
        igrad_copy.start()
        SR[z, 0] = SG[...]
        for k in range(1, NZ):
            small_z(k)[0].start()

    def small_sums():
        for k in range(1, NZ):
            small_z(k)[1].wait_recv()
        SR[place, 1] = SR[0, 0] + SR[1, 0] + SR[2, 0] + SR[3, 0]
        for k in range(3):
            small_xy(k)[0].start()

    lead_in = LEAD_TWO
    merge = PAIRS - 1

    def tick(m):
        i, q = m // 2 - lead_in, m % 2
        is_back = jnp.logical_or(i == merge, i > merge + 1)

        @pl.when(jnp.logical_not(is_back))
        def _():
            forward_tick(jnp.where(i < merge, i, merge), q)

        @pl.when(is_back)
        def _():
            backward_tick(jnp.where(i == merge, 0, i - PAIRS), q)

    loop(2 * (2 * PAIRS + lead_in + LAG_LAST), tick)

    own_square = jnp.sum(jnp.sum(NB[...], axis=1, keepdims=True), axis=0, keepdims=True)
    NZC[z, c] = jnp.broadcast_to(own_square, (8, 128))
    nm_z = []
    for j, (zz, cc, frm, dev) in enumerate(
        [(z, 1 - c, z, dev_core)]
        + [(z_to(k), c, z_from(k), dev_z(k)) for k in range(1, NZ)]
        + [(z_to(k), 1 - c, z_from(k), dev_zc(k)) for k in range(1, NZ)]
    ):
        got = NZC.at[frm, cc]
        nm_z.append(
            (
                remote(NZC.at[z, c], NZC.at[z, c], nm_s.at[j], nm_r.at[j], dev),
                remote(got, got, nm_s.at[j], nm_r.at[j], dev),
            )
        )
    for s, _ in nm_z:
        s.start()
    for k in range(3):
        small_xy(k)[1].wait_recv()
    total_small = SR[0, 1] + SR[1, 1] + SR[2, 1] + SR[3, 1]
    out_small[...] = total_small
    small_square = jnp.sum(jnp.sum(total_small * total_small, axis=1, keepdims=True), axis=0, keepdims=True)
    for _, r in nm_z:
        r.wait_recv()
    square = NZC[0, 0] + NZC[0, 1]
    for zz in range(1, NZ):
        square = square + (NZC[zz, 0] + NZC[zz, 1])
    NXY[place] = square
    nm_xy = [
        (
            remote(NXY.at[place], NXY.at[place], nm_s.at[7 + k], nm_r.at[7 + k], dev),
            remote(NXY.at[there], NXY.at[there], nm_s.at[7 + k], nm_r.at[7 + k], dev),
        )
        for k, (there, dev) in enumerate(around)
    ]
    for s, _ in nm_xy:
        s.start()
    for _, r in nm_xy:
        r.wait_recv()
    out_norm[...] = jnp.sqrt(NXY[0] + NXY[1] + NXY[2] + NXY[3] + small_square)

    for s, _ in [small_z(k) for k in range(1, NZ)] + [small_xy(k) for k in range(3)] + nm_z + nm_xy + gain_z:
        s.wait_send()
    gain_x[0].wait_send()
    patch_out.wait_send()
    loop(PAIRS, scatter_sent)
    igrad_copy.wait()


def big_step(weights, patches, cotangent, mask_index, mask_count, small):
    vm = pl.BlockSpec(memory_space=pltpu.VMEM)
    hb = pl.BlockSpec(memory_space=pl.ANY)
    sm = pl.BlockSpec(memory_space=pltpu.SMEM)
    dma = pltpu.SemaphoreType.DMA
    V = pltpu.VMEM
    scratch = [
        V((PAIRS, 2, NZ, NX, PARTS, PART, WIDE), BF16),
        V((LEAD_ONE, 2, ROWS, COL), F32),
        V((2, SEQ, D), F32),
        V((2, SEQ, D), F32),
        V((2, SEQ, D), BF16),
        V((2, SEQ, D), BF16),
        V((2, 2, SEQ, WIDE), BF16),
        V((2, 2, SEQ, COL), BF16),
        V((2, 2, SEQ, COL), BF16),
        V((2, 2, 2, SEQ, WIDE), BF16),
        V((2, 2, 2, SEQ, WIDE), BF16),
        V((SEQ, D), F32),
        V((SEQ, D), F32),
        V((SEQ, D), BF16),
        V((2, SEQ, D), BF16),
        V((SEQ, D), BF16),
        V((D, SEQ), BF16),
        V((D, SEQ), BF16),
        V((2, 2, SEQ, WIDE), BF16),
        V((2, SEQ, COL), BF16),
        V((2, SEQ, WIDE), BF16),
        V((2, SEQ, COL), BF16),
        V((SEQ, 1), F32),
        V((8, D), F32),
        V((NZ, NX, 8, 128), F32),
        V((8, D), F32),
        V((4, 2, 8, D), F32),
        V((8, 128), F32),
        V((NZ, 2, 8, 128), F32),
        V((4, 8, 128), F32),
        V((PAIRS + PAIRS // 2, NZ, NX, PART, WIDE), BF16),
        V((PAIRS + PAIRS // 2, 2, NZ, PART, WIDE), BF16),
        V((PAIRS, 2, NZ, PART, WIDE), BF16),
        V((PAIRS, NZ - 1, 2, PART, WIDE), BF16),
        V((PAIRS, 2, NZ - 1, PART, WIDE), BF16),
        V((PAIRS, PART, WIDE), BF16),
        dma((LEAD_ONE,)),
        dma((PAIRS, PARTS, 5)), dma((PAIRS, PARTS, 5)),
        dma((PAIRS, PARTS, 5)), dma((PAIRS, PARTS, 5)),
        dma((2,)), dma((2, 2)),
        dma((2,)), dma((2,)), dma((4,)),
        dma((4,)), dma((4,)),
        dma((6,)), dma((6,)),
        dma((10,)), dma((10,)),
    ]
    return pl.pallas_call(
        step_kernel,
        out_shape=(
            jax.ShapeDtypeStruct((TM, D), F32),
            jax.ShapeDtypeStruct((TM, D), F32),
            jax.ShapeDtypeStruct((PAIRS, PARTS, PART, WIDE), F32),
            jax.ShapeDtypeStruct((8, D), F32),
            jax.ShapeDtypeStruct((8, 128), F32),
        ),
        in_specs=[hb, hb, hb, vm, sm, vm],
        out_specs=(hb, hb, vm, vm, vm),
        scratch_shapes=scratch,
        compiler_params=pltpu.CompilerParams(
            collective_id=0, has_side_effects=True, vmem_limit_bytes=62 << 20
        ),
        name="train_step",
    )(weights, patches, cotangent, mask_index, mask_count, small)


def adam_values(weight_in, moment_one, moment_two, gradient, step_rate, decay_rate):
    moment_one = BETA_ONE * moment_one + (1.0 - BETA_ONE) * gradient
    moment_two = BETA_TWO * moment_two + (1.0 - BETA_TWO) * gradient * gradient
    first_hat = moment_one / (1.0 - BETA_ONE**STEP)
    second_hat = moment_two / (1.0 - BETA_TWO**STEP)
    updated = weight_in - step_rate * (
        first_hat / (jnp.sqrt(second_hat) + EPS_ADAM) + decay_rate * weight_in
    )
    return (updated, moment_one, moment_two)


def adam_kernel(
    norm, grad, small_total, small, small_one, small_two, block, igrad, w, m, v,
    nw, nm, nv, ns, nsm, nsv, grad_norm, block_out, igrad_out,
):
    factor = jnp.minimum(1.0, CLIP_MAX / norm[0:1, 0:1])
    for i in range(PAIRS // ADAM_STEPS):
        g = grad[i].reshape(ROWS, WIDE) * factor
        for j in range(2):
            k = 2 * i + j
            nw[k], nm[k], nv[k] = adam_values(
                w[k], m[k], v[k], g[:, j * COL : (j + 1) * COL], D ** (-0.5), DECAY_RATE
            )
    block_out[...] = block[...]
    igrad_out[...] = igrad[...]

    @pl.when(pl.program_id(0) == 0)
    def _():
        first = ROWS * lax.axis_index("wide")
        row = lax.broadcasted_iota(jnp.int32, (D, ROWS), 0)
        column = lax.broadcasted_iota(jnp.int32, (D, ROWS), 1)
        pick = jnp.where(row == column + first, 1.0, 0.0)
        own = lax.dot_general(
            small_total[...], pick, (((1,), (0,)), ((), ())),
            precision=lax.Precision.HIGHEST, preferred_element_type=F32,
        )[0:5]
        ns[...], nsm[...], nsv[...] = adam_values(
            small[...], small_one[...], small_two[...], own * factor, RATE_SMALL, 0.0
        )
        grad_norm[...] = norm[0:1, 0:1]


def adam_all(norm, grad, small_total, smalls, rows, matrices):
    shape = matrices[0].shape
    flat = (LAYERS * 12, ROWS, COL)
    blk = pl.BlockSpec((2 * PAIRS // ADAM_STEPS, ROWS, COL), lambda i: (i, 0, 0))
    row_blk = pl.BlockSpec((TM // ADAM_STEPS, D), lambda i: (i, 0))

    def whole(*dims):
        return pl.BlockSpec(dims, lambda i: (0,) * len(dims))

    outs = pl.pallas_call(
        adam_kernel,
        grid=(ADAM_STEPS,),
        out_shape=(
            *(jax.ShapeDtypeStruct(flat, F32) for _ in range(3)),
            *(jax.ShapeDtypeStruct((5, ROWS), F32) for _ in range(3)),
            jax.ShapeDtypeStruct((1, 1), F32),
            *(jax.ShapeDtypeStruct((TM, D), F32) for _ in range(2)),
        ),
        in_specs=[
            whole(8, 128),
            pl.BlockSpec((PAIRS // ADAM_STEPS, PARTS, PART, WIDE), lambda i: (i, 0, 0, 0)),
            whole(8, D),
            *(whole(5, ROWS) for _ in range(3)),
            row_blk, row_blk,
            blk, blk, blk,
        ],
        out_specs=(
            blk, blk, blk, *(whole(5, ROWS) for _ in range(3)), whole(1, 1), row_blk, row_blk,
        ),
        compiler_params=pltpu.CompilerParams(vmem_limit_bytes=62 << 20),
        name="adam",
    )(norm, grad, small_total, *smalls, *rows, *(a.reshape(flat) for a in matrices))
    return tuple(o.reshape(shape) for o in outs[:3]), outs[3:6], outs[6].reshape(()), outs[7:]


def shards(patches, cotangent, mask_index, mask_count, weights, first_moment, second_moment,
           small_params, small_first, small_second):
    block_output, input_grad, grad_own, small_total, norm = big_step(
        weights.reshape(LAYERS * 12, ROWS, COL), patches, cotangent, mask_index, mask_count, small_params
    )
    new_matrices, new_smalls, grad_norm, rows = adam_all(
        norm, grad_own, small_total, (small_params, small_first, small_second),
        (block_output, input_grad), (weights, first_moment, second_moment),
    )
    return (*rows, *new_matrices, *new_smalls, grad_norm)


def layer_norm(values, gain):
    centre = values - jnp.mean(values, axis=-1, keepdims=True)
    spread = jnp.mean(centre * centre, axis=-1, keepdims=True)
    return centre * lax.rsqrt(spread + EPS_NORM) * gain


def exact_gelu(values):
    return jax.nn.gelu(values, approximate=False)


def gather_rows(share):
    return lax.all_gather(share, "narrow", axis=0, tiled=True)


def gather_grads(share):
    return lax.all_gather(share, "narrow", axis=0, tiled=True)


def branch_total(term, row_count):
    return lax.psum_scatter(
        term(jnp.int32(0), row_count * lax.axis_size("narrow")).astype(jnp.bfloat16),
        "narrow",
        scatter_dimension=0,
        tiled=True,
    ).astype(jnp.float32)


def input_total(term, row_count):
    return lax.psum_scatter(
        term(jnp.int32(0), row_count * lax.axis_size("narrow")).astype(jnp.bfloat16),
        "narrow",
        scatter_dimension=0,
        tiled=True,
    ).astype(jnp.float32)


def heads_of(values, clip_count):
    return values.reshape(clip_count, SEQ, values.shape[1] // HD, HD)


def attend_clip(parts):
    queries, key_rows, value_rows = parts
    scores = jnp.einsum(
        "qhd,khd->hqk", queries, key_rows, preferred_element_type=jnp.float32
    ) * HD ** (-0.5)
    probs = jax.nn.softmax(scores, axis=-1)
    return jnp.einsum(
        "hqk,khd->qhd", probs.astype(jnp.bfloat16), value_rows, preferred_element_type=jnp.float32
    ).astype(jnp.bfloat16)


def attend_back_clip(parts):
    queries, key_rows, value_rows, grad_mix = parts
    scale = HD ** (-0.5)
    scores = (
        jnp.einsum("qhd,khd->hqk", queries, key_rows, preferred_element_type=jnp.float32) * scale
    )
    probs = jax.nn.softmax(scores, axis=-1)
    grad_values = jnp.einsum(
        "hqk,qhd->khd", probs.astype(jnp.bfloat16), grad_mix, preferred_element_type=jnp.float32
    ).astype(jnp.bfloat16)
    grad_probs = jnp.einsum(
        "qhd,khd->hqk", grad_mix, value_rows, preferred_element_type=jnp.float32
    )
    grad_scores = probs * (grad_probs - jnp.sum(probs * grad_probs, axis=-1, keepdims=True))
    grad_scores = grad_scores.astype(jnp.bfloat16)
    grad_queries = (
        jnp.einsum("hqk,khd->qhd", grad_scores, key_rows, preferred_element_type=jnp.float32)
        * scale
    ).astype(jnp.bfloat16)
    grad_keys = (
        jnp.einsum("hqk,qhd->khd", grad_scores, queries, preferred_element_type=jnp.float32) * scale
    ).astype(jnp.bfloat16)
    return (grad_queries, grad_keys, grad_values)


def forward_layer(stream, weight, gain_one, gain_two):
    row_count = stream.shape[0]
    normed = gather_rows(layer_norm(stream, gain_one).astype(jnp.bfloat16))
    all_rows = normed.shape[0]
    clip_count = all_rows // SEQ
    project = jnp.einsum(
        "rd,sde->sre", normed, weight[0:3], preferred_element_type=jnp.float32
    ).astype(jnp.bfloat16)
    mixture = lax.map(
        attend_clip,
        (
            heads_of(project[0], clip_count),
            heads_of(project[1], clip_count),
            heads_of(project[2], clip_count),
        ),
    )
    mixture = mixture.reshape(all_rows, -1)

    def attn_term(first_row, row_num):
        return lax.dot_general(
            mixture, weight[3], (((1,), (1,)), ((), ())), preferred_element_type=jnp.float32
        )

    resid_one = stream + branch_total(attn_term, row_count)
    normed_two = gather_rows(layer_norm(resid_one, gain_two).astype(jnp.bfloat16))
    upward = jnp.einsum("rd,jde->jre", normed_two, weight[4:8], preferred_element_type=jnp.float32)
    hidden = exact_gelu(upward).astype(jnp.bfloat16)

    def mlp_term(first_row, row_num):
        return jnp.einsum("jre,jde->rd", hidden, weight[8:12], preferred_element_type=jnp.float32)

    result = resid_one + branch_total(mlp_term, row_count)
    return (result, (stream, normed, project, mixture, resid_one, normed_two, upward, hidden))


def backward_layer(grad_out, saved, weight, gain_one, gain_two):
    stream, normed, project, mixture, resid_one, normed_two, upward, hidden = saved
    row_count = stream.shape[0]
    all_rows = normed.shape[0]
    clip_count = all_rows // SEQ
    back_mlp = gather_grads(grad_out.astype(jnp.bfloat16))
    grad_down = jnp.einsum("rd,jre->jde", back_mlp, hidden, preferred_element_type=jnp.float32)
    grad_hidden = jnp.einsum(
        "rd,jde->jre", back_mlp, weight[8:12], preferred_element_type=jnp.float32
    )
    gelu_out, gelu_back = jax.vjp(exact_gelu, upward)
    grad_upward = gelu_back(grad_hidden)[0].astype(jnp.bfloat16)
    grad_up = jnp.einsum("rd,jre->jde", normed_two, grad_upward, preferred_element_type=jnp.float32)

    def up_term(first_row, row_num):
        return jnp.einsum(
            "jre,jde->rd", grad_upward, weight[4:8], preferred_element_type=jnp.float32
        )

    grad_normed_two = input_total(up_term, row_count)
    norm_out, norm_back = jax.vjp(layer_norm, resid_one, gain_two)
    part_stream, grad_gain_two = norm_back(grad_normed_two)
    grad_resid = grad_out + part_stream
    back_attn = gather_grads(grad_resid.astype(jnp.bfloat16))
    grad_out_proj = lax.dot_general(
        back_attn, mixture, (((0,), (0,)), ((), ())), preferred_element_type=jnp.float32
    )
    grad_mixture = jnp.dot(back_attn, weight[3], preferred_element_type=jnp.float32).astype(
        jnp.bfloat16
    )
    grad_heads = lax.map(
        attend_back_clip,
        (
            heads_of(project[0], clip_count),
            heads_of(project[1], clip_count),
            heads_of(project[2], clip_count),
            heads_of(grad_mixture, clip_count),
        ),
    )
    grad_project = jnp.stack([piece.reshape(all_rows, -1) for piece in grad_heads])
    grad_qkv = jnp.einsum("rd,sre->sde", normed, grad_project, preferred_element_type=jnp.float32)

    def qkv_term(first_row, row_num):
        return jnp.einsum(
            "sre,sde->rd", grad_project, weight[0:3], preferred_element_type=jnp.float32
        )

    grad_normed = input_total(qkv_term, row_count)
    norm_out_one, norm_back_one = jax.vjp(layer_norm, stream, gain_one)
    part_in, grad_gain_one = norm_back_one(grad_normed)
    grad_matrix = jnp.concatenate([grad_qkv, grad_out_proj[None], grad_up, grad_down], axis=0)
    return (grad_resid + part_in, grad_matrix, grad_gain_one, grad_gain_two)


def masked_rows(mask_index, mask_count, row_count):
    positions = lax.iota(jnp.int32, SEQ)
    slots = lax.iota(jnp.int32, mask_index.shape[1])
    live = slots[None, :] < mask_count[:, None]
    hits = (mask_index[:, :, None] == positions[None, None, :]) & live[:, :, None]
    flag_all = jnp.any(hits, axis=1).astype(jnp.float32).reshape(-1)
    return lax.dynamic_slice_in_dim(flag_all, lax.axis_index("narrow") * row_count, row_count, 0)


def shards_general(
    patches,
    cotangent,
    mask_index,
    mask_count,
    weights,
    first_moment,
    second_moment,
    small_params,
    small_first,
    small_second,
):
    row_count = patches.shape[0]
    narrow_size = lax.axis_size("narrow")
    owned_rows = weights.shape[2]
    matrices, small_low = (
        lax.all_gather(weights.astype(jnp.bfloat16), "wide", axis=2, tiled=True),
        lax.all_gather(small_params.astype(jnp.bfloat16), "wide", axis=1, tiled=True),
    )
    gains = small_low.astype(jnp.float32)
    flags = masked_rows(mask_index, mask_count, row_count)[:, None]
    stream = patches.astype(jnp.float32) * (1.0 - flags) + flags * gains[2 * LAYERS][None, :]
    saved_all = []
    for layer_idx in range(LAYERS):
        stream, saved = forward_layer(
            stream, matrices[layer_idx], gains[2 * layer_idx], gains[2 * layer_idx + 1]
        )
        saved_all.append(saved)
    grad_stream = cotangent
    grad_mats = [None] * LAYERS
    grad_gains = [None] * (2 * LAYERS)
    for layer_idx in reversed(range(LAYERS)):
        (
            grad_stream,
            grad_mats[layer_idx],
            grad_gains[2 * layer_idx],
            grad_gains[2 * layer_idx + 1],
        ) = backward_layer(
            grad_stream,
            saved_all[layer_idx],
            matrices[layer_idx],
            gains[2 * layer_idx],
            gains[2 * layer_idx + 1],
        )
    input_grad = grad_stream * (1.0 - flags)
    grad_embed = jnp.sum(grad_stream * flags, axis=0)
    grad_small = jnp.stack(grad_gains + [grad_embed])
    grad_matrix = jnp.stack(grad_mats)
    first_col = lax.axis_index("wide") * owned_rows
    small_total = lax.psum(grad_small, ("wide", "narrow"))
    small_own = lax.dynamic_slice_in_dim(small_total, first_col, owned_rows, 1)
    matrix_total = lax.psum(grad_matrix, "wide")
    matrix_own = lax.dynamic_slice_in_dim(matrix_total, first_col, owned_rows, 2)
    local_square = jnp.sum(matrix_own * matrix_own) + jnp.sum(small_own * small_own) / narrow_size
    grad_norm = jnp.sqrt(lax.psum(local_square, ("wide", "narrow")))
    factor = jnp.minimum(1.0, CLIP_MAX / grad_norm)
    new_weights, new_first, new_second = adam_values(
        weights, first_moment, second_moment, matrix_own * factor, D ** (-0.5), DECAY_RATE
    )
    new_small, new_small_first, new_small_second = adam_values(
        small_params, small_first, small_second, small_own * factor, RATE_SMALL, 0.0
    )
    return (
        stream,
        input_grad,
        new_weights,
        new_first,
        new_second,
        new_small,
        new_small_first,
        new_small_second,
        grad_norm,
    )


def solution(mesh):
    in_specs = (
        P(("wide", "narrow"), None),
        P(("wide", "narrow"), None),
        P("wide", None),
        P("wide"),
        P(None, None, "wide", "narrow"),
        P(None, None, "wide", "narrow"),
        P(None, None, "wide", "narrow"),
        P(None, "wide"),
        P(None, "wide"),
        P(None, "wide"),
    )
    out_specs = (
        P(("wide", "narrow"), None),
        P(("wide", "narrow"), None),
        P(None, None, "wide", "narrow"),
        P(None, None, "wide", "narrow"),
        P(None, None, "wide", "narrow"),
        P(None, "wide"),
        P(None, "wide"),
        P(None, "wide"),
        P(),
    )
    fits = mesh.shape["wide"] == NZ * NX and mesh.shape["narrow"] == 4
    step = shards if fits else shards_general
    return jax.shard_map(step, mesh=mesh, in_specs=in_specs, out_specs=out_specs, check_vma=False)
```

```python
import functools

import jax
import jax.numpy as jnp
from jax import lax
from jax.experimental import pallas as pl
from jax.experimental.pallas import tpu as pltpu
from jax.sharding import PartitionSpec as P

D = 768
HD = 64
LAYERS = 2
SEQ = 512
STEP = 10

EPS_NORM = 1e-06
BETA_ONE = 0.9
BETA_TWO = 0.999
EPS_ADAM = 1e-08
DECAY_RATE = 0.05
RATE_SMALL = 0.6
CLIP_MAX = 1.0

MESH = pl.DeviceIdType.MESH
F32 = jnp.float32
BF16 = jnp.bfloat16

PAIRS = 12
ADAM_STEPS = 2
PER = 6
NZ, NX = 4, 2
ROWS = 96
PARTS = 3
PART = ROWS // PARTS
COL = 192
WIDE = 2 * COL
SCALE = HD ** (-0.5)
TM = 256
TR = 64
HEADS_Y = COL // HD

WSLOTS = 4
STEPS = 100
BEGUN = 3
PLAN_WORDS = (
    (
        0, 0, 0, 0, 32, 516, 0, 8240, 4608, 131073, 0, 4112,
        0, 256, 272, 4099, 65792, 32, 4096, 65537, 256, 65552, 8192, 65792,
        0, 0, 0, 65536, 256, 69664, 0, 4352, 256, 0, 0, 69632,
        0, 65536, 4096, 0, 65536, 0, 0, 0, 65536, 0, 0, 0,
        0, 0, 0, 0, 0, 0, 0, 0, 0, 0, 0, 0,
        0, 0, 0, 0, 0, 0, 0, 0, 0, 0, 0, 0,
        0, 0, 0, 0, 0, 0, 0, 0, 0, 0, 0, 0,
        0, 0, 0, 0, 0, 0, 0, 0, 0, 0, 0, 0,
        0, 0, 0, 0,
    ),
    (
        0, 0, 0, 0, 0, 3, 0, 32, 8704, 7, 0, 12368,
        0, 1024, 1376, 16392, 132608, 112, 20480, 196619, 1792, 262288, 24576, 329728,
        0, 0, 0, 393216, 2304, 491680, 0, 39424, 2816, 0, 0, 565248,
        0, 589824, 45056, 0, 655360, 0, 0, 0, 720896, 0, 0, 0,
        0, 0, 0, 0, 0, 0, 0, 0, 0, 0, 0, 0,
        0, 0, 0, 0, 0, 0, 0, 0, 0, 0, 0, 0,
        0, 0, 0, 0, 0, 0, 0, 0, 0, 0, 0, 0,
        0, 0, 0, 0, 0, 0, 0, 0, 0, 0, 0, 0,
        0, 0, 0, 0,
    ),
    (
        0, 0, 0, 0, 0, 0, 0, 0, 0, 0, 0, 0,
        0, 0, 0, 0, 0, 0, 0, 0, 0, 0, 0, 0,
        0, 0, 0, 0, 0, 0, 0, 0, 0, 0, 0, 0,
        0, 0, 0, 0, 0, 0, 0, 1, 0, 0, 0, 1,
        0, 0, 1, 16, 1, 0, 0, 0, 256, 0, 0, 16,
        0, 33, 0, 257, 4096, 16, 256, 257, 0, 0, 4352, 1,
        16, 0, 4096, 4128, 4353, 256, 1, 256, 0, 0, 1, 69648,
        0, 0, 0, 0, 0, 0, 16, 0, 200705, 0, 256, 65536,
        0, 4352, 16, 475664,
    ),
    (
        0, 0, 0, 0, 0, 0, 0, 0, 0, 0, 0, 0,
        0, 0, 0, 0, 0, 0, 0, 0, 0, 0, 0, 0,
        0, 0, 0, 0, 0, 0, 0, 0, 0, 0, 0, 0,
        0, 0, 0, 0, 0, 0, 0, 0, 0, 0, 0, 1,
        0, 0, 2, 0, 3, 0, 0, 0, 0, 0, 0, 16,
        0, 36, 0, 261, 0, 64, 512, 774, 0, 0, 5120, 7,
        80, 0, 8192, 12384, 17672, 1536, 9, 1792, 0, 0, 10, 20608,
        0, 0, 0, 0, 0, 0, 144, 0, 90123, 0, 2048, 262144,
        0, 30976, 160, 363184,
    ),
    (
        0, 0, 1, 0, 0, 2, 0, 3, 0, 4, 0, 5,
        6, 70, 7, 8, 0, 9, 0, 73, 0, 10, 0, 11,
        12, 35, 0, 36, 0, 37, 38, 102, 39, 40, 0, 41,
        0, 105, 45, 0, 42, 46, 110, 0, 43, 47, 111, 44,
        48, 49, 50, 51, 52, 53, 54, 55, 56, 118, 119, 120,
        57, 58, 59, 60, 13, 14, 78, 15, 79, 16, 17, 18,
        19, 20, 21, 22, 23, 24, 86, 87, 88, 25, 26, 27,
        28, 29, 0, 0, 0, 0, 0, 0, 0, 30, 0, 0,
        0, 0, 0, 0,
    ),
)


def mm(a, b):
    return lax.dot_general(a, b, (((1,), (0,)), ((), ())), preferred_element_type=F32)


def mm_nt(a, b):
    return lax.dot_general(a, b, (((1,), (1,)), ((), ())), preferred_element_type=F32)


def mm_tn(a, b):
    return lax.dot_general(a, b, (((0,), (0,)), ((), ())), preferred_element_type=F32)


def loop(count, body):
    def wrapped(i, carry):
        body(i)
        return carry

    lax.fori_loop(0, count, wrapped, 0)


def rows_at(i, size):
    return pl.ds(pl.multiple_of(i * size, size), size)


def step_kernel(
    weights, patch, cot, mask_index, mask_count, small,
    out_block, out_igrad, out_grad, out_small, out_norm,
    G, WF, S, R1, NRM, NRM2, QK, V, MIX, GP, HID, GR, ACC, XS, XR, BK, TA, TB, GU, GM, DQK, DV,
    FL, GAIN, GPIECE, SG, SR, NB, NZC, NXY, RB0Y, RB0X, RB1, RB2, RB2X, RBZ, RBM, RBMZ,
    wf_s, ag_s, ag_r, ex_s, ex_r, in_s, in_r, lc_s, gn_s, gn_r, fs_s, fs_r, nm_s, nm_r,
):
    wide = lax.axis_index("wide")
    narrow = lax.axis_index("narrow")
    z, x = wide // NX, wide % NX
    y, c = narrow // 2, narrow % 2

    dev_core = (wide, 2 * y + 1 - c)
    dev_x = (z * NX + 1 - x, narrow)
    dev_y = (wide, 2 * (1 - y) + c)

    def z_to(k):
        return (z + k) % NZ

    def z_from(k):
        return (z + NZ - k) % NZ

    def dev_z(k):
        return (z_to(k) * NX + x, narrow)

    dev_xy = (z * NX + 1 - x, 2 * (1 - y) + c)

    def dev_zc(k):
        return (z_to(k) * NX + x, 2 * y + 1 - c)

    def load_pair(p):
        return pltpu.make_async_copy(weights.at[pl.ds(2 * p, 2)], WF.at[p % WSLOTS], wf_s.at[p % WSLOTS])

    for p in range(WSLOTS):
        load_pair(p).start()

    greeted = [dev_core, dev_x, dev_y, dev_xy] + [dev(k) for k in range(1, NZ) for dev in (dev_z, dev_zc)]
    barrier = pltpu.get_barrier_semaphore()
    for dev in greeted:
        pl.semaphore_signal(barrier, inc=1, device_id=dev, device_id_type=MESH)
    pl.semaphore_wait(barrier, len(greeted))

    def remote(src, dst, send, recv, dev):
        return pltpu.make_async_remote_copy(
            src_ref=src, dst_ref=dst, send_sem=send, recv_sem=recv, device_id=dev, device_id_type=MESH
        )

    def lazy(*what):
        return lambda: remote(*what)

    ALL = slice(None)
    own = {"x": x, "y": y, "z": z}
    far = NZ - 1
    inner = jnp.logical_and(z > 0, z < far)
    outer = jnp.logical_or(z == 0, z == far)

    def block(p, h, where):
        return G.at[p, where["y"], where["z"], where["x"], h]

    def gather_order(even, h):
        if h == 0:
            return ("z", "x", "y") if even else ("z", "y", "x")
        return ("x", "z", "y") if h == 1 else ("y", "z", "x")

    def holding(axes):
        return {q: (ALL if q in axes else own[q]) for q in own}

    def along(axis):
        return (3, dev_x, 1 - x) if axis == "x" else (4, dev_y, 1 - y)

    def along_z(action):
        @pl.when(z != far)
        def _():
            action(1)

        action(2)

        @pl.when(z != 0)
        def _():
            action(3)

    def each_part(p, action):
        @pl.when(p % 2 == 0)
        def _():
            action(0, gather_order(True, 0))

        @pl.when(p % 2 == 1)
        def _():
            action(0, gather_order(False, 0))

        for h in range(1, PARTS):
            action(h, gather_order(True, h))

    def gather_plain(p, h, order, axis):
        slot, dev, there = along(axis)
        have = holding(order[: order.index(axis)])
        src = block(p, h, have)
        got = block(p, h, {**have, axis: there})
        send, recv = ag_s.at[p, h, slot], ag_r.at[p, h, slot]
        return lazy(src, src, send, recv, dev), lazy(got, got, send, recv, dev)

    def gather_z(p, h, order, k):
        have = holding(order[: order.index("z")])
        src = block(p, h, have)
        got = block(p, h, {**have, "z": z_from(k)})
        send, recv = ag_s.at[p, h, k - 1], ag_r.at[p, h, k - 1]
        return lazy(src, src, send, recv, dev_z(k)), lazy(got, got, send, recv, dev_z(k))

    def gather_relay(p, h, order):
        have = holding(order[: order.index("z")])
        src = block(p, h, {**have, "z": z_from(2)})
        dev = (far * (z - 1) * NX + x, narrow)
        return lazy(src, src, ag_s.at[p, h, 5], ag_r.at[p, h, 2 * (z - 1)], dev)

    def gather_steps(order):
        at = order.index("z") + 1
        return order[:at] + ("relay",) + order[at:]

    def gather_issue(p, step):
        def action(h, order):
            steps = gather_steps(order)
            before = steps[step - 1] if step > 0 else None
            if before == "z":
                gather_z(p, h, order, 2)[1]().wait_recv()
            elif before == "relay":
                for k in (1, 3):
                    gather_z(p, h, order, k)[1]().wait_recv()
            elif before is not None:
                gather_plain(p, h, order, before)[1]().wait_recv()
            if step == len(steps):
                return
            if steps[step] == "z":
                along_z(lambda k: gather_z(p, h, order, k)[0]().start())
            elif steps[step] == "relay":

                @pl.when(inner)
                def _():
                    gather_relay(p, h, order)().start()

            else:
                gather_plain(p, h, order, steps[step])[0]().start()

        each_part(p, action)

    def gather_sent(p):
        def action(h, order):
            along_z(lambda k: gather_z(p, h, order, k)[0]().wait_send())

            @pl.when(inner)
            def _():
                gather_relay(p, h, order)().wait_send()

            for axis in ("x", "y"):
                gather_plain(p, h, order, axis)[0]().wait_send()

        each_part(p, action)

    def pack(p):
        load_pair(p).wait()
        slot = p % WSLOTS
        both = jnp.concatenate([WF[slot, 0].astype(BF16), WF[slot, 1].astype(BF16)], axis=1)
        G[p, y, z, x] = both.reshape(PARTS, PART, WIDE)

        @pl.when(p + WSLOTS < PAIRS)
        def _():
            load_pair(p + WSLOTS).start()

    half = TM * c
    BKh = BK.at[pl.ds(pl.multiple_of(half, TM), TM)]
    GRh = GR.at[pl.ds(pl.multiple_of(half, TM), TM)]
    other = TM * (1 - c)
    BKo = BK.at[pl.ds(pl.multiple_of(other, TM), TM)]
    GRo = GR.at[pl.ds(pl.multiple_of(other, TM), TM)]
    patch_out = remote(patch, BKh, in_s.at[0], in_r.at[0], dev_core)
    patch_in = remote(patch, BKo, in_s.at[0], in_r.at[0], dev_core)
    cot_out = remote(cot, GRh, in_s.at[1], in_r.at[1], dev_core)
    cot_in = remote(cot, GRo, in_s.at[1], in_r.at[1], dev_core)
    patch_own = pltpu.make_async_copy(patch, BKh, lc_s.at[0])
    cot_own = pltpu.make_async_copy(cot, GRh, lc_s.at[1])
    patch_own.start()
    cot_own.start()
    patch_out.start()
    GPIECE[z, x] = jnp.zeros((8, 128), F32)
    GPIECE[z, x, 0:5, 0:ROWS] = small[...].astype(BF16).astype(F32)
    gain_z = [
        (
            remote(GPIECE.at[z, x], GPIECE.at[z, x], gn_s.at[k - 1], gn_r.at[k - 1], dev_z(k)),
            remote(GPIECE.at[z_from(k), x], GPIECE.at[z_from(k), x], gn_s.at[k - 1], gn_r.at[k - 1], dev_z(k)),
        )
        for k in range(1, NZ)
    ]
    gain_x = (
        remote(GPIECE.at[:, x], GPIECE.at[:, x], gn_s.at[3], gn_r.at[3], dev_x),
        remote(GPIECE.at[:, 1 - x], GPIECE.at[:, 1 - x], gn_s.at[3], gn_r.at[3], dev_x),
    )
    for s, _ in gain_z:
        s.start()
    def begin(p):
        pack(p)
        gather_issue(p, 0)

    loop(BEGUN, begin)
    cot_out.start()
    loop(PAIRS - BEGUN, lambda i: pack(i + BEGUN))

    index_row = mask_index[pl.ds(y, 1), :]
    count = mask_count[y]
    spot = lax.broadcasted_iota(jnp.int32, (SEQ, index_row.shape[1]), 0)
    live = lax.broadcasted_iota(jnp.int32, (1, index_row.shape[1]), 1) < count
    hits = jnp.where(jnp.logical_and(spot == index_row, live), 1.0, 0.0)
    FL[...] = jnp.max(hits, axis=1, keepdims=True)

    def gains_across(l, yy):
        for _, r in gain_z:
            r.wait_recv()
        gain_x[0].start()

    def first_rows(l, yy):
        gain_x[1].wait_recv()
        lane = lax.broadcasted_iota(jnp.int32, (128, D), 0)
        feature = lax.broadcasted_iota(jnp.int32, (128, D), 1)
        gains = jnp.zeros((8, D), F32)
        for zz in range(NZ):
            for xx in range(NX):
                place = jnp.logical_and(feature - ROWS * (zz * NX + xx) == lane, lane < ROWS)
                gains = gains + mm(GPIECE[zz, xx].astype(BF16), jnp.where(place, 1.0, 0.0).astype(BF16))
        GAIN[...] = gains
        patch_own.wait()
        patch_in.wait_recv()
        embed = GAIN[4:5, :]

        def mask_tile(i):
            rows = rows_at(i, TR)
            flag = FL[rows, :]
            S[0, rows, :] = BK[rows, :].astype(F32) * (1.0 - flag) + flag * embed

        loop(SEQ // TR, mask_tile)

    def norm_parts(values):
        centre = values - jnp.mean(values, axis=-1, keepdims=True)
        spread = jnp.mean(centre * centre, axis=-1, keepdims=True)
        return centre, lax.rsqrt(spread + EPS_NORM)

    def norm_into(dst, src, gain_row):
        gain = GAIN[pl.ds(gain_row, 1), :]

        def tile(i):
            rows = rows_at(i, TR)
            centre, inv = norm_parts(src[rows, :])
            dst[rows, :] = (centre * inv * gain).astype(BF16)

        loop(SEQ // TR, tile)

    def matrix(p, yy):
        return G[p, yy].reshape(D, WIDE)

    def exchange_copy(e, i):
        rows = rows_at(i, TM)
        return remote(XS.at[rows], XR.at[e, rows], ex_s.at[i], ex_r.at[e, i], dev_core)

    def give(e, value):
        XS[...] = value.astype(BF16)
        loop(SEQ // TM, lambda i: exchange_copy(e, i).start())

    def receive(e, take):
        def chunk(i):
            exchange_copy(e, i).wait_recv()

            def tile(j):
                rows = pl.ds(pl.multiple_of(i * TM + j * TR, TR), TR)
                take(rows, XS[rows, :].astype(F32) + XR[e, rows, :].astype(F32))

            loop(TM // TR, tile)

        loop(SEQ // TM, chunk)
        loop(SEQ // TM, lambda i: exchange_copy(e, i).wait_send())

    def attend(l, yy):
        def tile(i):
            rows = rows_at(i, TM)
            outs = []
            for hd in range(HEADS_Y):
                lo = hd * HD
                q = QK[l, yy, rows, lo : lo + HD]
                k = QK[l, yy, :, COL + lo : COL + lo + HD]
                v = V[l, yy, :, lo : lo + HD]
                s = mm_nt(q, k) * SCALE
                e = jnp.exp(s - jnp.max(s, axis=1, keepdims=True))
                probs = e / jnp.sum(e, axis=1, keepdims=True)
                outs.append(mm(probs.astype(BF16), v))
            MIX[l, yy, rows, :] = jnp.concatenate(outs, axis=1).astype(BF16)

        loop(SEQ // TM, tile)

    def attend_back(l, yy, hd):
        lo = hd * HD
        k = QK[l, yy, :, COL + lo : COL + lo + HD]
        v = V[l, yy, :, lo : lo + HD]

        def tile(i, carry):
            dk, dv = carry
            rows = rows_at(i, TM)
            q = QK[l, yy, rows, lo : lo + HD]
            dm = GM[yy, rows, lo : lo + HD]
            s = mm_nt(k, q) * SCALE
            e = jnp.exp(s - jnp.max(s, axis=0, keepdims=True))
            probs = e / jnp.sum(e, axis=0, keepdims=True)
            dp = mm_nt(v, dm)
            ds = probs * (dp - jnp.sum(probs * dp, axis=0, keepdims=True))
            ds = ds.astype(BF16)
            dv = dv + mm(probs.astype(BF16), dm)
            dk = dk + mm(ds, q)
            dq = mm_tn(ds, k) * SCALE
            DQK[yy, rows, lo : lo + HD] = dq.astype(BF16)
            return dk, dv

        zero = jnp.zeros((SEQ, HD), F32)
        dk, dv = lax.fori_loop(0, SEQ // TM, tile, (zero, zero))
        DQK[yy, :, COL + lo : COL + lo + HD] = (dk * SCALE).astype(BF16)
        DV[yy, :, lo : lo + HD] = dv.astype(BF16)

    def up_part(l, u, yy, p):
        ACC[:, 0:WIDE] = mm(NRM2[l], matrix(p, yy))

        def gelu(i):
            rows = rows_at(i, TR)
            v = ACC[rows, 0:WIDE]
            cdf = 0.5 * (1.0 + lax.erf(v * (2.0 ** -0.5)))
            HID[l, u, yy, rows, :] = (v * cdf).astype(BF16)
            pdf = jnp.exp(-0.5 * v * v) * 0.3989422804014327
            GP[l, u, yy, rows, :] = (cdf + v * pdf).astype(BF16)

        loop(SEQ // TR, gelu)

    def ln_one(l, yy):
        norm_into(NRM.at[l], S.at[l], 2 * l)

    def project_qk(l, yy):
        def one(side):
            QK[l, side] = mm(NRM[l], matrix(l * PER, side)).astype(BF16)

        loop(2, one)

    def project_v(l, yy):
        def one(side):
            V[l, side] = mm(NRM[l], matrix(l * PER + 1, side)[:, :COL]).astype(BF16)

        loop(2, one)

    def attn_out(l, yy):
        p = l * PER + 1
        total = mm_nt(MIX[l, 0], matrix(p, 0)[:, COL:])
        give(0, total + mm_nt(MIX[l, 1], matrix(p, 1)[:, COL:]))

    def attn_resid(l, yy):
        def take(rows, total):
            R1[l, rows, :] = S[l, rows, :] + total

        receive(0, take)
        norm_into(NRM2.at[l], R1.at[l], 2 * l + 1)

    def up(l, u):
        loop(2, lambda side: up_part(l, u, side, l * PER + 2 + u))

    def down_one(l, yy):
        p = l * PER + 4
        ACC[...] = mm_nt(HID[l, 0, 0], matrix(p, 0)) + mm_nt(HID[l, 0, 1], matrix(p, 1))

    def down_two(l, yy):
        p = l * PER + 5
        total = ACC[...] + mm_nt(HID[l, 1, 0], matrix(p, 0))
        give(1, total + mm_nt(HID[l, 1, 1], matrix(p, 1)))

    def layer_end(l, yy):
        def take(rows, total):
            value = R1[l, rows, :] + total

            @pl.when(l == 0)
            def _():
                S[1, rows, :] = value

            @pl.when(l == 1)
            def _():
                ACC[rows, :] = value

        receive(1, take)

        @pl.when(l == 1)
        def _():
            block_copy.start()

    block_copy = pltpu.make_async_copy(ACC.at[pl.ds(pl.multiple_of(half, TM), TM)], out_block, lc_s.at[2])

    def scatter_plain(p, h, order, axis):
        slot, dev, there = along(axis)
        place = order.index(axis)
        have = {q: (own[q] if q in order[:place] else ALL) for q in own}
        if place == 0:
            dst = (RB0Y if axis == "y" else RB0X).at[p if h > 0 else PAIRS + p // 2]
        else:
            dst = RB1.at[p] if h == 0 else RB2X.at[p, h - 1]
        send, recv = ag_s.at[p, h, slot], ag_r.at[late(p), h, slot]
        src = block(p, h, {**have, axis: there})
        return lazy(src, dst, send, recv, dev), lazy(dst, dst, send, recv, dev), dst

    def late(p):
        return (p + PER) % PAIRS

    def scatter_have(order):
        return {q: (own[q] if q in order[: order.index("z")] else ALL) for q in own}

    def scatter_z(p, h, order, k):
        dst = RB2.at[p, k - 1] if h == 0 else RBZ.at[p, h - 1, k - 1]
        send, recv = ag_s.at[p, h, k - 1], ag_r.at[late(p), h, k - 1]
        src = block(p, h, {**scatter_have(order), "z": z_to(k)})
        return lazy(src, dst, send, recv, dev_z(k)), lazy(dst, dst, send, recv, dev_z(k)), dst

    def scatter_merge(p, h, order):
        dst = RBM.at[p] if h == 0 else RBMZ.at[p, h - 1]
        dev = ((1 + z // far) * NX + x, narrow)
        send, recv = ag_s.at[p, h, 5], ag_r.at[late(p), h, 5]
        src = block(p, h, {**scatter_have(order), "z": far - z})
        return lazy(src, dst, send, recv, dev), lazy(dst, dst, send, recv, dev), dst

    def scatter_steps(order):
        at = order.index("z")
        return order[:at] + ("merge",) + order[at:]

    def scatter_issue(p, step):
        def action(h, forward_order):
            order = forward_order[::-1]
            steps = scatter_steps(order)
            before = steps[step - 1] if step > 0 else None
            if before is not None and before != "merge":
                have = {q: (own[q] if q in order[: order.index(before) + 1] else ALL) for q in own}
                view = block(p, h, have)
                if before == "z":
                    scatter_z(p, h, order, 2)[1]().wait_recv()

                    @pl.when(z != 0)
                    def _():
                        scatter_z(p, h, order, 1)[1]().wait_recv()

                    @pl.when(z != far)
                    def _():
                        scatter_z(p, h, order, 3)[1]().wait_recv()

                    total = view[...].astype(F32) + scatter_z(p, h, order, 2)[2][...].astype(F32)
                    for k, there in ((1, z != 0), (3, z != far)):
                        total = total + jnp.where(there, scatter_z(p, h, order, k)[2][...].astype(F32), 0.0)
                else:
                    scatter_plain(p, h, order, before)[1]().wait_recv()
                    total = view[...].astype(F32) + scatter_plain(p, h, order, before)[2][...].astype(F32)
                if step < len(steps):
                    view[...] = total.astype(BF16)
                else:
                    out_grad[p, h] = total
                    NB[...] += fold(total * total)
            if step == len(steps):
                return
            if steps[step] == "merge":

                @pl.when(outer)
                def _():
                    scatter_merge(p, h, order)[0]().start()

            elif steps[step] == "z":

                @pl.when(inner)
                def _():
                    scatter_merge(p, h, order)[1]().wait_recv()
                    view = block(p, h, {**scatter_have(order), "z": z_to(2)})
                    term = scatter_merge(p, h, order)[2][...].astype(F32)
                    view[...] = (view[...].astype(F32) + term).astype(BF16)

                along_z(lambda k: scatter_z(p, h, order, k)[0]().start())
            else:
                scatter_plain(p, h, order, steps[step])[0]().start()

        each_part(p, action)

    def fold(sq):
        sq = jnp.sum(sq.reshape(PART // 8, 8, WIDE), axis=0)
        return sq[:, 0:128] + sq[:, 128:256] + sq[:, 256:384]

    def scatter_sent(p):
        def action(h, forward_order):
            order = forward_order[::-1]
            for axis in ("x", "y"):
                scatter_plain(p, h, order, axis)[0]().wait_send()

            @pl.when(outer)
            def _():
                scatter_merge(p, h, order)[0]().wait_send()

            along_z(lambda k: scatter_z(p, h, order, k)[0]().wait_send())

        each_part(p, action)

    NB[...] = jnp.zeros((8, 128), F32)
    SG[...] = jnp.zeros_like(SG)

    def transpose_into(dst, src):
        def tile(i):
            rows = rows_at(i, 128)
            dst[:, rows] = jnp.transpose(src[rows, :])

        loop(SEQ // 128, tile)

    def put_grad(p, yy, left, right):
        G[p, yy] = mm(left[...], right).astype(BF16).reshape(NZ, NX, PARTS, PART, WIDE)

    def norm_back(e, src, gain_row):
        gain = GAIN[pl.ds(gain_row, 1), :]
        def take(rows, dn):
            centre, inv = norm_parts(src[rows, :])
            xhat = centre * inv
            dh = dn * gain
            dv = inv * (
                dh
                - jnp.mean(dh, axis=-1, keepdims=True)
                - xhat * jnp.mean(dh * xhat, axis=-1, keepdims=True)
            )
            GR[rows, :] += dv
            SG[pl.ds(gain_row, 1), :] += jnp.sum(dn * xhat, axis=0, keepdims=True)

        receive(e, take)

    def cast_rows(dst, src):
        def tile(i):
            rows = rows_at(i, TR)
            dst[rows, :] = src[rows, :].astype(BF16)

        loop(SEQ // TR, tile)

    def both(action):
        loop(2, action)

    def back_prepare(l, yy):
        @pl.when(l == 1)
        def _():
            cot_own.wait()
            cot_in.wait_recv()
            cot_out.wait_send()

        cast_rows(BK, GR)
        transpose_into(TA, BK)
        transpose_into(TB, NRM2.at[l])

    def back_down(l, u, side):
        p = l * PER + 4 + u

        @pl.when(side == 0)
        def _():
            gather_sent(p)

        gh = mm(BK[...], matrix(p, side))
        GU[u, side] = (gh * GP[l, u, side].astype(F32)).astype(BF16)
        put_grad(p, side, TA, HID[l, u, side])

    def back_up_sum(l, yy):
        p = l * PER + 2

        @pl.when(l == 1)
        def _():
            block_copy.wait()

        ACC[...] = mm_nt(GU[0, 0], matrix(p, 0)) + mm_nt(GU[0, 1], matrix(p, 1))

    def back_up_give(l, yy):
        p = l * PER + 3
        total = ACC[...] + mm_nt(GU[1, 0], matrix(p, 0))
        give(0, total + mm_nt(GU[1, 1], matrix(p, 1)))

    def back_up(l, u):
        p = l * PER + 2 + u
        gather_sent(p)
        both(lambda side: put_grad(p, side, TB, GU[u, side]))

    def back_norm_two(l, yy):
        norm_back(0, R1.at[l], 2 * l + 1)

    def back_attn_prepare(l, yy):
        cast_rows(BK, GR)
        transpose_into(TA, BK)
        transpose_into(TB, NRM.at[l])

        def grad_mix(side):
            GM[side] = mm(BK[...], matrix(l * PER + 1, side)[:, COL:]).astype(BF16)

        both(grad_mix)

    def back_attn_grads(l, yy):
        p = l * PER + 1
        gather_sent(p)
        ACC[...] = mm_nt(DV[0], matrix(p, 0)[:, :COL]) + mm_nt(DV[1], matrix(p, 1)[:, :COL])

        def grads(side):
            gv = mm(TB[...], DV[side])
            go = mm(TA[...], MIX[l, side])
            pair = jnp.concatenate([gv, go], axis=1).astype(BF16)
            G[p, side] = pair.reshape(NZ, NX, PARTS, PART, WIDE)

        both(grads)

    def back_qk_give(l, yy):
        p = l * PER
        total = ACC[...] + mm_nt(DQK[0], matrix(p, 0))
        give(1, total + mm_nt(DQK[1], matrix(p, 1)))

    def back_qk(l, yy):
        p = l * PER
        gather_sent(p)
        both(lambda side: put_grad(p, side, TB, DQK[side]))

    def back_norm_one(l, yy):
        norm_back(1, S.at[l], 2 * l)

    def position(i):
        s = i % PER
        slot = jnp.where(s < 2, s + 4, jnp.where(s < 4, s, 5 - s))
        return (LAYERS - 1 - i // PER) * PER + slot

    def scatter_at(t, phase):
        scatter_issue(position(t), phase)

    igrad_copy = pltpu.make_async_copy(GRh, out_igrad, lc_s.at[3])
    place = 2 * y + x
    around = ((2 * y + 1 - x, dev_x), (2 * (1 - y) + x, dev_y), (2 * (1 - y) + 1 - x, dev_xy))

    def small_z(k):
        got = SR.at[z_from(k), 0]
        return (
            remote(SR.at[z, 0], SR.at[z, 0], fs_s.at[k - 1], fs_r.at[k - 1], dev_z(k)),
            remote(got, got, fs_s.at[k - 1], fs_r.at[k - 1], dev_z(k)),
        )

    def small_xy(k):
        there, dev = around[k]
        return (
            remote(SR.at[place, 1], SR.at[place, 1], fs_s.at[3 + k], fs_r.at[3 + k], dev),
            remote(SR.at[there, 1], SR.at[there, 1], fs_s.at[3 + k], fs_r.at[3 + k], dev),
        )

    def rows_done():
        def finish_tile(i):
            rows = rows_at(i, TR)
            flag = FL[rows, :]
            value = GR[rows, :]
            SG[4:5, :] += jnp.sum(value * flag, axis=0, keepdims=True)
            GR[rows, :] = value * (1.0 - flag)

        loop(SEQ // TR, finish_tile)
        igrad_copy.start()
        SR[z, 0] = SG[...]
        for k in range(1, NZ):
            small_z(k)[0].start()

    def small_sums():
        for k in range(1, NZ):
            small_z(k)[1].wait_recv()
        SR[place, 1] = SR[0, 0] + SR[1, 0] + SR[2, 0] + SR[3, 0]
        for k in range(3):
            small_xy(k)[0].start()

    pieces = {
        "g1": gains_across,
        "g2": first_rows,
        "ln1": ln_one,
        "qk": project_qk,
        "v": project_v,
        "at": attend,
        "out": attn_out,
        "res": attn_resid,
        "up": up,
        "dn0": down_one,
        "dn1": down_two,
        "fin": layer_end,
        "b4p": back_prepare,
        "b4": lambda l, side: back_down(l, 0, side),
        "b5": lambda l, side: back_down(l, 1, side),
        "b2a": back_up_sum,
        "b2b": lambda l, yy: back_up(l, 0),
        "b3a": back_up_give,
        "b3b": lambda l, yy: back_up(l, 1),
        "b3c": back_norm_two,
        "b1p": back_attn_prepare,
        "ab0": lambda l, side: attend_back(l, side, 0),
        "ab1": lambda l, side: attend_back(l, side, 1),
        "ab2": lambda l, side: attend_back(l, side, 2),
        "b1f": back_attn_grads,
        "b0a": back_qk_give,
        "b0b": back_qk,
        "b0c": back_norm_one,
        "rows": lambda l, yy: rows_done(),
        "small": lambda l, yy: small_sums(),
    }
    def digit(word, k, base):
        return lax.rem(lax.div(word, base**k), base)

    def plan_of(m, low, high):
        if high - low == 1:
            return tuple(jnp.int32(words[low]) for words in PLAN_WORDS)
        middle = (low + high) // 2
        return lax.cond(m < middle, lambda: plan_of(m, low, middle), lambda: plan_of(m, middle, high))

    def micro(m):
        plan = plan_of(m, 0, STEPS)
        for counts, firsts, action in ((plan[0], plan[1], gather_issue), (plan[2], plan[3], scatter_at)):

            @pl.when(counts > 0)
            def _():
                for kind in range(5):
                    count, first = digit(counts, kind, 16), digit(firsts, kind, 16)

                    @pl.when(count > 0)
                    def _():
                        def one(i, carry):
                            action(first + i, kind)
                            return carry

                        lax.fori_loop(0, count, one, 0)

        word = plan[4]

        @pl.when(word > 0)
        def _():
            what, l, yy = lax.rem(word, 32), digit(lax.div(word, 32), 0, 2), lax.div(word, 64)
            for i, action in enumerate(pieces.values()):

                @pl.when(what == i + 1)
                def _():
                    action(l, yy)

    loop(STEPS, micro)

    own_square = jnp.sum(jnp.sum(NB[...], axis=1, keepdims=True), axis=0, keepdims=True)
    NZC[z, c] = jnp.broadcast_to(own_square, (8, 128))
    nm_z = []
    for j, (zz, cc, frm, dev) in enumerate(
        [(z, 1 - c, z, dev_core)]
        + [(z_to(k), c, z_from(k), dev_z(k)) for k in range(1, NZ)]
        + [(z_to(k), 1 - c, z_from(k), dev_zc(k)) for k in range(1, NZ)]
    ):
        got = NZC.at[frm, cc]
        nm_z.append(
            (
                remote(NZC.at[z, c], NZC.at[z, c], nm_s.at[j], nm_r.at[j], dev),
                remote(got, got, nm_s.at[j], nm_r.at[j], dev),
            )
        )
    for s, _ in nm_z:
        s.start()
    for k in range(3):
        small_xy(k)[1].wait_recv()
    total_small = SR[0, 1] + SR[1, 1] + SR[2, 1] + SR[3, 1]
    out_small[...] = total_small
    small_square = jnp.sum(jnp.sum(total_small * total_small, axis=1, keepdims=True), axis=0, keepdims=True)
    for _, r in nm_z:
        r.wait_recv()
    square = NZC[0, 0] + NZC[0, 1]
    for zz in range(1, NZ):
        square = square + (NZC[zz, 0] + NZC[zz, 1])
    NXY[place] = square
    nm_xy = [
        (
            remote(NXY.at[place], NXY.at[place], nm_s.at[7 + k], nm_r.at[7 + k], dev),
            remote(NXY.at[there], NXY.at[there], nm_s.at[7 + k], nm_r.at[7 + k], dev),
        )
        for k, (there, dev) in enumerate(around)
    ]
    for s, _ in nm_xy:
        s.start()
    for _, r in nm_xy:
        r.wait_recv()
    out_norm[...] = jnp.sqrt(NXY[0] + NXY[1] + NXY[2] + NXY[3] + small_square)

    for s, _ in [small_z(k) for k in range(1, NZ)] + [small_xy(k) for k in range(3)] + nm_z + nm_xy + gain_z:
        s.wait_send()
    gain_x[0].wait_send()
    patch_out.wait_send()
    loop(PAIRS, scatter_sent)
    igrad_copy.wait()


def big_step(weights, patches, cotangent, mask_index, mask_count, small):
    vm = pl.BlockSpec(memory_space=pltpu.VMEM)
    hb = pl.BlockSpec(memory_space=pl.ANY)
    sm = pl.BlockSpec(memory_space=pltpu.SMEM)
    dma = pltpu.SemaphoreType.DMA
    V = pltpu.VMEM
    scratch = [
        V((PAIRS, 2, NZ, NX, PARTS, PART, WIDE), BF16),
        V((WSLOTS, 2, ROWS, COL), F32),
        V((2, SEQ, D), F32),
        V((2, SEQ, D), F32),
        V((2, SEQ, D), BF16),
        V((2, SEQ, D), BF16),
        V((2, 2, SEQ, WIDE), BF16),
        V((2, 2, SEQ, COL), BF16),
        V((2, 2, SEQ, COL), BF16),
        V((2, 2, 2, SEQ, WIDE), BF16),
        V((2, 2, 2, SEQ, WIDE), BF16),
        V((SEQ, D), F32),
        V((SEQ, D), F32),
        V((SEQ, D), BF16),
        V((2, SEQ, D), BF16),
        V((SEQ, D), BF16),
        V((D, SEQ), BF16),
        V((D, SEQ), BF16),
        V((2, 2, SEQ, WIDE), BF16),
        V((2, SEQ, COL), BF16),
        V((2, SEQ, WIDE), BF16),
        V((2, SEQ, COL), BF16),
        V((SEQ, 1), F32),
        V((8, D), F32),
        V((NZ, NX, 8, 128), F32),
        V((8, D), F32),
        V((4, 2, 8, D), F32),
        V((8, 128), F32),
        V((NZ, 2, 8, 128), F32),
        V((4, 8, 128), F32),
        V((PAIRS + PAIRS // 2, NZ, NX, PART, WIDE), BF16),
        V((PAIRS + PAIRS // 2, 2, NZ, PART, WIDE), BF16),
        V((PAIRS, NZ, PART, WIDE), BF16),
        V((PAIRS, NZ - 1, PART, WIDE), BF16),
        V((PAIRS, 2, PART, WIDE), BF16),
        V((PAIRS, 2, NZ - 1, 2, PART, WIDE), BF16),
        V((PAIRS, PART, WIDE), BF16),
        V((PAIRS, 2, 2, PART, WIDE), BF16),
        dma((WSLOTS,)),
        dma((PAIRS, PARTS, 6)), dma((PAIRS, PARTS, 6)),
        dma((2,)), dma((2, 2)),
        dma((2,)), dma((2,)), dma((4,)),
        dma((4,)), dma((4,)),
        dma((6,)), dma((6,)),
        dma((10,)), dma((10,)),
    ]
    return pl.pallas_call(
        step_kernel,
        out_shape=(
            jax.ShapeDtypeStruct((TM, D), F32),
            jax.ShapeDtypeStruct((TM, D), F32),
            jax.ShapeDtypeStruct((PAIRS, PARTS, PART, WIDE), F32),
            jax.ShapeDtypeStruct((8, D), F32),
            jax.ShapeDtypeStruct((8, 128), F32),
        ),
        in_specs=[hb, hb, hb, vm, sm, vm],
        out_specs=(hb, hb, vm, vm, vm),
        scratch_shapes=scratch,
        compiler_params=pltpu.CompilerParams(
            collective_id=0, has_side_effects=True, vmem_limit_bytes=62 << 20
        ),
        name="train_step",
    )(weights, patches, cotangent, mask_index, mask_count, small)


def adam_values(weight_in, moment_one, moment_two, gradient, step_rate, decay_rate):
    moment_one = BETA_ONE * moment_one + (1.0 - BETA_ONE) * gradient
    moment_two = BETA_TWO * moment_two + (1.0 - BETA_TWO) * gradient * gradient
    first_hat = moment_one / (1.0 - BETA_ONE**STEP)
    second_hat = moment_two / (1.0 - BETA_TWO**STEP)
    updated = weight_in - step_rate * (
        first_hat / (jnp.sqrt(second_hat) + EPS_ADAM) + decay_rate * weight_in
    )
    return (updated, moment_one, moment_two)


def adam_kernel(
    norm, grad, small_total, small, small_one, small_two, block, igrad, w, m, v,
    nw, nm, nv, ns, nsm, nsv, grad_norm, block_out, igrad_out,
):
    factor = jnp.minimum(1.0, CLIP_MAX / norm[0:1, 0:1])
    for i in range(PAIRS // ADAM_STEPS):
        g = grad[i].reshape(ROWS, WIDE) * factor
        for j in range(2):
            k = 2 * i + j
            nw[k], nm[k], nv[k] = adam_values(
                w[k], m[k], v[k], g[:, j * COL : (j + 1) * COL], D ** (-0.5), DECAY_RATE
            )
    block_out[...] = block[...]
    igrad_out[...] = igrad[...]

    @pl.when(pl.program_id(0) == 0)
    def _():
        first = ROWS * lax.axis_index("wide")
        row = lax.broadcasted_iota(jnp.int32, (D, ROWS), 0)
        column = lax.broadcasted_iota(jnp.int32, (D, ROWS), 1)
        pick = jnp.where(row == column + first, 1.0, 0.0)
        own = lax.dot_general(
            small_total[...], pick, (((1,), (0,)), ((), ())),
            precision=lax.Precision.HIGHEST, preferred_element_type=F32,
        )[0:5]
        ns[...], nsm[...], nsv[...] = adam_values(
            small[...], small_one[...], small_two[...], own * factor, RATE_SMALL, 0.0
        )
        grad_norm[...] = norm[0:1, 0:1]


def adam_all(norm, grad, small_total, smalls, rows, matrices):
    shape = matrices[0].shape
    flat = (LAYERS * 12, ROWS, COL)
    blk = pl.BlockSpec((2 * PAIRS // ADAM_STEPS, ROWS, COL), lambda i: (i, 0, 0))
    row_blk = pl.BlockSpec((TM // ADAM_STEPS, D), lambda i: (i, 0))

    def whole(*dims):
        return pl.BlockSpec(dims, lambda i: (0,) * len(dims))

    outs = pl.pallas_call(
        adam_kernel,
        grid=(ADAM_STEPS,),
        out_shape=(
            *(jax.ShapeDtypeStruct(flat, F32) for _ in range(3)),
            *(jax.ShapeDtypeStruct((5, ROWS), F32) for _ in range(3)),
            jax.ShapeDtypeStruct((1, 1), F32),
            *(jax.ShapeDtypeStruct((TM, D), F32) for _ in range(2)),
        ),
        in_specs=[
            whole(8, 128),
            pl.BlockSpec((PAIRS // ADAM_STEPS, PARTS, PART, WIDE), lambda i: (i, 0, 0, 0)),
            whole(8, D),
            *(whole(5, ROWS) for _ in range(3)),
            row_blk, row_blk,
            blk, blk, blk,
        ],
        out_specs=(
            blk, blk, blk, *(whole(5, ROWS) for _ in range(3)), whole(1, 1), row_blk, row_blk,
        ),
        compiler_params=pltpu.CompilerParams(vmem_limit_bytes=62 << 20),
        name="adam",
    )(norm, grad, small_total, *smalls, *rows, *(a.reshape(flat) for a in matrices))
    return tuple(o.reshape(shape) for o in outs[:3]), outs[3:6], outs[6].reshape(()), outs[7:]


def shards(patches, cotangent, mask_index, mask_count, weights, first_moment, second_moment,
           small_params, small_first, small_second):
    block_output, input_grad, grad_own, small_total, norm = big_step(
        weights.reshape(LAYERS * 12, ROWS, COL), patches, cotangent, mask_index, mask_count, small_params
    )
    new_matrices, new_smalls, grad_norm, rows = adam_all(
        norm, grad_own, small_total, (small_params, small_first, small_second),
        (block_output, input_grad), (weights, first_moment, second_moment),
    )
    return (*rows, *new_matrices, *new_smalls, grad_norm)


def layer_norm(values, gain):
    centre = values - jnp.mean(values, axis=-1, keepdims=True)
    spread = jnp.mean(centre * centre, axis=-1, keepdims=True)
    return centre * lax.rsqrt(spread + EPS_NORM) * gain


def exact_gelu(values):
    return jax.nn.gelu(values, approximate=False)


def gather_rows(share):
    return lax.all_gather(share, "narrow", axis=0, tiled=True)


def gather_grads(share):
    return lax.all_gather(share, "narrow", axis=0, tiled=True)


def branch_total(term, row_count):
    return lax.psum_scatter(
        term(jnp.int32(0), row_count * lax.axis_size("narrow")).astype(jnp.bfloat16),
        "narrow",
        scatter_dimension=0,
        tiled=True,
    ).astype(jnp.float32)


def input_total(term, row_count):
    return lax.psum_scatter(
        term(jnp.int32(0), row_count * lax.axis_size("narrow")).astype(jnp.bfloat16),
        "narrow",
        scatter_dimension=0,
        tiled=True,
    ).astype(jnp.float32)


def heads_of(values, clip_count):
    return values.reshape(clip_count, SEQ, values.shape[1] // HD, HD)


def attend_clip(parts):
    queries, key_rows, value_rows = parts
    scores = jnp.einsum(
        "qhd,khd->hqk", queries, key_rows, preferred_element_type=jnp.float32
    ) * HD ** (-0.5)
    probs = jax.nn.softmax(scores, axis=-1)
    return jnp.einsum(
        "hqk,khd->qhd", probs.astype(jnp.bfloat16), value_rows, preferred_element_type=jnp.float32
    ).astype(jnp.bfloat16)


def attend_back_clip(parts):
    queries, key_rows, value_rows, grad_mix = parts
    scale = HD ** (-0.5)
    scores = (
        jnp.einsum("qhd,khd->hqk", queries, key_rows, preferred_element_type=jnp.float32) * scale
    )
    probs = jax.nn.softmax(scores, axis=-1)
    grad_values = jnp.einsum(
        "hqk,qhd->khd", probs.astype(jnp.bfloat16), grad_mix, preferred_element_type=jnp.float32
    ).astype(jnp.bfloat16)
    grad_probs = jnp.einsum(
        "qhd,khd->hqk", grad_mix, value_rows, preferred_element_type=jnp.float32
    )
    grad_scores = probs * (grad_probs - jnp.sum(probs * grad_probs, axis=-1, keepdims=True))
    grad_scores = grad_scores.astype(jnp.bfloat16)
    grad_queries = (
        jnp.einsum("hqk,khd->qhd", grad_scores, key_rows, preferred_element_type=jnp.float32)
        * scale
    ).astype(jnp.bfloat16)
    grad_keys = (
        jnp.einsum("hqk,qhd->khd", grad_scores, queries, preferred_element_type=jnp.float32) * scale
    ).astype(jnp.bfloat16)
    return (grad_queries, grad_keys, grad_values)


def forward_layer(stream, weight, gain_one, gain_two):
    row_count = stream.shape[0]
    normed = gather_rows(layer_norm(stream, gain_one).astype(jnp.bfloat16))
    all_rows = normed.shape[0]
    clip_count = all_rows // SEQ
    project = jnp.einsum(
        "rd,sde->sre", normed, weight[0:3], preferred_element_type=jnp.float32
    ).astype(jnp.bfloat16)
    mixture = lax.map(
        attend_clip,
        (
            heads_of(project[0], clip_count),
            heads_of(project[1], clip_count),
            heads_of(project[2], clip_count),
        ),
    )
    mixture = mixture.reshape(all_rows, -1)

    def attn_term(first_row, row_num):
        return lax.dot_general(
            mixture, weight[3], (((1,), (1,)), ((), ())), preferred_element_type=jnp.float32
        )

    resid_one = stream + branch_total(attn_term, row_count)
    normed_two = gather_rows(layer_norm(resid_one, gain_two).astype(jnp.bfloat16))
    upward = jnp.einsum("rd,jde->jre", normed_two, weight[4:8], preferred_element_type=jnp.float32)
    hidden = exact_gelu(upward).astype(jnp.bfloat16)

    def mlp_term(first_row, row_num):
        return jnp.einsum("jre,jde->rd", hidden, weight[8:12], preferred_element_type=jnp.float32)

    result = resid_one + branch_total(mlp_term, row_count)
    return (result, (stream, normed, project, mixture, resid_one, normed_two, upward, hidden))


def backward_layer(grad_out, saved, weight, gain_one, gain_two):
    stream, normed, project, mixture, resid_one, normed_two, upward, hidden = saved
    row_count = stream.shape[0]
    all_rows = normed.shape[0]
    clip_count = all_rows // SEQ
    back_mlp = gather_grads(grad_out.astype(jnp.bfloat16))
    grad_down = jnp.einsum("rd,jre->jde", back_mlp, hidden, preferred_element_type=jnp.float32)
    grad_hidden = jnp.einsum(
        "rd,jde->jre", back_mlp, weight[8:12], preferred_element_type=jnp.float32
    )
    gelu_out, gelu_back = jax.vjp(exact_gelu, upward)
    grad_upward = gelu_back(grad_hidden)[0].astype(jnp.bfloat16)
    grad_up = jnp.einsum("rd,jre->jde", normed_two, grad_upward, preferred_element_type=jnp.float32)

    def up_term(first_row, row_num):
        return jnp.einsum(
            "jre,jde->rd", grad_upward, weight[4:8], preferred_element_type=jnp.float32
        )

    grad_normed_two = input_total(up_term, row_count)
    norm_out, norm_back = jax.vjp(layer_norm, resid_one, gain_two)
    part_stream, grad_gain_two = norm_back(grad_normed_two)
    grad_resid = grad_out + part_stream
    back_attn = gather_grads(grad_resid.astype(jnp.bfloat16))
    grad_out_proj = lax.dot_general(
        back_attn, mixture, (((0,), (0,)), ((), ())), preferred_element_type=jnp.float32
    )
    grad_mixture = jnp.dot(back_attn, weight[3], preferred_element_type=jnp.float32).astype(
        jnp.bfloat16
    )
    grad_heads = lax.map(
        attend_back_clip,
        (
            heads_of(project[0], clip_count),
            heads_of(project[1], clip_count),
            heads_of(project[2], clip_count),
            heads_of(grad_mixture, clip_count),
        ),
    )
    grad_project = jnp.stack([piece.reshape(all_rows, -1) for piece in grad_heads])
    grad_qkv = jnp.einsum("rd,sre->sde", normed, grad_project, preferred_element_type=jnp.float32)

    def qkv_term(first_row, row_num):
        return jnp.einsum(
            "sre,sde->rd", grad_project, weight[0:3], preferred_element_type=jnp.float32
        )

    grad_normed = input_total(qkv_term, row_count)
    norm_out_one, norm_back_one = jax.vjp(layer_norm, stream, gain_one)
    part_in, grad_gain_one = norm_back_one(grad_normed)
    grad_matrix = jnp.concatenate([grad_qkv, grad_out_proj[None], grad_up, grad_down], axis=0)
    return (grad_resid + part_in, grad_matrix, grad_gain_one, grad_gain_two)


def masked_rows(mask_index, mask_count, row_count):
    positions = lax.iota(jnp.int32, SEQ)
    slots = lax.iota(jnp.int32, mask_index.shape[1])
    live = slots[None, :] < mask_count[:, None]
    hits = (mask_index[:, :, None] == positions[None, None, :]) & live[:, :, None]
    flag_all = jnp.any(hits, axis=1).astype(jnp.float32).reshape(-1)
    return lax.dynamic_slice_in_dim(flag_all, lax.axis_index("narrow") * row_count, row_count, 0)


def shards_general(
    patches,
    cotangent,
    mask_index,
    mask_count,
    weights,
    first_moment,
    second_moment,
    small_params,
    small_first,
    small_second,
):
    row_count = patches.shape[0]
    narrow_size = lax.axis_size("narrow")
    owned_rows = weights.shape[2]
    matrices, small_low = (
        lax.all_gather(weights.astype(jnp.bfloat16), "wide", axis=2, tiled=True),
        lax.all_gather(small_params.astype(jnp.bfloat16), "wide", axis=1, tiled=True),
    )
    gains = small_low.astype(jnp.float32)
    flags = masked_rows(mask_index, mask_count, row_count)[:, None]
    stream = patches.astype(jnp.float32) * (1.0 - flags) + flags * gains[2 * LAYERS][None, :]
    saved_all = []
    for layer_idx in range(LAYERS):
        stream, saved = forward_layer(
            stream, matrices[layer_idx], gains[2 * layer_idx], gains[2 * layer_idx + 1]
        )
        saved_all.append(saved)
    grad_stream = cotangent
    grad_mats = [None] * LAYERS
    grad_gains = [None] * (2 * LAYERS)
    for layer_idx in reversed(range(LAYERS)):
        (
            grad_stream,
            grad_mats[layer_idx],
            grad_gains[2 * layer_idx],
            grad_gains[2 * layer_idx + 1],
        ) = backward_layer(
            grad_stream,
            saved_all[layer_idx],
            matrices[layer_idx],
            gains[2 * layer_idx],
            gains[2 * layer_idx + 1],
        )
    input_grad = grad_stream * (1.0 - flags)
    grad_embed = jnp.sum(grad_stream * flags, axis=0)
    grad_small = jnp.stack(grad_gains + [grad_embed])
    grad_matrix = jnp.stack(grad_mats)
    first_col = lax.axis_index("wide") * owned_rows
    small_total = lax.psum(grad_small, ("wide", "narrow"))
    small_own = lax.dynamic_slice_in_dim(small_total, first_col, owned_rows, 1)
    matrix_total = lax.psum(grad_matrix, "wide")
    matrix_own = lax.dynamic_slice_in_dim(matrix_total, first_col, owned_rows, 2)
    local_square = jnp.sum(matrix_own * matrix_own) + jnp.sum(small_own * small_own) / narrow_size
    grad_norm = jnp.sqrt(lax.psum(local_square, ("wide", "narrow")))
    factor = jnp.minimum(1.0, CLIP_MAX / grad_norm)
    new_weights, new_first, new_second = adam_values(
        weights, first_moment, second_moment, matrix_own * factor, D ** (-0.5), DECAY_RATE
    )
    new_small, new_small_first, new_small_second = adam_values(
        small_params, small_first, small_second, small_own * factor, RATE_SMALL, 0.0
    )
    return (
        stream,
        input_grad,
        new_weights,
        new_first,
        new_second,
        new_small,
        new_small_first,
        new_small_second,
        grad_norm,
    )


def solution(mesh):
    in_specs = (
        P(("wide", "narrow"), None),
        P(("wide", "narrow"), None),
        P("wide", None),
        P("wide"),
        P(None, None, "wide", "narrow"),
        P(None, None, "wide", "narrow"),
        P(None, None, "wide", "narrow"),
        P(None, "wide"),
        P(None, "wide"),
        P(None, "wide"),
    )
    out_specs = (
        P(("wide", "narrow"), None),
        P(("wide", "narrow"), None),
        P(None, None, "wide", "narrow"),
        P(None, None, "wide", "narrow"),
        P(None, None, "wide", "narrow"),
        P(None, "wide"),
        P(None, "wide"),
        P(None, "wide"),
        P(),
    )
    fits = mesh.shape["wide"] == NZ * NX and mesh.shape["narrow"] == 4
    step = shards if fits else shards_general
    return jax.shard_map(step, mesh=mesh, in_specs=in_specs, out_specs=out_specs, check_vma=False)
```

```python
import functools

import jax
import jax.numpy as jnp
from jax import lax
from jax.experimental import pallas as pl
from jax.experimental.pallas import tpu as pltpu
from jax.sharding import PartitionSpec as P

D = 768
HD = 64
LAYERS = 2
SEQ = 512
STEP = 10

EPS_NORM = 1e-06
BETA_ONE = 0.9
BETA_TWO = 0.999
EPS_ADAM = 1e-08
DECAY_RATE = 0.05
RATE_SMALL = 0.6
CLIP_MAX = 1.0

MESH = pl.DeviceIdType.MESH
F32 = jnp.float32
BF16 = jnp.bfloat16

PAIRS = 12
ADAM_STEPS = 2
PER = 6
NZ, NX = 4, 2
ROWS = 96
PARTS = 3
PART = ROWS // PARTS
COL = 192
WIDE = 2 * COL
SCALE = HD ** (-0.5)
TM = 256
TR = 64
HEADS_Y = COL // HD

WSLOTS = 4
STEPS = 100
BEGUN = 3
PLAN_WORDS = (
    (
        0, 4401, 17, 8704, 16, 65536, 0, 256, 131331, 4112, 16, 4097,
        0, 0, 0, 65792, 272, 4098, 4112, 65792, 0, 65536, 0, 1,
        4368, 16, 65536, 4352, 16, 65536, 4352, 0, 256, 4096, 0, 69632,
        0, 65536, 0, 0, 65536, 0, 0, 0, 65536, 0, 0, 0,
        0, 0, 0, 0, 0, 0, 0, 0, 0, 0, 0, 0,
        0, 0, 0, 0, 0, 0, 0, 0, 0, 0, 0, 0,
        0, 0, 0, 0, 0, 0, 0, 0, 0, 0, 0, 0,
        0, 0, 0, 0, 0, 0, 0, 0, 0, 0, 0, 0,
        0, 0, 0, 0,
    ),
    (
        0, 3, 52, 4352, 64, 0, 0, 768, 66565, 12368, 96, 16392,
        0, 0, 0, 197888, 1648, 20489, 24704, 263936, 0, 327680, 0, 11,
        30864, 160, 393216, 35072, 176, 458752, 39424, 0, 2816, 40960, 0, 569344,
        0, 589824, 0, 0, 655360, 0, 0, 0, 720896, 0, 0, 0,
        0, 0, 0, 0, 0, 0, 0, 0, 0, 0, 0, 0,
        0, 0, 0, 0, 0, 0, 0, 0, 0, 0, 0, 0,
        0, 0, 0, 0, 0, 0, 0, 0, 0, 0, 0, 0,
        0, 0, 0, 0, 0, 0, 0, 0, 0, 0, 0, 0,
        0, 0, 0, 0,
    ),
    (
        0, 0, 0, 0, 0, 0, 0, 0, 0, 0, 0, 0,
        0, 0, 0, 0, 0, 0, 0, 0, 0, 0, 0, 0,
        0, 0, 0, 0, 0, 0, 0, 0, 0, 0, 0, 0,
        0, 0, 0, 0, 0, 0, 0, 1, 0, 0, 0, 0,
        1, 0, 16, 1, 0, 0, 272, 1, 0, 256, 0, 4096,
        32, 257, 256, 1, 0, 16, 4096, 4097, 272, 1, 0, 256,
        0, 16, 8193, 256, 4112, 1, 4112, 256, 0, 0, 272, 257,
        0, 0, 4096, 16, 0, 4097, 0, 65792, 65536, 16, 65536, 4096,
        65536, 256, 131072, 401408,
    ),
    (
        0, 0, 0, 0, 0, 0, 0, 0, 0, 0, 0, 0,
        0, 0, 0, 0, 0, 0, 0, 0, 0, 0, 0, 0,
        0, 0, 0, 0, 0, 0, 0, 0, 0, 0, 0, 0,
        0, 0, 0, 0, 0, 0, 0, 0, 0, 0, 0, 0,
        1, 0, 0, 2, 0, 0, 16, 3, 0, 256, 0, 0,
        32, 516, 768, 5, 0, 64, 4096, 8198, 1104, 7, 0, 1280,
        0, 96, 12296, 1536, 20592, 9, 24704, 1792, 0, 0, 2192, 2314,
        0, 0, 28672, 160, 0, 32779, 0, 2560, 65536, 176, 131072, 36864,
        196608, 2816, 262144, 434176,
    ),
    (
        0, 0, 1, 0, 0, 2, 0, 3, 0, 4, 0, 5,
        6, 70, 7, 8, 0, 9, 0, 73, 0, 10, 0, 11,
        12, 35, 0, 36, 0, 37, 38, 102, 39, 40, 0, 41,
        0, 105, 45, 0, 42, 46, 110, 0, 43, 47, 111, 44,
        48, 49, 50, 51, 52, 53, 54, 55, 56, 118, 119, 120,
        57, 58, 59, 60, 13, 14, 78, 15, 79, 16, 17, 18,
        19, 20, 21, 22, 23, 24, 86, 87, 88, 25, 26, 27,
        28, 29, 0, 0, 0, 0, 0, 0, 0, 30, 0, 0,
        0, 0, 0, 0,
    ),
)


def mm(a, b):
    return lax.dot_general(a, b, (((1,), (0,)), ((), ())), preferred_element_type=F32)


def mm_nt(a, b):
    return lax.dot_general(a, b, (((1,), (1,)), ((), ())), preferred_element_type=F32)


def mm_tn(a, b):
    return lax.dot_general(a, b, (((0,), (0,)), ((), ())), preferred_element_type=F32)


def loop(count, body):
    def wrapped(i, carry):
        body(i)
        return carry

    lax.fori_loop(0, count, wrapped, 0)


def rows_at(i, size):
    return pl.ds(pl.multiple_of(i * size, size), size)


def step_kernel(
    weights, patch, cot, mask_index, mask_count, small,
    out_block, out_igrad, out_grad, out_small, out_norm,
    G, WF, S, R1, NRM, NRM2, QK, V, MIX, GP, HID, GR, ACC, XS, XR, BK, TA, TB, GU, GM, DQK, DV,
    FL, GAIN, GPIECE, SG, SR, NB, NZC, NXY, RB0Y, RB0X, RB1, RB2, RB2X, RBZ, RBM, RBMZ,
    wf_s, ag_s, ag_r, ex_s, ex_r, in_s, in_r, lc_s, gn_s, gn_r, fs_s, fs_r, nm_s, nm_r,
):
    wide = lax.axis_index("wide")
    narrow = lax.axis_index("narrow")
    z, x = wide // NX, wide % NX
    y, c = narrow // 2, narrow % 2

    dev_core = (wide, 2 * y + 1 - c)
    dev_x = (z * NX + 1 - x, narrow)
    dev_y = (wide, 2 * (1 - y) + c)

    def z_to(k):
        return (z + k) % NZ

    def z_from(k):
        return (z + NZ - k) % NZ

    def dev_z(k):
        return (z_to(k) * NX + x, narrow)

    dev_xy = (z * NX + 1 - x, 2 * (1 - y) + c)

    def dev_zc(k):
        return (z_to(k) * NX + x, 2 * y + 1 - c)

    def load_pair(p):
        return pltpu.make_async_copy(weights.at[pl.ds(2 * p, 2)], WF.at[p % WSLOTS], wf_s.at[p % WSLOTS])

    for p in range(WSLOTS):
        load_pair(p).start()

    greeted = [dev_core, dev_x, dev_y, dev_xy] + [dev(k) for k in range(1, NZ) for dev in (dev_z, dev_zc)]
    barrier = pltpu.get_barrier_semaphore()
    for dev in greeted:
        pl.semaphore_signal(barrier, inc=1, device_id=dev, device_id_type=MESH)

    def remote(src, dst, send, recv, dev):
        return pltpu.make_async_remote_copy(
            src_ref=src, dst_ref=dst, send_sem=send, recv_sem=recv, device_id=dev, device_id_type=MESH
        )

    def lazy(*what):
        return lambda: remote(*what)

    ALL = slice(None)
    own = {"x": x, "y": y, "z": z}
    far = NZ - 1
    inner = jnp.logical_and(z > 0, z < far)
    outer = jnp.logical_or(z == 0, z == far)

    def block(p, h, where):
        return G.at[p, where["y"], where["z"], where["x"], h]

    def gather_order(even, h):
        if h == 0:
            return ("z", "x", "y") if even else ("z", "y", "x")
        return ("x", "z", "y") if h == 1 else ("y", "z", "x")

    def holding(axes):
        return {q: (ALL if q in axes else own[q]) for q in own}

    def along(axis):
        return (3, dev_x, 1 - x) if axis == "x" else (4, dev_y, 1 - y)

    def along_z(action):
        @pl.when(z != far)
        def _():
            action(1)

        action(2)

        @pl.when(z != 0)
        def _():
            action(3)

    def each_part(p, action):
        @pl.when(p % 2 == 0)
        def _():
            action(0, gather_order(True, 0))

        @pl.when(p % 2 == 1)
        def _():
            action(0, gather_order(False, 0))

        for h in range(1, PARTS):
            action(h, gather_order(True, h))

    def gather_plain(p, h, order, axis):
        slot, dev, there = along(axis)
        have = holding(order[: order.index(axis)])
        src = block(p, h, have)
        got = block(p, h, {**have, axis: there})
        send, recv = ag_s.at[p, h, slot], ag_r.at[p, h, slot]
        return lazy(src, src, send, recv, dev), lazy(got, got, send, recv, dev)

    def gather_z(p, h, order, k):
        have = holding(order[: order.index("z")])
        src = block(p, h, have)
        got = block(p, h, {**have, "z": z_from(k)})
        send, recv = ag_s.at[p, h, k - 1], ag_r.at[p, h, k - 1]
        return lazy(src, src, send, recv, dev_z(k)), lazy(got, got, send, recv, dev_z(k))

    def gather_relay(p, h, order):
        have = holding(order[: order.index("z")])
        src = block(p, h, {**have, "z": z_from(2)})
        dev = (far * (z - 1) * NX + x, narrow)
        return lazy(src, src, ag_s.at[p, h, 5], ag_r.at[p, h, 2 * (z - 1)], dev)

    def gather_steps(order):
        at = order.index("z") + 1
        return order[:at] + ("relay",) + order[at:]

    def gather_issue(p, step):
        def action(h, order):
            steps = gather_steps(order)
            before = steps[step - 1] if step > 0 else None
            if before == "z":
                gather_z(p, h, order, 2)[1]().wait_recv()
            elif before == "relay":
                for k in (1, 3):
                    gather_z(p, h, order, k)[1]().wait_recv()
            elif before is not None:
                gather_plain(p, h, order, before)[1]().wait_recv()
            if step == len(steps):
                return
            if steps[step] == "z":
                along_z(lambda k: gather_z(p, h, order, k)[0]().start())
            elif steps[step] == "relay":

                @pl.when(inner)
                def _():
                    gather_relay(p, h, order)().start()

            else:
                gather_plain(p, h, order, steps[step])[0]().start()

        each_part(p, action)

    def gather_sent(p):
        def action(h, order):
            along_z(lambda k: gather_z(p, h, order, k)[0]().wait_send())

            @pl.when(inner)
            def _():
                gather_relay(p, h, order)().wait_send()

            for axis in ("x", "y"):
                gather_plain(p, h, order, axis)[0]().wait_send()

        each_part(p, action)

    def pack(p):
        load_pair(p).wait()
        slot = p % WSLOTS
        both = jnp.concatenate([WF[slot, 0].astype(BF16), WF[slot, 1].astype(BF16)], axis=1)
        G[p, y, z, x] = both.reshape(PARTS, PART, WIDE)

        @pl.when(p + WSLOTS < PAIRS)
        def _():
            load_pair(p + WSLOTS).start()

    half = TM * c
    BKh = BK.at[pl.ds(pl.multiple_of(half, TM), TM)]
    GRh = GR.at[pl.ds(pl.multiple_of(half, TM), TM)]
    other = TM * (1 - c)
    BKo = BK.at[pl.ds(pl.multiple_of(other, TM), TM)]
    GRo = GR.at[pl.ds(pl.multiple_of(other, TM), TM)]
    patch_out = remote(patch, BKh, in_s.at[0], in_r.at[0], dev_core)
    patch_in = remote(patch, BKo, in_s.at[0], in_r.at[0], dev_core)
    cot_out = remote(cot, GRh, in_s.at[1], in_r.at[1], dev_core)
    cot_in = remote(cot, GRo, in_s.at[1], in_r.at[1], dev_core)
    patch_own = pltpu.make_async_copy(patch, BKh, lc_s.at[0])
    cot_own = pltpu.make_async_copy(cot, GRh, lc_s.at[1])
    patch_own.start()
    cot_own.start()
    GPIECE[z, x] = jnp.zeros((8, 128), F32)
    GPIECE[z, x, 0:5, 0:ROWS] = small[...].astype(BF16).astype(F32)
    gain_z = [
        (
            remote(GPIECE.at[z, x], GPIECE.at[z, x], gn_s.at[k - 1], gn_r.at[k - 1], dev_z(k)),
            remote(GPIECE.at[z_from(k), x], GPIECE.at[z_from(k), x], gn_s.at[k - 1], gn_r.at[k - 1], dev_z(k)),
        )
        for k in range(1, NZ)
    ]
    gain_x = (
        remote(GPIECE.at[:, x], GPIECE.at[:, x], gn_s.at[3], gn_r.at[3], dev_x),
        remote(GPIECE.at[:, 1 - x], GPIECE.at[:, 1 - x], gn_s.at[3], gn_r.at[3], dev_x),
    )
    loop(BEGUN, pack)
    pl.semaphore_wait(barrier, len(greeted))
    for s, _ in gain_z:
        s.start()
    patch_out.start()
    loop(BEGUN, lambda p: gather_issue(p, 0))
    cot_out.start()
    loop(PAIRS - BEGUN, lambda i: pack(i + BEGUN))

    index_row = mask_index[pl.ds(y, 1), :]
    count = mask_count[y]
    spot = lax.broadcasted_iota(jnp.int32, (SEQ, index_row.shape[1]), 0)
    live = lax.broadcasted_iota(jnp.int32, (1, index_row.shape[1]), 1) < count
    hits = jnp.where(jnp.logical_and(spot == index_row, live), 1.0, 0.0)
    FL[...] = jnp.max(hits, axis=1, keepdims=True)

    def gains_across(l, yy):
        for _, r in gain_z:
            r.wait_recv()
        gain_x[0].start()

    def first_rows(l, yy):
        gain_x[1].wait_recv()
        lane = lax.broadcasted_iota(jnp.int32, (128, D), 0)
        feature = lax.broadcasted_iota(jnp.int32, (128, D), 1)
        gains = jnp.zeros((8, D), F32)
        for zz in range(NZ):
            for xx in range(NX):
                place = jnp.logical_and(feature - ROWS * (zz * NX + xx) == lane, lane < ROWS)
                gains = gains + mm(GPIECE[zz, xx].astype(BF16), jnp.where(place, 1.0, 0.0).astype(BF16))
        GAIN[...] = gains
        patch_own.wait()
        patch_in.wait_recv()
        embed = GAIN[4:5, :]

        def mask_tile(i):
            rows = rows_at(i, TR)
            flag = FL[rows, :]
            S[0, rows, :] = BK[rows, :].astype(F32) * (1.0 - flag) + flag * embed

        loop(SEQ // TR, mask_tile)

    def norm_parts(values):
        centre = values - jnp.mean(values, axis=-1, keepdims=True)
        spread = jnp.mean(centre * centre, axis=-1, keepdims=True)
        return centre, lax.rsqrt(spread + EPS_NORM)

    def norm_into(dst, src, gain_row):
        gain = GAIN[pl.ds(gain_row, 1), :]

        def tile(i):
            rows = rows_at(i, TR)
            centre, inv = norm_parts(src[rows, :])
            dst[rows, :] = (centre * inv * gain).astype(BF16)

        loop(SEQ // TR, tile)

    def matrix(p, yy):
        return G[p, yy].reshape(D, WIDE)

    def exchange_copy(e, i):
        rows = rows_at(i, TM)
        return remote(XS.at[rows], XR.at[e, rows], ex_s.at[i], ex_r.at[e, i], dev_core)

    def give(e, value):
        XS[...] = value.astype(BF16)
        loop(SEQ // TM, lambda i: exchange_copy(e, i).start())

    def receive(e, take):
        def chunk(i):
            exchange_copy(e, i).wait_recv()

            def tile(j):
                rows = pl.ds(pl.multiple_of(i * TM + j * TR, TR), TR)
                take(rows, XS[rows, :].astype(F32) + XR[e, rows, :].astype(F32))

            loop(TM // TR, tile)

        loop(SEQ // TM, chunk)
        loop(SEQ // TM, lambda i: exchange_copy(e, i).wait_send())

    def attend(l, yy):
        def tile(i):
            rows = rows_at(i, TM)
            outs = []
            for hd in range(HEADS_Y):
                lo = hd * HD
                q = QK[l, yy, rows, lo : lo + HD]
                k = QK[l, yy, :, COL + lo : COL + lo + HD]
                v = V[l, yy, :, lo : lo + HD]
                s = mm_nt(q, k) * SCALE
                e = jnp.exp(s - jnp.max(s, axis=1, keepdims=True))
                probs = e / jnp.sum(e, axis=1, keepdims=True)
                outs.append(mm(probs.astype(BF16), v))
            MIX[l, yy, rows, :] = jnp.concatenate(outs, axis=1).astype(BF16)

        loop(SEQ // TM, tile)

    def attend_back(l, yy, hd):
        lo = hd * HD
        k = QK[l, yy, :, COL + lo : COL + lo + HD]
        v = V[l, yy, :, lo : lo + HD]

        def tile(i, carry):
            dk, dv = carry
            rows = rows_at(i, TM)
            q = QK[l, yy, rows, lo : lo + HD]
            dm = GM[yy, rows, lo : lo + HD]
            s = mm_nt(k, q) * SCALE
            e = jnp.exp(s - jnp.max(s, axis=0, keepdims=True))
            probs = e / jnp.sum(e, axis=0, keepdims=True)
            dp = mm_nt(v, dm)
            ds = probs * (dp - jnp.sum(probs * dp, axis=0, keepdims=True))
            ds = ds.astype(BF16)
            dv = dv + mm(probs.astype(BF16), dm)
            dk = dk + mm(ds, q)
            dq = mm_tn(ds, k) * SCALE
            DQK[yy, rows, lo : lo + HD] = dq.astype(BF16)
            return dk, dv

        zero = jnp.zeros((SEQ, HD), F32)
        dk, dv = lax.fori_loop(0, SEQ // TM, tile, (zero, zero))
        DQK[yy, :, COL + lo : COL + lo + HD] = (dk * SCALE).astype(BF16)
        DV[yy, :, lo : lo + HD] = dv.astype(BF16)

    def up_part(l, u, yy, p):
        ACC[:, 0:WIDE] = mm(NRM2[l], matrix(p, yy))

        def gelu(i):
            rows = rows_at(i, TR)
            v = ACC[rows, 0:WIDE]
            cdf = 0.5 * (1.0 + lax.erf(v * (2.0 ** -0.5)))
            HID[l, u, yy, rows, :] = (v * cdf).astype(BF16)
            pdf = jnp.exp(-0.5 * v * v) * 0.3989422804014327
            GP[l, u, yy, rows, :] = (cdf + v * pdf).astype(BF16)

        loop(SEQ // TR, gelu)

    def ln_one(l, yy):
        norm_into(NRM.at[l], S.at[l], 2 * l)

    def project_qk(l, yy):
        def one(side):
            QK[l, side] = mm(NRM[l], matrix(l * PER, side)).astype(BF16)

        loop(2, one)

    def project_v(l, yy):
        def one(side):
            V[l, side] = mm(NRM[l], matrix(l * PER + 1, side)[:, :COL]).astype(BF16)

        loop(2, one)

    def attn_out(l, yy):
        p = l * PER + 1
        total = mm_nt(MIX[l, 0], matrix(p, 0)[:, COL:])
        give(0, total + mm_nt(MIX[l, 1], matrix(p, 1)[:, COL:]))

    def attn_resid(l, yy):
        def take(rows, total):
            R1[l, rows, :] = S[l, rows, :] + total

        receive(0, take)
        norm_into(NRM2.at[l], R1.at[l], 2 * l + 1)

    def up(l, u):
        loop(2, lambda side: up_part(l, u, side, l * PER + 2 + u))

    def down_one(l, yy):
        p = l * PER + 4
        ACC[...] = mm_nt(HID[l, 0, 0], matrix(p, 0)) + mm_nt(HID[l, 0, 1], matrix(p, 1))

    def down_two(l, yy):
        p = l * PER + 5
        total = ACC[...] + mm_nt(HID[l, 1, 0], matrix(p, 0))
        give(1, total + mm_nt(HID[l, 1, 1], matrix(p, 1)))

    def layer_end(l, yy):
        def take(rows, total):
            value = R1[l, rows, :] + total

            @pl.when(l == 0)
            def _():
                S[1, rows, :] = value

            @pl.when(l == 1)
            def _():
                ACC[rows, :] = value

        receive(1, take)

        @pl.when(l == 1)
        def _():
            block_copy.start()

    block_copy = pltpu.make_async_copy(ACC.at[pl.ds(pl.multiple_of(half, TM), TM)], out_block, lc_s.at[2])

    def scatter_plain(p, h, order, axis):
        slot, dev, there = along(axis)
        place = order.index(axis)
        have = {q: (own[q] if q in order[:place] else ALL) for q in own}
        if place == 0:
            dst = (RB0Y if axis == "y" else RB0X).at[p if h > 0 else PAIRS + p // 2]
        else:
            dst = RB1.at[p] if h == 0 else RB2X.at[p, h - 1]
        send, recv = ag_s.at[p, h, slot], ag_r.at[late(p), h, slot]
        src = block(p, h, {**have, axis: there})
        return lazy(src, dst, send, recv, dev), lazy(dst, dst, send, recv, dev), dst

    def late(p):
        return (p + PER) % PAIRS

    def scatter_have(order):
        return {q: (own[q] if q in order[: order.index("z")] else ALL) for q in own}

    def scatter_z(p, h, order, k):
        dst = RB2.at[p, k - 1] if h == 0 else RBZ.at[p, h - 1, k - 1]
        send, recv = ag_s.at[p, h, k - 1], ag_r.at[late(p), h, k - 1]
        src = block(p, h, {**scatter_have(order), "z": z_to(k)})
        return lazy(src, dst, send, recv, dev_z(k)), lazy(dst, dst, send, recv, dev_z(k)), dst

    def scatter_merge(p, h, order):
        dst = RBM.at[p] if h == 0 else RBMZ.at[p, h - 1]
        dev = ((1 + z // far) * NX + x, narrow)
        send, recv = ag_s.at[p, h, 5], ag_r.at[late(p), h, 5]
        src = block(p, h, {**scatter_have(order), "z": far - z})
        return lazy(src, dst, send, recv, dev), lazy(dst, dst, send, recv, dev), dst

    def scatter_steps(order):
        at = order.index("z")
        return order[:at] + ("merge",) + order[at:]

    def scatter_issue(p, step):
        def action(h, forward_order):
            order = forward_order[::-1]
            steps = scatter_steps(order)
            before = steps[step - 1] if step > 0 else None
            if before is not None and before != "merge":
                have = {q: (own[q] if q in order[: order.index(before) + 1] else ALL) for q in own}
                view = block(p, h, have)
                if before == "z":
                    scatter_z(p, h, order, 2)[1]().wait_recv()

                    @pl.when(z != 0)
                    def _():
                        scatter_z(p, h, order, 1)[1]().wait_recv()

                    @pl.when(z != far)
                    def _():
                        scatter_z(p, h, order, 3)[1]().wait_recv()

                    total = view[...].astype(F32) + scatter_z(p, h, order, 2)[2][...].astype(F32)
                    for k, there in ((1, z != 0), (3, z != far)):
                        total = total + jnp.where(there, scatter_z(p, h, order, k)[2][...].astype(F32), 0.0)
                else:
                    scatter_plain(p, h, order, before)[1]().wait_recv()
                    total = view[...].astype(F32) + scatter_plain(p, h, order, before)[2][...].astype(F32)
                if step < len(steps):
                    view[...] = total.astype(BF16)
                else:
                    out_grad[p, h] = total
                    NB[...] += fold(total * total)
            if step == len(steps):
                return
            if steps[step] == "merge":

                @pl.when(outer)
                def _():
                    scatter_merge(p, h, order)[0]().start()

            elif steps[step] == "z":

                @pl.when(inner)
                def _():
                    scatter_merge(p, h, order)[1]().wait_recv()
                    view = block(p, h, {**scatter_have(order), "z": z_to(2)})
                    term = scatter_merge(p, h, order)[2][...].astype(F32)
                    view[...] = (view[...].astype(F32) + term).astype(BF16)

                along_z(lambda k: scatter_z(p, h, order, k)[0]().start())
            else:
                scatter_plain(p, h, order, steps[step])[0]().start()

        each_part(p, action)

    def fold(sq):
        sq = jnp.sum(sq.reshape(PART // 8, 8, WIDE), axis=0)
        return sq[:, 0:128] + sq[:, 128:256] + sq[:, 256:384]

    def scatter_sent(p):
        def action(h, forward_order):
            order = forward_order[::-1]
            for axis in ("x", "y"):
                scatter_plain(p, h, order, axis)[0]().wait_send()

            @pl.when(outer)
            def _():
                scatter_merge(p, h, order)[0]().wait_send()

            along_z(lambda k: scatter_z(p, h, order, k)[0]().wait_send())

        each_part(p, action)

    NB[...] = jnp.zeros((8, 128), F32)
    SG[...] = jnp.zeros_like(SG)

    def transpose_into(dst, src):
        def tile(i):
            rows = rows_at(i, 128)
            dst[:, rows] = jnp.transpose(src[rows, :])

        loop(SEQ // 128, tile)

    def put_grad(p, yy, left, right):
        G[p, yy] = mm(left[...], right).astype(BF16).reshape(NZ, NX, PARTS, PART, WIDE)

    def norm_back(e, src, gain_row):
        gain = GAIN[pl.ds(gain_row, 1), :]
        def take(rows, dn):
            centre, inv = norm_parts(src[rows, :])
            xhat = centre * inv
            dh = dn * gain
            dv = inv * (
                dh
                - jnp.mean(dh, axis=-1, keepdims=True)
                - xhat * jnp.mean(dh * xhat, axis=-1, keepdims=True)
            )
            GR[rows, :] += dv
            SG[pl.ds(gain_row, 1), :] += jnp.sum(dn * xhat, axis=0, keepdims=True)

        receive(e, take)

    def cast_rows(dst, src):
        def tile(i):
            rows = rows_at(i, TR)
            dst[rows, :] = src[rows, :].astype(BF16)

        loop(SEQ // TR, tile)

    def both(action):
        loop(2, action)

    def back_prepare(l, yy):
        @pl.when(l == 1)
        def _():
            cot_own.wait()
            cot_in.wait_recv()
            cot_out.wait_send()

        cast_rows(BK, GR)
        transpose_into(TA, BK)
        transpose_into(TB, NRM2.at[l])

    def back_down(l, u, side):
        p = l * PER + 4 + u

        @pl.when(side == 0)
        def _():
            gather_sent(p)

        gh = mm(BK[...], matrix(p, side))
        GU[u, side] = (gh * GP[l, u, side].astype(F32)).astype(BF16)
        put_grad(p, side, TA, HID[l, u, side])

    def back_up_sum(l, yy):
        p = l * PER + 2

        @pl.when(l == 1)
        def _():
            block_copy.wait()

        ACC[...] = mm_nt(GU[0, 0], matrix(p, 0)) + mm_nt(GU[0, 1], matrix(p, 1))

    def back_up_give(l, yy):
        p = l * PER + 3
        total = ACC[...] + mm_nt(GU[1, 0], matrix(p, 0))
        give(0, total + mm_nt(GU[1, 1], matrix(p, 1)))

    def back_up(l, u):
        p = l * PER + 2 + u
        gather_sent(p)
        both(lambda side: put_grad(p, side, TB, GU[u, side]))

    def back_norm_two(l, yy):
        norm_back(0, R1.at[l], 2 * l + 1)

    def back_attn_prepare(l, yy):
        cast_rows(BK, GR)
        transpose_into(TA, BK)
        transpose_into(TB, NRM.at[l])

        def grad_mix(side):
            GM[side] = mm(BK[...], matrix(l * PER + 1, side)[:, COL:]).astype(BF16)

        both(grad_mix)

    def back_attn_grads(l, yy):
        p = l * PER + 1
        gather_sent(p)
        ACC[...] = mm_nt(DV[0], matrix(p, 0)[:, :COL]) + mm_nt(DV[1], matrix(p, 1)[:, :COL])

        def grads(side):
            gv = mm(TB[...], DV[side])
            go = mm(TA[...], MIX[l, side])
            pair = jnp.concatenate([gv, go], axis=1).astype(BF16)
            G[p, side] = pair.reshape(NZ, NX, PARTS, PART, WIDE)

        both(grads)

    def back_qk_give(l, yy):
        p = l * PER
        total = ACC[...] + mm_nt(DQK[0], matrix(p, 0))
        give(1, total + mm_nt(DQK[1], matrix(p, 1)))

    def back_qk(l, yy):
        p = l * PER
        gather_sent(p)
        both(lambda side: put_grad(p, side, TB, DQK[side]))

    def back_norm_one(l, yy):
        norm_back(1, S.at[l], 2 * l)

    def position(i):
        s = i % PER
        slot = jnp.where(s < 2, s + 4, jnp.where(s < 4, s, 5 - s))
        return (LAYERS - 1 - i // PER) * PER + slot

    def scatter_at(t, phase):
        scatter_issue(position(t), phase)

    igrad_copy = pltpu.make_async_copy(GRh, out_igrad, lc_s.at[3])
    place = 2 * y + x
    around = ((2 * y + 1 - x, dev_x), (2 * (1 - y) + x, dev_y), (2 * (1 - y) + 1 - x, dev_xy))

    def small_z(k):
        got = SR.at[z_from(k), 0]
        return (
            remote(SR.at[z, 0], SR.at[z, 0], fs_s.at[k - 1], fs_r.at[k - 1], dev_z(k)),
            remote(got, got, fs_s.at[k - 1], fs_r.at[k - 1], dev_z(k)),
        )

    def small_xy(k):
        there, dev = around[k]
        return (
            remote(SR.at[place, 1], SR.at[place, 1], fs_s.at[3 + k], fs_r.at[3 + k], dev),
            remote(SR.at[there, 1], SR.at[there, 1], fs_s.at[3 + k], fs_r.at[3 + k], dev),
        )

    def rows_done():
        def finish_tile(i):
            rows = rows_at(i, TR)
            flag = FL[rows, :]
            value = GR[rows, :]
            SG[4:5, :] += jnp.sum(value * flag, axis=0, keepdims=True)
            GR[rows, :] = value * (1.0 - flag)

        loop(SEQ // TR, finish_tile)
        igrad_copy.start()
        SR[z, 0] = SG[...]
        for k in range(1, NZ):
            small_z(k)[0].start()

    def small_sums():
        for k in range(1, NZ):
            small_z(k)[1].wait_recv()
        SR[place, 1] = SR[0, 0] + SR[1, 0] + SR[2, 0] + SR[3, 0]
        for k in range(3):
            small_xy(k)[0].start()

    pieces = {
        "g1": gains_across,
        "g2": first_rows,
        "ln1": ln_one,
        "qk": project_qk,
        "v": project_v,
        "at": attend,
        "out": attn_out,
        "res": attn_resid,
        "up": up,
        "dn0": down_one,
        "dn1": down_two,
        "fin": layer_end,
        "b4p": back_prepare,
        "b4": lambda l, side: back_down(l, 0, side),
        "b5": lambda l, side: back_down(l, 1, side),
        "b2a": back_up_sum,
        "b2b": lambda l, yy: back_up(l, 0),
        "b3a": back_up_give,
        "b3b": lambda l, yy: back_up(l, 1),
        "b3c": back_norm_two,
        "b1p": back_attn_prepare,
        "ab0": lambda l, side: attend_back(l, side, 0),
        "ab1": lambda l, side: attend_back(l, side, 1),
        "ab2": lambda l, side: attend_back(l, side, 2),
        "b1f": back_attn_grads,
        "b0a": back_qk_give,
        "b0b": back_qk,
        "b0c": back_norm_one,
        "rows": lambda l, yy: rows_done(),
        "small": lambda l, yy: small_sums(),
    }
    def digit(word, k, base):
        return lax.rem(lax.div(word, base**k), base)

    def plan_of(m, low, high):
        if high - low == 1:
            return tuple(jnp.int32(words[low]) for words in PLAN_WORDS)
        middle = (low + high) // 2
        return lax.cond(m < middle, lambda: plan_of(m, low, middle), lambda: plan_of(m, middle, high))

    def micro(m):
        plan = plan_of(m, 0, STEPS)
        for counts, firsts, action in ((plan[0], plan[1], gather_issue), (plan[2], plan[3], scatter_at)):

            @pl.when(counts > 0)
            def _():
                for kind in range(5):
                    count, first = digit(counts, kind, 16), digit(firsts, kind, 16)

                    @pl.when(count > 0)
                    def _():
                        def one(i, carry):
                            action(first + i, kind)
                            return carry

                        lax.fori_loop(0, count, one, 0)

        word = plan[4]

        @pl.when(word > 0)
        def _():
            what, l, yy = lax.rem(word, 32), digit(lax.div(word, 32), 0, 2), lax.div(word, 64)
            for i, action in enumerate(pieces.values()):

                @pl.when(what == i + 1)
                def _():
                    action(l, yy)

    loop(STEPS, micro)

    own_square = jnp.sum(jnp.sum(NB[...], axis=1, keepdims=True), axis=0, keepdims=True)
    NZC[z, c] = jnp.broadcast_to(own_square, (8, 128))
    nm_z = []
    for j, (zz, cc, frm, dev) in enumerate(
        [(z, 1 - c, z, dev_core)]
        + [(z_to(k), c, z_from(k), dev_z(k)) for k in range(1, NZ)]
        + [(z_to(k), 1 - c, z_from(k), dev_zc(k)) for k in range(1, NZ)]
    ):
        got = NZC.at[frm, cc]
        nm_z.append(
            (
                remote(NZC.at[z, c], NZC.at[z, c], nm_s.at[j], nm_r.at[j], dev),
                remote(got, got, nm_s.at[j], nm_r.at[j], dev),
            )
        )
    for s, _ in nm_z:
        s.start()
    for k in range(3):
        small_xy(k)[1].wait_recv()
    total_small = SR[0, 1] + SR[1, 1] + SR[2, 1] + SR[3, 1]
    out_small[...] = total_small
    small_square = jnp.sum(jnp.sum(total_small * total_small, axis=1, keepdims=True), axis=0, keepdims=True)
    for _, r in nm_z:
        r.wait_recv()
    square = NZC[0, 0] + NZC[0, 1]
    for zz in range(1, NZ):
        square = square + (NZC[zz, 0] + NZC[zz, 1])
    NXY[place] = square
    nm_xy = [
        (
            remote(NXY.at[place], NXY.at[place], nm_s.at[7 + k], nm_r.at[7 + k], dev),
            remote(NXY.at[there], NXY.at[there], nm_s.at[7 + k], nm_r.at[7 + k], dev),
        )
        for k, (there, dev) in enumerate(around)
    ]
    for s, _ in nm_xy:
        s.start()
    for _, r in nm_xy:
        r.wait_recv()
    out_norm[...] = jnp.sqrt(NXY[0] + NXY[1] + NXY[2] + NXY[3] + small_square)

    for s, _ in [small_z(k) for k in range(1, NZ)] + [small_xy(k) for k in range(3)] + nm_z + nm_xy + gain_z:
        s.wait_send()
    gain_x[0].wait_send()
    patch_out.wait_send()
    loop(PAIRS, scatter_sent)
    igrad_copy.wait()


def big_step(weights, patches, cotangent, mask_index, mask_count, small):
    vm = pl.BlockSpec(memory_space=pltpu.VMEM)
    hb = pl.BlockSpec(memory_space=pl.ANY)
    sm = pl.BlockSpec(memory_space=pltpu.SMEM)
    dma = pltpu.SemaphoreType.DMA
    V = pltpu.VMEM
    scratch = [
        V((PAIRS, 2, NZ, NX, PARTS, PART, WIDE), BF16),
        V((WSLOTS, 2, ROWS, COL), F32),
        V((2, SEQ, D), F32),
        V((2, SEQ, D), F32),
        V((2, SEQ, D), BF16),
        V((2, SEQ, D), BF16),
        V((2, 2, SEQ, WIDE), BF16),
        V((2, 2, SEQ, COL), BF16),
        V((2, 2, SEQ, COL), BF16),
        V((2, 2, 2, SEQ, WIDE), BF16),
        V((2, 2, 2, SEQ, WIDE), BF16),
        V((SEQ, D), F32),
        V((SEQ, D), F32),
        V((SEQ, D), BF16),
        V((2, SEQ, D), BF16),
        V((SEQ, D), BF16),
        V((D, SEQ), BF16),
        V((D, SEQ), BF16),
        V((2, 2, SEQ, WIDE), BF16),
        V((2, SEQ, COL), BF16),
        V((2, SEQ, WIDE), BF16),
        V((2, SEQ, COL), BF16),
        V((SEQ, 1), F32),
        V((8, D), F32),
        V((NZ, NX, 8, 128), F32),
        V((8, D), F32),
        V((4, 2, 8, D), F32),
        V((8, 128), F32),
        V((NZ, 2, 8, 128), F32),
        V((4, 8, 128), F32),
        V((PAIRS + PAIRS // 2, NZ, NX, PART, WIDE), BF16),
        V((PAIRS + PAIRS // 2, 2, NZ, PART, WIDE), BF16),
        V((PAIRS, NZ, PART, WIDE), BF16),
        V((PAIRS, NZ - 1, PART, WIDE), BF16),
        V((PAIRS, 2, PART, WIDE), BF16),
        V((PAIRS, 2, NZ - 1, 2, PART, WIDE), BF16),
        V((PAIRS, PART, WIDE), BF16),
        V((PAIRS, 2, 2, PART, WIDE), BF16),
        dma((WSLOTS,)),
        dma((PAIRS, PARTS, 6)), dma((PAIRS, PARTS, 6)),
        dma((2,)), dma((2, 2)),
        dma((2,)), dma((2,)), dma((4,)),
        dma((4,)), dma((4,)),
        dma((6,)), dma((6,)),
        dma((10,)), dma((10,)),
    ]
    return pl.pallas_call(
        step_kernel,
        out_shape=(
            jax.ShapeDtypeStruct((TM, D), F32),
            jax.ShapeDtypeStruct((TM, D), F32),
            jax.ShapeDtypeStruct((PAIRS, PARTS, PART, WIDE), F32),
            jax.ShapeDtypeStruct((8, D), F32),
            jax.ShapeDtypeStruct((8, 128), F32),
        ),
        in_specs=[hb, hb, hb, vm, sm, vm],
        out_specs=(hb, hb, vm, vm, vm),
        scratch_shapes=scratch,
        compiler_params=pltpu.CompilerParams(
            collective_id=0, has_side_effects=True, vmem_limit_bytes=62 << 20
        ),
        name="train_step",
    )(weights, patches, cotangent, mask_index, mask_count, small)


def adam_values(weight_in, moment_one, moment_two, gradient, step_rate, decay_rate):
    moment_one = BETA_ONE * moment_one + (1.0 - BETA_ONE) * gradient
    moment_two = BETA_TWO * moment_two + (1.0 - BETA_TWO) * gradient * gradient
    first_hat = moment_one / (1.0 - BETA_ONE**STEP)
    second_hat = moment_two / (1.0 - BETA_TWO**STEP)
    updated = weight_in - step_rate * (
        first_hat / (jnp.sqrt(second_hat) + EPS_ADAM) + decay_rate * weight_in
    )
    return (updated, moment_one, moment_two)


def adam_kernel(
    norm, grad, small_total, small, small_one, small_two, block, igrad, w, m, v,
    nw, nm, nv, ns, nsm, nsv, grad_norm, block_out, igrad_out,
):
    factor = jnp.minimum(1.0, CLIP_MAX / norm[0:1, 0:1])
    for i in range(PAIRS // ADAM_STEPS):
        g = grad[i].reshape(ROWS, WIDE) * factor
        for j in range(2):
            k = 2 * i + j
            nw[k], nm[k], nv[k] = adam_values(
                w[k], m[k], v[k], g[:, j * COL : (j + 1) * COL], D ** (-0.5), DECAY_RATE
            )
    block_out[...] = block[...]
    igrad_out[...] = igrad[...]

    @pl.when(pl.program_id(0) == 0)
    def _():
        first = ROWS * lax.axis_index("wide")
        row = lax.broadcasted_iota(jnp.int32, (D, ROWS), 0)
        column = lax.broadcasted_iota(jnp.int32, (D, ROWS), 1)
        pick = jnp.where(row == column + first, 1.0, 0.0)
        own = lax.dot_general(
            small_total[...], pick, (((1,), (0,)), ((), ())),
            precision=lax.Precision.HIGHEST, preferred_element_type=F32,
        )[0:5]
        ns[...], nsm[...], nsv[...] = adam_values(
            small[...], small_one[...], small_two[...], own * factor, RATE_SMALL, 0.0
        )
        grad_norm[...] = norm[0:1, 0:1]


def adam_all(norm, grad, small_total, smalls, rows, matrices):
    shape = matrices[0].shape
    flat = (LAYERS * 12, ROWS, COL)
    blk = pl.BlockSpec((2 * PAIRS // ADAM_STEPS, ROWS, COL), lambda i: (i, 0, 0))
    row_blk = pl.BlockSpec((TM // ADAM_STEPS, D), lambda i: (i, 0))

    def whole(*dims):
        return pl.BlockSpec(dims, lambda i: (0,) * len(dims))

    outs = pl.pallas_call(
        adam_kernel,
        grid=(ADAM_STEPS,),
        out_shape=(
            *(jax.ShapeDtypeStruct(flat, F32) for _ in range(3)),
            *(jax.ShapeDtypeStruct((5, ROWS), F32) for _ in range(3)),
            jax.ShapeDtypeStruct((1, 1), F32),
            *(jax.ShapeDtypeStruct((TM, D), F32) for _ in range(2)),
        ),
        in_specs=[
            whole(8, 128),
            pl.BlockSpec((PAIRS // ADAM_STEPS, PARTS, PART, WIDE), lambda i: (i, 0, 0, 0)),
            whole(8, D),
            *(whole(5, ROWS) for _ in range(3)),
            row_blk, row_blk,
            blk, blk, blk,
        ],
        out_specs=(
            blk, blk, blk, *(whole(5, ROWS) for _ in range(3)), whole(1, 1), row_blk, row_blk,
        ),
        compiler_params=pltpu.CompilerParams(vmem_limit_bytes=62 << 20),
        name="adam",
    )(norm, grad, small_total, *smalls, *rows, *(a.reshape(flat) for a in matrices))
    return tuple(o.reshape(shape) for o in outs[:3]), outs[3:6], outs[6].reshape(()), outs[7:]


def shards(patches, cotangent, mask_index, mask_count, weights, first_moment, second_moment,
           small_params, small_first, small_second):
    block_output, input_grad, grad_own, small_total, norm = big_step(
        weights.reshape(LAYERS * 12, ROWS, COL), patches, cotangent, mask_index, mask_count, small_params
    )
    new_matrices, new_smalls, grad_norm, rows = adam_all(
        norm, grad_own, small_total, (small_params, small_first, small_second),
        (block_output, input_grad), (weights, first_moment, second_moment),
    )
    return (*rows, *new_matrices, *new_smalls, grad_norm)


def layer_norm(values, gain):
    centre = values - jnp.mean(values, axis=-1, keepdims=True)
    spread = jnp.mean(centre * centre, axis=-1, keepdims=True)
    return centre * lax.rsqrt(spread + EPS_NORM) * gain


def exact_gelu(values):
    return jax.nn.gelu(values, approximate=False)


def gather_rows(share):
    return lax.all_gather(share, "narrow", axis=0, tiled=True)


def gather_grads(share):
    return lax.all_gather(share, "narrow", axis=0, tiled=True)


def branch_total(term, row_count):
    return lax.psum_scatter(
        term(jnp.int32(0), row_count * lax.axis_size("narrow")).astype(jnp.bfloat16),
        "narrow",
        scatter_dimension=0,
        tiled=True,
    ).astype(jnp.float32)


def input_total(term, row_count):
    return lax.psum_scatter(
        term(jnp.int32(0), row_count * lax.axis_size("narrow")).astype(jnp.bfloat16),
        "narrow",
        scatter_dimension=0,
        tiled=True,
    ).astype(jnp.float32)


def heads_of(values, clip_count):
    return values.reshape(clip_count, SEQ, values.shape[1] // HD, HD)


def attend_clip(parts):
    queries, key_rows, value_rows = parts
    scores = jnp.einsum(
        "qhd,khd->hqk", queries, key_rows, preferred_element_type=jnp.float32
    ) * HD ** (-0.5)
    probs = jax.nn.softmax(scores, axis=-1)
    return jnp.einsum(
        "hqk,khd->qhd", probs.astype(jnp.bfloat16), value_rows, preferred_element_type=jnp.float32
    ).astype(jnp.bfloat16)


def attend_back_clip(parts):
    queries, key_rows, value_rows, grad_mix = parts
    scale = HD ** (-0.5)
    scores = (
        jnp.einsum("qhd,khd->hqk", queries, key_rows, preferred_element_type=jnp.float32) * scale
    )
    probs = jax.nn.softmax(scores, axis=-1)
    grad_values = jnp.einsum(
        "hqk,qhd->khd", probs.astype(jnp.bfloat16), grad_mix, preferred_element_type=jnp.float32
    ).astype(jnp.bfloat16)
    grad_probs = jnp.einsum(
        "qhd,khd->hqk", grad_mix, value_rows, preferred_element_type=jnp.float32
    )
    grad_scores = probs * (grad_probs - jnp.sum(probs * grad_probs, axis=-1, keepdims=True))
    grad_scores = grad_scores.astype(jnp.bfloat16)
    grad_queries = (
        jnp.einsum("hqk,khd->qhd", grad_scores, key_rows, preferred_element_type=jnp.float32)
        * scale
    ).astype(jnp.bfloat16)
    grad_keys = (
        jnp.einsum("hqk,qhd->khd", grad_scores, queries, preferred_element_type=jnp.float32) * scale
    ).astype(jnp.bfloat16)
    return (grad_queries, grad_keys, grad_values)


def forward_layer(stream, weight, gain_one, gain_two):
    row_count = stream.shape[0]
    normed = gather_rows(layer_norm(stream, gain_one).astype(jnp.bfloat16))
    all_rows = normed.shape[0]
    clip_count = all_rows // SEQ
    project = jnp.einsum(
        "rd,sde->sre", normed, weight[0:3], preferred_element_type=jnp.float32
    ).astype(jnp.bfloat16)
    mixture = lax.map(
        attend_clip,
        (
            heads_of(project[0], clip_count),
            heads_of(project[1], clip_count),
            heads_of(project[2], clip_count),
        ),
    )
    mixture = mixture.reshape(all_rows, -1)

    def attn_term(first_row, row_num):
        return lax.dot_general(
            mixture, weight[3], (((1,), (1,)), ((), ())), preferred_element_type=jnp.float32
        )

    resid_one = stream + branch_total(attn_term, row_count)
    normed_two = gather_rows(layer_norm(resid_one, gain_two).astype(jnp.bfloat16))
    upward = jnp.einsum("rd,jde->jre", normed_two, weight[4:8], preferred_element_type=jnp.float32)
    hidden = exact_gelu(upward).astype(jnp.bfloat16)

    def mlp_term(first_row, row_num):
        return jnp.einsum("jre,jde->rd", hidden, weight[8:12], preferred_element_type=jnp.float32)

    result = resid_one + branch_total(mlp_term, row_count)
    return (result, (stream, normed, project, mixture, resid_one, normed_two, upward, hidden))


def backward_layer(grad_out, saved, weight, gain_one, gain_two):
    stream, normed, project, mixture, resid_one, normed_two, upward, hidden = saved
    row_count = stream.shape[0]
    all_rows = normed.shape[0]
    clip_count = all_rows // SEQ
    back_mlp = gather_grads(grad_out.astype(jnp.bfloat16))
    grad_down = jnp.einsum("rd,jre->jde", back_mlp, hidden, preferred_element_type=jnp.float32)
    grad_hidden = jnp.einsum(
        "rd,jde->jre", back_mlp, weight[8:12], preferred_element_type=jnp.float32
    )
    gelu_out, gelu_back = jax.vjp(exact_gelu, upward)
    grad_upward = gelu_back(grad_hidden)[0].astype(jnp.bfloat16)
    grad_up = jnp.einsum("rd,jre->jde", normed_two, grad_upward, preferred_element_type=jnp.float32)

    def up_term(first_row, row_num):
        return jnp.einsum(
            "jre,jde->rd", grad_upward, weight[4:8], preferred_element_type=jnp.float32
        )

    grad_normed_two = input_total(up_term, row_count)
    norm_out, norm_back = jax.vjp(layer_norm, resid_one, gain_two)
    part_stream, grad_gain_two = norm_back(grad_normed_two)
    grad_resid = grad_out + part_stream
    back_attn = gather_grads(grad_resid.astype(jnp.bfloat16))
    grad_out_proj = lax.dot_general(
        back_attn, mixture, (((0,), (0,)), ((), ())), preferred_element_type=jnp.float32
    )
    grad_mixture = jnp.dot(back_attn, weight[3], preferred_element_type=jnp.float32).astype(
        jnp.bfloat16
    )
    grad_heads = lax.map(
        attend_back_clip,
        (
            heads_of(project[0], clip_count),
            heads_of(project[1], clip_count),
            heads_of(project[2], clip_count),
            heads_of(grad_mixture, clip_count),
        ),
    )
    grad_project = jnp.stack([piece.reshape(all_rows, -1) for piece in grad_heads])
    grad_qkv = jnp.einsum("rd,sre->sde", normed, grad_project, preferred_element_type=jnp.float32)

    def qkv_term(first_row, row_num):
        return jnp.einsum(
            "sre,sde->rd", grad_project, weight[0:3], preferred_element_type=jnp.float32
        )

    grad_normed = input_total(qkv_term, row_count)
    norm_out_one, norm_back_one = jax.vjp(layer_norm, stream, gain_one)
    part_in, grad_gain_one = norm_back_one(grad_normed)
    grad_matrix = jnp.concatenate([grad_qkv, grad_out_proj[None], grad_up, grad_down], axis=0)
    return (grad_resid + part_in, grad_matrix, grad_gain_one, grad_gain_two)


def masked_rows(mask_index, mask_count, row_count):
    positions = lax.iota(jnp.int32, SEQ)
    slots = lax.iota(jnp.int32, mask_index.shape[1])
    live = slots[None, :] < mask_count[:, None]
    hits = (mask_index[:, :, None] == positions[None, None, :]) & live[:, :, None]
    flag_all = jnp.any(hits, axis=1).astype(jnp.float32).reshape(-1)
    return lax.dynamic_slice_in_dim(flag_all, lax.axis_index("narrow") * row_count, row_count, 0)


def shards_general(
    patches,
    cotangent,
    mask_index,
    mask_count,
    weights,
    first_moment,
    second_moment,
    small_params,
    small_first,
    small_second,
):
    row_count = patches.shape[0]
    narrow_size = lax.axis_size("narrow")
    owned_rows = weights.shape[2]
    matrices, small_low = (
        lax.all_gather(weights.astype(jnp.bfloat16), "wide", axis=2, tiled=True),
        lax.all_gather(small_params.astype(jnp.bfloat16), "wide", axis=1, tiled=True),
    )
    gains = small_low.astype(jnp.float32)
    flags = masked_rows(mask_index, mask_count, row_count)[:, None]
    stream = patches.astype(jnp.float32) * (1.0 - flags) + flags * gains[2 * LAYERS][None, :]
    saved_all = []
    for layer_idx in range(LAYERS):
        stream, saved = forward_layer(
            stream, matrices[layer_idx], gains[2 * layer_idx], gains[2 * layer_idx + 1]
        )
        saved_all.append(saved)
    grad_stream = cotangent
    grad_mats = [None] * LAYERS
    grad_gains = [None] * (2 * LAYERS)
    for layer_idx in reversed(range(LAYERS)):
        (
            grad_stream,
            grad_mats[layer_idx],
            grad_gains[2 * layer_idx],
            grad_gains[2 * layer_idx + 1],
        ) = backward_layer(
            grad_stream,
            saved_all[layer_idx],
            matrices[layer_idx],
            gains[2 * layer_idx],
            gains[2 * layer_idx + 1],
        )
    input_grad = grad_stream * (1.0 - flags)
    grad_embed = jnp.sum(grad_stream * flags, axis=0)
    grad_small = jnp.stack(grad_gains + [grad_embed])
    grad_matrix = jnp.stack(grad_mats)
    first_col = lax.axis_index("wide") * owned_rows
    small_total = lax.psum(grad_small, ("wide", "narrow"))
    small_own = lax.dynamic_slice_in_dim(small_total, first_col, owned_rows, 1)
    matrix_total = lax.psum(grad_matrix, "wide")
    matrix_own = lax.dynamic_slice_in_dim(matrix_total, first_col, owned_rows, 2)
    local_square = jnp.sum(matrix_own * matrix_own) + jnp.sum(small_own * small_own) / narrow_size
    grad_norm = jnp.sqrt(lax.psum(local_square, ("wide", "narrow")))
    factor = jnp.minimum(1.0, CLIP_MAX / grad_norm)
    new_weights, new_first, new_second = adam_values(
        weights, first_moment, second_moment, matrix_own * factor, D ** (-0.5), DECAY_RATE
    )
    new_small, new_small_first, new_small_second = adam_values(
        small_params, small_first, small_second, small_own * factor, RATE_SMALL, 0.0
    )
    return (
        stream,
        input_grad,
        new_weights,
        new_first,
        new_second,
        new_small,
        new_small_first,
        new_small_second,
        grad_norm,
    )


def solution(mesh):
    in_specs = (
        P(("wide", "narrow"), None),
        P(("wide", "narrow"), None),
        P("wide", None),
        P("wide"),
        P(None, None, "wide", "narrow"),
        P(None, None, "wide", "narrow"),
        P(None, None, "wide", "narrow"),
        P(None, "wide"),
        P(None, "wide"),
        P(None, "wide"),
    )
    out_specs = (
        P(("wide", "narrow"), None),
        P(("wide", "narrow"), None),
        P(None, None, "wide", "narrow"),
        P(None, None, "wide", "narrow"),
        P(None, None, "wide", "narrow"),
        P(None, "wide"),
        P(None, "wide"),
        P(None, "wide"),
        P(),
    )
    fits = mesh.shape["wide"] == NZ * NX and mesh.shape["narrow"] == 4
    step = shards if fits else shards_general
    return jax.shard_map(step, mesh=mesh, in_specs=in_specs, out_specs=out_specs, check_vma=False)
```

```python
import functools

import jax
import jax.numpy as jnp
from jax import lax
from jax.experimental import pallas as pl
from jax.experimental.pallas import tpu as pltpu
from jax.sharding import PartitionSpec as P

D = 768
HD = 64
LAYERS = 2
SEQ = 512
STEP = 10

EPS_NORM = 1e-06
BETA_ONE = 0.9
BETA_TWO = 0.999
EPS_ADAM = 1e-08
DECAY_RATE = 0.05
RATE_SMALL = 0.6
CLIP_MAX = 1.0

MESH = pl.DeviceIdType.MESH
F32 = jnp.float32
BF16 = jnp.bfloat16

PAIRS = 12
ADAM_STEPS = 2
PER = 6
NZ, NX = 4, 2
ROWS = 96
PARTS = 3
EARLY = 2
PART = ROWS // PARTS
COL = 192
WIDE = 2 * COL
SCALE = HD ** (-0.5)
TM = 256
TR = 64
HEADS_Y = COL // HD

WSLOTS = 4
STEPS = 100
BEGUN = 3
PLAN_WORDS = (
    (
        0, 0, 17, 257, 0, 272, 32, 4098, 256, 69648, 4352, 65568,
        0, 4096, 0, 256, 65793, 0, 0, 69633, 256, 69665, 257, 69632,
        257, 4112, 16, 65552, 256, 69632, 0, 4352, 0, 256, 0, 69632,
        0, 69632, 0, 0, 65536, 0, 0, 65536, 0, 0, 0, 0,
        0, 0, 0, 0, 0, 0, 0, 0, 0, 0, 0, 0,
        0, 0, 0, 0, 0, 0, 0, 0, 0, 0, 0, 0,
        0, 0, 0, 0, 0, 0, 0, 0, 0, 0, 0, 0,
        0, 0, 0, 0, 0, 0, 0, 0, 0, 0, 0, 0,
        0, 0, 0, 0,
    ),
    (
        0, 0, 3, 4, 0, 272, 32, 5, 512, 4160, 8960, 65616,
        0, 12288, 0, 1024, 132359, 0, 0, 213000, 1536, 282745, 1802, 352256,
        2059, 28816, 160, 393392, 2304, 491520, 0, 39424, 0, 2816, 0, 565248,
        0, 634880, 0, 0, 655360, 0, 0, 720896, 0, 0, 0, 0,
        0, 0, 0, 0, 0, 0, 0, 0, 0, 0, 0, 0,
        0, 0, 0, 0, 0, 0, 0, 0, 0, 0, 0, 0,
        0, 0, 0, 0, 0, 0, 0, 0, 0, 0, 0, 0,
        0, 0, 0, 0, 0, 0, 0, 0, 0, 0, 0, 0,
        0, 0, 0, 0,
    ),
    (
        0, 0, 0, 0, 0, 0, 0, 0, 0, 0, 0, 0,
        0, 0, 0, 0, 0, 0, 0, 0, 0, 0, 0, 0,
        0, 0, 0, 0, 0, 0, 0, 0, 0, 0, 0, 0,
        0, 0, 0, 0, 0, 0, 0, 1, 0, 0, 0, 1,
        0, 0, 0, 16, 2, 0, 16, 256, 16, 0, 0, 4096,
        272, 1, 512, 1, 0, 0, 16, 1, 272, 1, 0, 256,
        0, 12304, 17, 4097, 4096, 256, 0, 16, 256, 16, 257, 0,
        69889, 0, 0, 0, 0, 0, 16, 16, 0, 12288, 69888, 0,
        0, 0, 0, 659712,
    ),
    (
        0, 0, 0, 0, 0, 0, 0, 0, 0, 0, 0, 0,
        0, 0, 0, 0, 0, 0, 0, 0, 0, 0, 0, 0,
        0, 0, 0, 0, 0, 0, 0, 0, 0, 0, 0, 0,
        0, 0, 0, 0, 0, 0, 0, 0, 0, 0, 0, 1,
        0, 0, 0, 0, 2, 0, 16, 0, 32, 0, 0, 0,
        304, 4, 512, 5, 0, 0, 64, 6, 1104, 7, 0, 1280,
        0, 4192, 120, 16393, 20480, 1536, 0, 128, 1792, 144, 2058, 0,
        26891, 0, 0, 0, 0, 0, 160, 176, 0, 28672, 109056, 0,
        0, 0, 0, 178944,
    ),
    (
        0, 0, 1, 0, 0, 2, 0, 3, 0, 4, 0, 5,
        6, 70, 7, 8, 0, 9, 0, 73, 0, 10, 0, 11,
        12, 35, 0, 36, 0, 37, 38, 102, 39, 40, 0, 41,
        0, 105, 45, 0, 42, 46, 110, 0, 43, 47, 111, 44,
        48, 49, 50, 51, 52, 53, 54, 55, 56, 118, 119, 120,
        57, 58, 59, 60, 13, 14, 78, 15, 79, 16, 17, 18,
        19, 20, 21, 22, 23, 24, 86, 87, 88, 25, 26, 27,
        28, 29, 0, 0, 0, 0, 0, 0, 0, 30, 0, 0,
        0, 0, 0, 0,
    ),
)


def mm(a, b):
    return lax.dot_general(a, b, (((1,), (0,)), ((), ())), preferred_element_type=F32)


def mm_nt(a, b):
    return lax.dot_general(a, b, (((1,), (1,)), ((), ())), preferred_element_type=F32)


def mm_tn(a, b):
    return lax.dot_general(a, b, (((0,), (0,)), ((), ())), preferred_element_type=F32)


def loop(count, body):
    def wrapped(i, carry):
        body(i)
        return carry

    lax.fori_loop(0, count, wrapped, 0)


def rows_at(i, size):
    return pl.ds(pl.multiple_of(i * size, size), size)


def step_kernel(
    weights, patch, cot, mask_index, mask_count, small,
    out_block, out_igrad, out_grad, out_small, out_norm,
    G, WF, S, R1, NRM, NRM2, QK, V, MIX, GP, HID, GR, ACC, XS, XR, BK, TA, TB, GU, GM, DQK, DV,
    FL, GAIN, GPIECE, SG, SR, NB, NZC, NXY, RB0Y, RB0X, RB1, RB2, RB2X, RBZ, RBM, RBMZ,
    wf_s, ag_s, ag_r, ex_s, ex_r, in_s, in_r, lc_s, gn_s, gn_r, fs_s, fs_r, nm_s, nm_r,
):
    wide = lax.axis_index("wide")
    narrow = lax.axis_index("narrow")
    z, x = wide // NX, wide % NX
    y, c = narrow // 2, narrow % 2

    dev_core = (wide, 2 * y + 1 - c)
    dev_x = (z * NX + 1 - x, narrow)
    dev_y = (wide, 2 * (1 - y) + c)

    def z_to(k):
        return (z + k) % NZ

    def z_from(k):
        return (z + NZ - k) % NZ

    def dev_z(k):
        return (z_to(k) * NX + x, narrow)

    dev_xy = (z * NX + 1 - x, 2 * (1 - y) + c)

    def dev_zc(k):
        return (z_to(k) * NX + x, 2 * y + 1 - c)

    def load_pair(p):
        return pltpu.make_async_copy(weights.at[pl.ds(2 * p, 2)], WF.at[p % WSLOTS], wf_s.at[p % WSLOTS])

    for p in range(WSLOTS):
        load_pair(p).start()

    greeted = [dev_core, dev_x, dev_y, dev_xy] + [dev(k) for k in range(1, NZ) for dev in (dev_z, dev_zc)]
    barrier = pltpu.get_barrier_semaphore()
    for dev in greeted:
        pl.semaphore_signal(barrier, inc=1, device_id=dev, device_id_type=MESH)

    def remote(src, dst, send, recv, dev):
        return pltpu.make_async_remote_copy(
            src_ref=src, dst_ref=dst, send_sem=send, recv_sem=recv, device_id=dev, device_id_type=MESH
        )

    def lazy(*what):
        return lambda: remote(*what)

    ALL = slice(None)
    own = {"x": x, "y": y, "z": z}
    far = NZ - 1
    inner = jnp.logical_and(z > 0, z < far)
    outer = jnp.logical_or(z == 0, z == far)

    def block(p, h, where):
        return G.at[p, where["y"], where["z"], where["x"], h]

    def holding(axes):
        return {q: (ALL if q in axes else own[q]) for q in own}

    def along(axis):
        return (3, dev_x, 1 - x) if axis == "x" else (4, dev_y, 1 - y)

    def along_z(action):
        @pl.when(z != far)
        def _():
            action(1)

        action(2)

        @pl.when(z != 0)
        def _():
            action(3)

    def each_part(p, action):
        for test, h, order in (
            (p % 2 == 0, 0, ("z", "x", "y")),
            (p % 2 == 1, 0, ("z", "y", "x")),
            (p < EARLY, 1, ("z", "y", "x")),
            (p >= EARLY, 1, ("x", "z", "y")),
            (p < EARLY, 2, ("z", "x", "y")),
            (p >= EARLY, 2, ("y", "z", "x")),
        ):

            @pl.when(test)
            def _():
                action(h, order)

    def gather_plain(p, h, order, axis):
        slot, dev, there = along(axis)
        have = holding(order[: order.index(axis)])
        src = block(p, h, have)
        got = block(p, h, {**have, axis: there})
        send, recv = ag_s.at[p, h, slot], ag_r.at[p, h, slot]
        return lazy(src, src, send, recv, dev), lazy(got, got, send, recv, dev)

    def gather_z(p, h, order, k):
        have = holding(order[: order.index("z")])
        src = block(p, h, have)
        got = block(p, h, {**have, "z": z_from(k)})
        send, recv = ag_s.at[p, h, k - 1], ag_r.at[p, h, k - 1]
        return lazy(src, src, send, recv, dev_z(k)), lazy(got, got, send, recv, dev_z(k))

    def gather_relay(p, h, order):
        have = holding(order[: order.index("z")])
        src = block(p, h, {**have, "z": z_from(2)})
        dev = (far * (z - 1) * NX + x, narrow)
        return lazy(src, src, ag_s.at[p, h, 5], ag_r.at[p, h, 2 * (z - 1)], dev)

    def gather_steps(order):
        at = order.index("z") + 1
        return order[:at] + ("relay",) + order[at:]

    def gather_issue(p, step):
        def action(h, order):
            steps = gather_steps(order)
            before = steps[step - 1] if step > 0 else None
            if before == "z":
                gather_z(p, h, order, 2)[1]().wait_recv()
            elif before == "relay":
                for k in (1, 3):
                    gather_z(p, h, order, k)[1]().wait_recv()
            elif before is not None:
                gather_plain(p, h, order, before)[1]().wait_recv()
            if step == len(steps):
                return
            if steps[step] == "z":
                along_z(lambda k: gather_z(p, h, order, k)[0]().start())
            elif steps[step] == "relay":

                @pl.when(inner)
                def _():
                    gather_relay(p, h, order)().start()

            else:
                gather_plain(p, h, order, steps[step])[0]().start()

        each_part(p, action)

    def gather_sent(p):
        def action(h, order):
            along_z(lambda k: gather_z(p, h, order, k)[0]().wait_send())

            @pl.when(inner)
            def _():
                gather_relay(p, h, order)().wait_send()

            for axis in ("x", "y"):
                gather_plain(p, h, order, axis)[0]().wait_send()

        each_part(p, action)

    def pack(p):
        load_pair(p).wait()
        slot = p % WSLOTS
        both = jnp.concatenate([WF[slot, 0].astype(BF16), WF[slot, 1].astype(BF16)], axis=1)
        G[p, y, z, x] = both.reshape(PARTS, PART, WIDE)

        @pl.when(p + WSLOTS < PAIRS)
        def _():
            load_pair(p + WSLOTS).start()

    half = TM * c
    BKh = BK.at[pl.ds(pl.multiple_of(half, TM), TM)]
    GRh = GR.at[pl.ds(pl.multiple_of(half, TM), TM)]
    other = TM * (1 - c)
    BKo = BK.at[pl.ds(pl.multiple_of(other, TM), TM)]
    GRo = GR.at[pl.ds(pl.multiple_of(other, TM), TM)]
    patch_out = remote(patch, BKh, in_s.at[0], in_r.at[0], dev_core)
    patch_in = remote(patch, BKo, in_s.at[0], in_r.at[0], dev_core)
    cot_out = remote(cot, GRh, in_s.at[1], in_r.at[1], dev_core)
    cot_in = remote(cot, GRo, in_s.at[1], in_r.at[1], dev_core)
    patch_own = pltpu.make_async_copy(patch, BKh, lc_s.at[0])
    cot_own = pltpu.make_async_copy(cot, GRh, lc_s.at[1])
    patch_own.start()
    cot_own.start()
    GPIECE[z, x] = jnp.zeros((8, 128), F32)
    GPIECE[z, x, 0:5, 0:ROWS] = small[...].astype(BF16).astype(F32)
    gain_z = [
        (
            remote(GPIECE.at[z, x], GPIECE.at[z, x], gn_s.at[k - 1], gn_r.at[k - 1], dev_z(k)),
            remote(GPIECE.at[z_from(k), x], GPIECE.at[z_from(k), x], gn_s.at[k - 1], gn_r.at[k - 1], dev_z(k)),
        )
        for k in range(1, NZ)
    ]
    gain_x = (
        remote(GPIECE.at[:, x], GPIECE.at[:, x], gn_s.at[3], gn_r.at[3], dev_x),
        remote(GPIECE.at[:, 1 - x], GPIECE.at[:, 1 - x], gn_s.at[3], gn_r.at[3], dev_x),
    )
    loop(BEGUN, pack)
    pl.semaphore_wait(barrier, len(greeted))
    for s, _ in gain_z:
        s.start()
    patch_out.start()
    loop(BEGUN, lambda p: gather_issue(p, 0))
    cot_out.start()
    loop(PAIRS - BEGUN, lambda i: pack(i + BEGUN))

    index_row = mask_index[pl.ds(y, 1), :]
    count = mask_count[y]
    spot = lax.broadcasted_iota(jnp.int32, (SEQ, index_row.shape[1]), 0)
    live = lax.broadcasted_iota(jnp.int32, (1, index_row.shape[1]), 1) < count
    hits = jnp.where(jnp.logical_and(spot == index_row, live), 1.0, 0.0)
    FL[...] = jnp.max(hits, axis=1, keepdims=True)

    def gains_across(l, yy):
        for _, r in gain_z:
            r.wait_recv()
        gain_x[0].start()

    def first_rows(l, yy):
        gain_x[1].wait_recv()
        lane = lax.broadcasted_iota(jnp.int32, (128, D), 0)
        feature = lax.broadcasted_iota(jnp.int32, (128, D), 1)
        gains = jnp.zeros((8, D), F32)
        for zz in range(NZ):
            for xx in range(NX):
                place = jnp.logical_and(feature - ROWS * (zz * NX + xx) == lane, lane < ROWS)
                gains = gains + mm(GPIECE[zz, xx].astype(BF16), jnp.where(place, 1.0, 0.0).astype(BF16))
        GAIN[...] = gains
        patch_own.wait()
        patch_in.wait_recv()
        embed = GAIN[4:5, :]

        def mask_tile(i):
            rows = rows_at(i, TR)
            flag = FL[rows, :]
            S[0, rows, :] = BK[rows, :].astype(F32) * (1.0 - flag) + flag * embed

        loop(SEQ // TR, mask_tile)

    def norm_parts(values):
        centre = values - jnp.mean(values, axis=-1, keepdims=True)
        spread = jnp.mean(centre * centre, axis=-1, keepdims=True)
        return centre, lax.rsqrt(spread + EPS_NORM)

    def norm_into(dst, src, gain_row):
        gain = GAIN[pl.ds(gain_row, 1), :]

        def tile(i):
            rows = rows_at(i, TR)
            centre, inv = norm_parts(src[rows, :])
            dst[rows, :] = (centre * inv * gain).astype(BF16)

        loop(SEQ // TR, tile)

    def matrix(p, yy):
        return G[p, yy].reshape(D, WIDE)

    def exchange_copy(e, i):
        rows = rows_at(i, TM)
        return remote(XS.at[rows], XR.at[e, rows], ex_s.at[i], ex_r.at[e, i], dev_core)

    def give(e, value):
        XS[...] = value.astype(BF16)
        loop(SEQ // TM, lambda i: exchange_copy(e, i).start())

    def receive(e, take):
        def chunk(i):
            exchange_copy(e, i).wait_recv()

            def tile(j):
                rows = pl.ds(pl.multiple_of(i * TM + j * TR, TR), TR)
                take(rows, XS[rows, :].astype(F32) + XR[e, rows, :].astype(F32))

            loop(TM // TR, tile)

        loop(SEQ // TM, chunk)
        loop(SEQ // TM, lambda i: exchange_copy(e, i).wait_send())

    def attend(l, yy):
        def tile(i):
            rows = rows_at(i, TM)
            outs = []
            for hd in range(HEADS_Y):
                lo = hd * HD
                q = QK[l, yy, rows, lo : lo + HD]
                k = QK[l, yy, :, COL + lo : COL + lo + HD]
                v = V[l, yy, :, lo : lo + HD]
                s = mm_nt(q, k) * SCALE
                e = jnp.exp(s - jnp.max(s, axis=1, keepdims=True))
                probs = e / jnp.sum(e, axis=1, keepdims=True)
                outs.append(mm(probs.astype(BF16), v))
            MIX[l, yy, rows, :] = jnp.concatenate(outs, axis=1).astype(BF16)

        loop(SEQ // TM, tile)

    def attend_back(l, yy, hd):
        lo = hd * HD
        k = QK[l, yy, :, COL + lo : COL + lo + HD]
        v = V[l, yy, :, lo : lo + HD]

        def tile(i, carry):
            dk, dv = carry
            rows = rows_at(i, TM)
            q = QK[l, yy, rows, lo : lo + HD]
            dm = GM[yy, rows, lo : lo + HD]
            s = mm_nt(k, q) * SCALE
            e = jnp.exp(s - jnp.max(s, axis=0, keepdims=True))
            probs = e / jnp.sum(e, axis=0, keepdims=True)
            dp = mm_nt(v, dm)
            ds = probs * (dp - jnp.sum(probs * dp, axis=0, keepdims=True))
            ds = ds.astype(BF16)
            dv = dv + mm(probs.astype(BF16), dm)
            dk = dk + mm(ds, q)
            dq = mm_tn(ds, k) * SCALE
            DQK[yy, rows, lo : lo + HD] = dq.astype(BF16)
            return dk, dv

        zero = jnp.zeros((SEQ, HD), F32)
        dk, dv = lax.fori_loop(0, SEQ // TM, tile, (zero, zero))
        DQK[yy, :, COL + lo : COL + lo + HD] = (dk * SCALE).astype(BF16)
        DV[yy, :, lo : lo + HD] = dv.astype(BF16)

    def up_part(l, u, yy, p):
        ACC[:, 0:WIDE] = mm(NRM2[l], matrix(p, yy))

        def gelu(i):
            rows = rows_at(i, TR)
            v = ACC[rows, 0:WIDE]
            cdf = 0.5 * (1.0 + lax.erf(v * (2.0 ** -0.5)))
            HID[l, u, yy, rows, :] = (v * cdf).astype(BF16)
            pdf = jnp.exp(-0.5 * v * v) * 0.3989422804014327
            GP[l, u, yy, rows, :] = (cdf + v * pdf).astype(BF16)

        loop(SEQ // TR, gelu)

    def ln_one(l, yy):
        norm_into(NRM.at[l], S.at[l], 2 * l)

    def project_qk(l, yy):
        def one(side):
            QK[l, side] = mm(NRM[l], matrix(l * PER, side)).astype(BF16)

        loop(2, one)

    def project_v(l, yy):
        def one(side):
            V[l, side] = mm(NRM[l], matrix(l * PER + 1, side)[:, :COL]).astype(BF16)

        loop(2, one)

    def attn_out(l, yy):
        p = l * PER + 1
        total = mm_nt(MIX[l, 0], matrix(p, 0)[:, COL:])
        give(0, total + mm_nt(MIX[l, 1], matrix(p, 1)[:, COL:]))

    def attn_resid(l, yy):
        def take(rows, total):
            R1[l, rows, :] = S[l, rows, :] + total

        receive(0, take)
        norm_into(NRM2.at[l], R1.at[l], 2 * l + 1)

    def up(l, u):
        loop(2, lambda side: up_part(l, u, side, l * PER + 2 + u))

    def down_one(l, yy):
        p = l * PER + 4
        ACC[...] = mm_nt(HID[l, 0, 0], matrix(p, 0)) + mm_nt(HID[l, 0, 1], matrix(p, 1))

    def down_two(l, yy):
        p = l * PER + 5
        total = ACC[...] + mm_nt(HID[l, 1, 0], matrix(p, 0))
        give(1, total + mm_nt(HID[l, 1, 1], matrix(p, 1)))

    def layer_end(l, yy):
        def take(rows, total):
            value = R1[l, rows, :] + total

            @pl.when(l == 0)
            def _():
                S[1, rows, :] = value

            @pl.when(l == 1)
            def _():
                ACC[rows, :] = value

        receive(1, take)

        @pl.when(l == 1)
        def _():
            block_copy.start()

    block_copy = pltpu.make_async_copy(ACC.at[pl.ds(pl.multiple_of(half, TM), TM)], out_block, lc_s.at[2])

    def scatter_plain(p, h, order, axis):
        slot, dev, there = along(axis)
        place = order.index(axis)
        have = {q: (own[q] if q in order[:place] else ALL) for q in own}
        if place == 0:
            dst = (RB0Y if axis == "y" else RB0X).at[p if h > 0 else PAIRS + p // 2]
        else:
            dst = RB1.at[first_slot(p, h)] if z_last(order) else RB2X.at[p - EARLY, h - 1]
        send, recv = ag_s.at[p, h, slot], ag_r.at[late(p), h, slot]
        src = block(p, h, {**have, axis: there})
        return lazy(src, dst, send, recv, dev), lazy(dst, dst, send, recv, dev), dst

    def z_last(order):
        return order[2] == "z"

    def first_slot(p, h):
        return p if h == 0 else PAIRS + EARLY * (h - 1) + p

    def late(p):
        return (p + PER) % PAIRS

    def scatter_have(order):
        return {q: (own[q] if q in order[: order.index("z")] else ALL) for q in own}

    def scatter_z(p, h, order, k):
        dst = RB2.at[first_slot(p, h), k - 1] if z_last(order) else RBZ.at[p - EARLY, h - 1, k - 1]
        send, recv = ag_s.at[p, h, k - 1], ag_r.at[late(p), h, k - 1]
        src = block(p, h, {**scatter_have(order), "z": z_to(k)})
        return lazy(src, dst, send, recv, dev_z(k)), lazy(dst, dst, send, recv, dev_z(k)), dst

    def scatter_merge(p, h, order):
        dst = RBM.at[first_slot(p, h)] if z_last(order) else RBMZ.at[p - EARLY, h - 1]
        dev = ((1 + z // far) * NX + x, narrow)
        send, recv = ag_s.at[p, h, 5], ag_r.at[late(p), h, 5]
        src = block(p, h, {**scatter_have(order), "z": far - z})
        return lazy(src, dst, send, recv, dev), lazy(dst, dst, send, recv, dev), dst

    def scatter_steps(order):
        at = order.index("z")
        return order[:at] + ("merge",) + order[at:]

    def scatter_issue(p, step):
        def action(h, forward_order):
            order = forward_order[::-1]
            steps = scatter_steps(order)
            before = steps[step - 1] if step > 0 else None
            if before is not None and before != "merge":
                have = {q: (own[q] if q in order[: order.index(before) + 1] else ALL) for q in own}
                view = block(p, h, have)
                if before == "z":
                    scatter_z(p, h, order, 2)[1]().wait_recv()

                    @pl.when(z != 0)
                    def _():
                        scatter_z(p, h, order, 1)[1]().wait_recv()

                    @pl.when(z != far)
                    def _():
                        scatter_z(p, h, order, 3)[1]().wait_recv()

                    total = view[...].astype(F32) + scatter_z(p, h, order, 2)[2][...].astype(F32)
                    for k, there in ((1, z != 0), (3, z != far)):
                        total = total + jnp.where(there, scatter_z(p, h, order, k)[2][...].astype(F32), 0.0)
                else:
                    scatter_plain(p, h, order, before)[1]().wait_recv()
                    total = view[...].astype(F32) + scatter_plain(p, h, order, before)[2][...].astype(F32)
                if step < len(steps):
                    view[...] = total.astype(BF16)
                else:
                    out_grad[p, h] = total
                    NB[...] += fold(total * total)
            if step == len(steps):
                return
            if steps[step] == "merge":

                @pl.when(outer)
                def _():
                    scatter_merge(p, h, order)[0]().start()

            elif steps[step] == "z":

                @pl.when(inner)
                def _():
                    scatter_merge(p, h, order)[1]().wait_recv()
                    view = block(p, h, {**scatter_have(order), "z": z_to(2)})
                    term = scatter_merge(p, h, order)[2][...].astype(F32)
                    view[...] = (view[...].astype(F32) + term).astype(BF16)

                along_z(lambda k: scatter_z(p, h, order, k)[0]().start())
            else:
                scatter_plain(p, h, order, steps[step])[0]().start()

        each_part(p, action)

    def fold(sq):
        sq = jnp.sum(sq.reshape(PART // 8, 8, WIDE), axis=0)
        return sq[:, 0:128] + sq[:, 128:256] + sq[:, 256:384]

    def scatter_sent(p):
        def action(h, forward_order):
            order = forward_order[::-1]
            for axis in ("x", "y"):
                scatter_plain(p, h, order, axis)[0]().wait_send()

            @pl.when(outer)
            def _():
                scatter_merge(p, h, order)[0]().wait_send()

            along_z(lambda k: scatter_z(p, h, order, k)[0]().wait_send())

        each_part(p, action)

    NB[...] = jnp.zeros((8, 128), F32)
    SG[...] = jnp.zeros_like(SG)

    def transpose_into(dst, src):
        def tile(i):
            rows = rows_at(i, 128)
            dst[:, rows] = jnp.transpose(src[rows, :])

        loop(SEQ // 128, tile)

    def put_grad(p, yy, left, right):
        G[p, yy] = mm(left[...], right).astype(BF16).reshape(NZ, NX, PARTS, PART, WIDE)

    def norm_back(e, src, gain_row):
        gain = GAIN[pl.ds(gain_row, 1), :]
        def take(rows, dn):
            centre, inv = norm_parts(src[rows, :])
            xhat = centre * inv
            dh = dn * gain
            dv = inv * (
                dh
                - jnp.mean(dh, axis=-1, keepdims=True)
                - xhat * jnp.mean(dh * xhat, axis=-1, keepdims=True)
            )
            GR[rows, :] += dv
            SG[pl.ds(gain_row, 1), :] += jnp.sum(dn * xhat, axis=0, keepdims=True)

        receive(e, take)

    def cast_rows(dst, src):
        def tile(i):
            rows = rows_at(i, TR)
            dst[rows, :] = src[rows, :].astype(BF16)

        loop(SEQ // TR, tile)

    def both(action):
        loop(2, action)

    def back_prepare(l, yy):
        @pl.when(l == 1)
        def _():
            cot_own.wait()
            cot_in.wait_recv()
            cot_out.wait_send()

        cast_rows(BK, GR)
        transpose_into(TA, BK)
        transpose_into(TB, NRM2.at[l])

    def back_down(l, u, side):
        p = l * PER + 4 + u

        @pl.when(side == 0)
        def _():
            gather_sent(p)

        gh = mm(BK[...], matrix(p, side))
        GU[u, side] = (gh * GP[l, u, side].astype(F32)).astype(BF16)
        put_grad(p, side, TA, HID[l, u, side])

    def back_up_sum(l, yy):
        p = l * PER + 2

        @pl.when(l == 1)
        def _():
            block_copy.wait()

        ACC[...] = mm_nt(GU[0, 0], matrix(p, 0)) + mm_nt(GU[0, 1], matrix(p, 1))

    def back_up_give(l, yy):
        p = l * PER + 3
        total = ACC[...] + mm_nt(GU[1, 0], matrix(p, 0))
        give(0, total + mm_nt(GU[1, 1], matrix(p, 1)))

    def back_up(l, u):
        p = l * PER + 2 + u
        gather_sent(p)
        both(lambda side: put_grad(p, side, TB, GU[u, side]))

    def back_norm_two(l, yy):
        norm_back(0, R1.at[l], 2 * l + 1)

    def back_attn_prepare(l, yy):
        cast_rows(BK, GR)
        transpose_into(TA, BK)
        transpose_into(TB, NRM.at[l])

        def grad_mix(side):
            GM[side] = mm(BK[...], matrix(l * PER + 1, side)[:, COL:]).astype(BF16)

        both(grad_mix)

    def back_attn_grads(l, yy):
        p = l * PER + 1
        gather_sent(p)
        ACC[...] = mm_nt(DV[0], matrix(p, 0)[:, :COL]) + mm_nt(DV[1], matrix(p, 1)[:, :COL])

        def grads(side):
            gv = mm(TB[...], DV[side])
            go = mm(TA[...], MIX[l, side])
            pair = jnp.concatenate([gv, go], axis=1).astype(BF16)
            G[p, side] = pair.reshape(NZ, NX, PARTS, PART, WIDE)

        both(grads)

    def back_qk_give(l, yy):
        p = l * PER
        total = ACC[...] + mm_nt(DQK[0], matrix(p, 0))
        give(1, total + mm_nt(DQK[1], matrix(p, 1)))

    def back_qk(l, yy):
        p = l * PER
        gather_sent(p)
        both(lambda side: put_grad(p, side, TB, DQK[side]))

    def back_norm_one(l, yy):
        norm_back(1, S.at[l], 2 * l)

    def position(i):
        s = i % PER
        slot = jnp.where(s < 2, s + 4, jnp.where(s < 4, s, 5 - s))
        return (LAYERS - 1 - i // PER) * PER + slot

    def scatter_at(t, phase):
        scatter_issue(position(t), phase)

    igrad_copy = pltpu.make_async_copy(GRh, out_igrad, lc_s.at[3])
    place = 2 * y + x
    around = ((2 * y + 1 - x, dev_x), (2 * (1 - y) + x, dev_y), (2 * (1 - y) + 1 - x, dev_xy))

    def small_z(k):
        got = SR.at[z_from(k), 0]
        return (
            remote(SR.at[z, 0], SR.at[z, 0], fs_s.at[k - 1], fs_r.at[k - 1], dev_z(k)),
            remote(got, got, fs_s.at[k - 1], fs_r.at[k - 1], dev_z(k)),
        )

    def small_xy(k):
        there, dev = around[k]
        return (
            remote(SR.at[place, 1], SR.at[place, 1], fs_s.at[3 + k], fs_r.at[3 + k], dev),
            remote(SR.at[there, 1], SR.at[there, 1], fs_s.at[3 + k], fs_r.at[3 + k], dev),
        )

    def rows_done():
        def finish_tile(i):
            rows = rows_at(i, TR)
            flag = FL[rows, :]
            value = GR[rows, :]
            SG[4:5, :] += jnp.sum(value * flag, axis=0, keepdims=True)
            GR[rows, :] = value * (1.0 - flag)

        loop(SEQ // TR, finish_tile)
        igrad_copy.start()
        SR[z, 0] = SG[...]
        for k in range(1, NZ):
            small_z(k)[0].start()

    def small_sums():
        for k in range(1, NZ):
            small_z(k)[1].wait_recv()
        SR[place, 1] = SR[0, 0] + SR[1, 0] + SR[2, 0] + SR[3, 0]
        for k in range(3):
            small_xy(k)[0].start()

    pieces = {
        "g1": gains_across,
        "g2": first_rows,
        "ln1": ln_one,
        "qk": project_qk,
        "v": project_v,
        "at": attend,
        "out": attn_out,
        "res": attn_resid,
        "up": up,
        "dn0": down_one,
        "dn1": down_two,
        "fin": layer_end,
        "b4p": back_prepare,
        "b4": lambda l, side: back_down(l, 0, side),
        "b5": lambda l, side: back_down(l, 1, side),
        "b2a": back_up_sum,
        "b2b": lambda l, yy: back_up(l, 0),
        "b3a": back_up_give,
        "b3b": lambda l, yy: back_up(l, 1),
        "b3c": back_norm_two,
        "b1p": back_attn_prepare,
        "ab0": lambda l, side: attend_back(l, side, 0),
        "ab1": lambda l, side: attend_back(l, side, 1),
        "ab2": lambda l, side: attend_back(l, side, 2),
        "b1f": back_attn_grads,
        "b0a": back_qk_give,
        "b0b": back_qk,
        "b0c": back_norm_one,
        "rows": lambda l, yy: rows_done(),
        "small": lambda l, yy: small_sums(),
    }
    def digit(word, k, base):
        return lax.rem(lax.div(word, base**k), base)

    def plan_of(m, low, high):
        if high - low == 1:
            return tuple(jnp.int32(words[low]) for words in PLAN_WORDS)
        middle = (low + high) // 2
        return lax.cond(m < middle, lambda: plan_of(m, low, middle), lambda: plan_of(m, middle, high))

    def micro(m):
        plan = plan_of(m, 0, STEPS)
        for counts, firsts, action in ((plan[0], plan[1], gather_issue), (plan[2], plan[3], scatter_at)):

            @pl.when(counts > 0)
            def _():
                for kind in range(5):
                    count, first = digit(counts, kind, 16), digit(firsts, kind, 16)

                    @pl.when(count > 0)
                    def _():
                        def one(i, carry):
                            action(first + i, kind)
                            return carry

                        lax.fori_loop(0, count, one, 0)

        word = plan[4]

        @pl.when(word > 0)
        def _():
            what, l, yy = lax.rem(word, 32), digit(lax.div(word, 32), 0, 2), lax.div(word, 64)
            for i, action in enumerate(pieces.values()):

                @pl.when(what == i + 1)
                def _():
                    action(l, yy)

    loop(STEPS, micro)

    own_square = jnp.sum(jnp.sum(NB[...], axis=1, keepdims=True), axis=0, keepdims=True)
    NZC[z, c] = jnp.broadcast_to(own_square, (8, 128))
    nm_z = []
    for j, (zz, cc, frm, dev) in enumerate(
        [(z, 1 - c, z, dev_core)]
        + [(z_to(k), c, z_from(k), dev_z(k)) for k in range(1, NZ)]
        + [(z_to(k), 1 - c, z_from(k), dev_zc(k)) for k in range(1, NZ)]
    ):
        got = NZC.at[frm, cc]
        nm_z.append(
            (
                remote(NZC.at[z, c], NZC.at[z, c], nm_s.at[j], nm_r.at[j], dev),
                remote(got, got, nm_s.at[j], nm_r.at[j], dev),
            )
        )
    for s, _ in nm_z:
        s.start()
    for k in range(3):
        small_xy(k)[1].wait_recv()
    total_small = SR[0, 1] + SR[1, 1] + SR[2, 1] + SR[3, 1]
    out_small[...] = total_small
    small_square = jnp.sum(jnp.sum(total_small * total_small, axis=1, keepdims=True), axis=0, keepdims=True)
    for _, r in nm_z:
        r.wait_recv()
    square = NZC[0, 0] + NZC[0, 1]
    for zz in range(1, NZ):
        square = square + (NZC[zz, 0] + NZC[zz, 1])
    NXY[place] = square
    nm_xy = [
        (
            remote(NXY.at[place], NXY.at[place], nm_s.at[7 + k], nm_r.at[7 + k], dev),
            remote(NXY.at[there], NXY.at[there], nm_s.at[7 + k], nm_r.at[7 + k], dev),
        )
        for k, (there, dev) in enumerate(around)
    ]
    for s, _ in nm_xy:
        s.start()
    for _, r in nm_xy:
        r.wait_recv()
    out_norm[...] = jnp.sqrt(NXY[0] + NXY[1] + NXY[2] + NXY[3] + small_square)

    for s, _ in [small_z(k) for k in range(1, NZ)] + [small_xy(k) for k in range(3)] + nm_z + nm_xy + gain_z:
        s.wait_send()
    gain_x[0].wait_send()
    patch_out.wait_send()
    loop(PAIRS, scatter_sent)
    igrad_copy.wait()


def big_step(weights, patches, cotangent, mask_index, mask_count, small):
    vm = pl.BlockSpec(memory_space=pltpu.VMEM)
    hb = pl.BlockSpec(memory_space=pl.ANY)
    sm = pl.BlockSpec(memory_space=pltpu.SMEM)
    dma = pltpu.SemaphoreType.DMA
    V = pltpu.VMEM
    scratch = [
        V((PAIRS, 2, NZ, NX, PARTS, PART, WIDE), BF16),
        V((WSLOTS, 2, ROWS, COL), F32),
        V((2, SEQ, D), F32),
        V((2, SEQ, D), F32),
        V((2, SEQ, D), BF16),
        V((2, SEQ, D), BF16),
        V((2, 2, SEQ, WIDE), BF16),
        V((2, 2, SEQ, COL), BF16),
        V((2, 2, SEQ, COL), BF16),
        V((2, 2, 2, SEQ, WIDE), BF16),
        V((2, 2, 2, SEQ, WIDE), BF16),
        V((SEQ, D), F32),
        V((SEQ, D), F32),
        V((SEQ, D), BF16),
        V((2, SEQ, D), BF16),
        V((SEQ, D), BF16),
        V((D, SEQ), BF16),
        V((D, SEQ), BF16),
        V((2, 2, SEQ, WIDE), BF16),
        V((2, SEQ, COL), BF16),
        V((2, SEQ, WIDE), BF16),
        V((2, SEQ, COL), BF16),
        V((SEQ, 1), F32),
        V((8, D), F32),
        V((NZ, NX, 8, 128), F32),
        V((8, D), F32),
        V((4, 2, 8, D), F32),
        V((8, 128), F32),
        V((NZ, 2, 8, 128), F32),
        V((4, 8, 128), F32),
        V((PAIRS + PAIRS // 2, NZ, NX, PART, WIDE), BF16),
        V((PAIRS + PAIRS // 2, 2, NZ, PART, WIDE), BF16),
        V((PAIRS + 2 * EARLY, NZ, PART, WIDE), BF16),
        V((PAIRS + 2 * EARLY, NZ - 1, PART, WIDE), BF16),
        V((PAIRS - EARLY, 2, PART, WIDE), BF16),
        V((PAIRS - EARLY, 2, NZ - 1, 2, PART, WIDE), BF16),
        V((PAIRS + 2 * EARLY, PART, WIDE), BF16),
        V((PAIRS - EARLY, 2, 2, PART, WIDE), BF16),
        dma((WSLOTS,)),
        dma((PAIRS, PARTS, 6)), dma((PAIRS, PARTS, 6)),
        dma((2,)), dma((2, 2)),
        dma((2,)), dma((2,)), dma((4,)),
        dma((4,)), dma((4,)),
        dma((6,)), dma((6,)),
        dma((10,)), dma((10,)),
    ]
    return pl.pallas_call(
        step_kernel,
        out_shape=(
            jax.ShapeDtypeStruct((TM, D), F32),
            jax.ShapeDtypeStruct((TM, D), F32),
            jax.ShapeDtypeStruct((PAIRS, PARTS, PART, WIDE), F32),
            jax.ShapeDtypeStruct((8, D), F32),
            jax.ShapeDtypeStruct((8, 128), F32),
        ),
        in_specs=[hb, hb, hb, vm, sm, vm],
        out_specs=(hb, hb, vm, vm, vm),
        scratch_shapes=scratch,
        compiler_params=pltpu.CompilerParams(
            collective_id=0, has_side_effects=True, vmem_limit_bytes=62 << 20
        ),
        name="train_step",
    )(weights, patches, cotangent, mask_index, mask_count, small)


def adam_values(weight_in, moment_one, moment_two, gradient, step_rate, decay_rate):
    moment_one = BETA_ONE * moment_one + (1.0 - BETA_ONE) * gradient
    moment_two = BETA_TWO * moment_two + (1.0 - BETA_TWO) * gradient * gradient
    first_hat = moment_one / (1.0 - BETA_ONE**STEP)
    second_hat = moment_two / (1.0 - BETA_TWO**STEP)
    updated = weight_in - step_rate * (
        first_hat / (jnp.sqrt(second_hat) + EPS_ADAM) + decay_rate * weight_in
    )
    return (updated, moment_one, moment_two)


def adam_kernel(
    norm, grad, small_total, small, small_one, small_two, block, igrad, w, m, v,
    nw, nm, nv, ns, nsm, nsv, grad_norm, block_out, igrad_out,
):
    factor = jnp.minimum(1.0, CLIP_MAX / norm[0:1, 0:1])
    for i in range(PAIRS // ADAM_STEPS):
        g = grad[i].reshape(ROWS, WIDE) * factor
        for j in range(2):
            k = 2 * i + j
            nw[k], nm[k], nv[k] = adam_values(
                w[k], m[k], v[k], g[:, j * COL : (j + 1) * COL], D ** (-0.5), DECAY_RATE
            )
    block_out[...] = block[...]
    igrad_out[...] = igrad[...]

    @pl.when(pl.program_id(0) == 0)
    def _():
        first = ROWS * lax.axis_index("wide")
        row = lax.broadcasted_iota(jnp.int32, (D, ROWS), 0)
        column = lax.broadcasted_iota(jnp.int32, (D, ROWS), 1)
        pick = jnp.where(row == column + first, 1.0, 0.0)
        own = lax.dot_general(
            small_total[...], pick, (((1,), (0,)), ((), ())),
            precision=lax.Precision.HIGHEST, preferred_element_type=F32,
        )[0:5]
        ns[...], nsm[...], nsv[...] = adam_values(
            small[...], small_one[...], small_two[...], own * factor, RATE_SMALL, 0.0
        )
        grad_norm[...] = norm[0:1, 0:1]


def adam_all(norm, grad, small_total, smalls, rows, matrices):
    shape = matrices[0].shape
    flat = (LAYERS * 12, ROWS, COL)
    blk = pl.BlockSpec((2 * PAIRS // ADAM_STEPS, ROWS, COL), lambda i: (i, 0, 0))
    row_blk = pl.BlockSpec((TM // ADAM_STEPS, D), lambda i: (i, 0))

    def whole(*dims):
        return pl.BlockSpec(dims, lambda i: (0,) * len(dims))

    outs = pl.pallas_call(
        adam_kernel,
        grid=(ADAM_STEPS,),
        out_shape=(
            *(jax.ShapeDtypeStruct(flat, F32) for _ in range(3)),
            *(jax.ShapeDtypeStruct((5, ROWS), F32) for _ in range(3)),
            jax.ShapeDtypeStruct((1, 1), F32),
            *(jax.ShapeDtypeStruct((TM, D), F32) for _ in range(2)),
        ),
        in_specs=[
            whole(8, 128),
            pl.BlockSpec((PAIRS // ADAM_STEPS, PARTS, PART, WIDE), lambda i: (i, 0, 0, 0)),
            whole(8, D),
            *(whole(5, ROWS) for _ in range(3)),
            row_blk, row_blk,
            blk, blk, blk,
        ],
        out_specs=(
            blk, blk, blk, *(whole(5, ROWS) for _ in range(3)), whole(1, 1), row_blk, row_blk,
        ),
        compiler_params=pltpu.CompilerParams(vmem_limit_bytes=62 << 20),
        name="adam",
    )(norm, grad, small_total, *smalls, *rows, *(a.reshape(flat) for a in matrices))
    return tuple(o.reshape(shape) for o in outs[:3]), outs[3:6], outs[6].reshape(()), outs[7:]


def shards(patches, cotangent, mask_index, mask_count, weights, first_moment, second_moment,
           small_params, small_first, small_second):
    block_output, input_grad, grad_own, small_total, norm = big_step(
        weights.reshape(LAYERS * 12, ROWS, COL), patches, cotangent, mask_index, mask_count, small_params
    )
    new_matrices, new_smalls, grad_norm, rows = adam_all(
        norm, grad_own, small_total, (small_params, small_first, small_second),
        (block_output, input_grad), (weights, first_moment, second_moment),
    )
    return (*rows, *new_matrices, *new_smalls, grad_norm)


def layer_norm(values, gain):
    centre = values - jnp.mean(values, axis=-1, keepdims=True)
    spread = jnp.mean(centre * centre, axis=-1, keepdims=True)
    return centre * lax.rsqrt(spread + EPS_NORM) * gain


def exact_gelu(values):
    return jax.nn.gelu(values, approximate=False)


def gather_rows(share):
    return lax.all_gather(share, "narrow", axis=0, tiled=True)


def gather_grads(share):
    return lax.all_gather(share, "narrow", axis=0, tiled=True)


def branch_total(term, row_count):
    return lax.psum_scatter(
        term(jnp.int32(0), row_count * lax.axis_size("narrow")).astype(jnp.bfloat16),
        "narrow",
        scatter_dimension=0,
        tiled=True,
    ).astype(jnp.float32)


def input_total(term, row_count):
    return lax.psum_scatter(
        term(jnp.int32(0), row_count * lax.axis_size("narrow")).astype(jnp.bfloat16),
        "narrow",
        scatter_dimension=0,
        tiled=True,
    ).astype(jnp.float32)


def heads_of(values, clip_count):
    return values.reshape(clip_count, SEQ, values.shape[1] // HD, HD)


def attend_clip(parts):
    queries, key_rows, value_rows = parts
    scores = jnp.einsum(
        "qhd,khd->hqk", queries, key_rows, preferred_element_type=jnp.float32
    ) * HD ** (-0.5)
    probs = jax.nn.softmax(scores, axis=-1)
    return jnp.einsum(
        "hqk,khd->qhd", probs.astype(jnp.bfloat16), value_rows, preferred_element_type=jnp.float32
    ).astype(jnp.bfloat16)


def attend_back_clip(parts):
    queries, key_rows, value_rows, grad_mix = parts
    scale = HD ** (-0.5)
    scores = (
        jnp.einsum("qhd,khd->hqk", queries, key_rows, preferred_element_type=jnp.float32) * scale
    )
    probs = jax.nn.softmax(scores, axis=-1)
    grad_values = jnp.einsum(
        "hqk,qhd->khd", probs.astype(jnp.bfloat16), grad_mix, preferred_element_type=jnp.float32
    ).astype(jnp.bfloat16)
    grad_probs = jnp.einsum(
        "qhd,khd->hqk", grad_mix, value_rows, preferred_element_type=jnp.float32
    )
    grad_scores = probs * (grad_probs - jnp.sum(probs * grad_probs, axis=-1, keepdims=True))
    grad_scores = grad_scores.astype(jnp.bfloat16)
    grad_queries = (
        jnp.einsum("hqk,khd->qhd", grad_scores, key_rows, preferred_element_type=jnp.float32)
        * scale
    ).astype(jnp.bfloat16)
    grad_keys = (
        jnp.einsum("hqk,qhd->khd", grad_scores, queries, preferred_element_type=jnp.float32) * scale
    ).astype(jnp.bfloat16)
    return (grad_queries, grad_keys, grad_values)


def forward_layer(stream, weight, gain_one, gain_two):
    row_count = stream.shape[0]
    normed = gather_rows(layer_norm(stream, gain_one).astype(jnp.bfloat16))
    all_rows = normed.shape[0]
    clip_count = all_rows // SEQ
    project = jnp.einsum(
        "rd,sde->sre", normed, weight[0:3], preferred_element_type=jnp.float32
    ).astype(jnp.bfloat16)
    mixture = lax.map(
        attend_clip,
        (
            heads_of(project[0], clip_count),
            heads_of(project[1], clip_count),
            heads_of(project[2], clip_count),
        ),
    )
    mixture = mixture.reshape(all_rows, -1)

    def attn_term(first_row, row_num):
        return lax.dot_general(
            mixture, weight[3], (((1,), (1,)), ((), ())), preferred_element_type=jnp.float32
        )

    resid_one = stream + branch_total(attn_term, row_count)
    normed_two = gather_rows(layer_norm(resid_one, gain_two).astype(jnp.bfloat16))
    upward = jnp.einsum("rd,jde->jre", normed_two, weight[4:8], preferred_element_type=jnp.float32)
    hidden = exact_gelu(upward).astype(jnp.bfloat16)

    def mlp_term(first_row, row_num):
        return jnp.einsum("jre,jde->rd", hidden, weight[8:12], preferred_element_type=jnp.float32)

    result = resid_one + branch_total(mlp_term, row_count)
    return (result, (stream, normed, project, mixture, resid_one, normed_two, upward, hidden))


def backward_layer(grad_out, saved, weight, gain_one, gain_two):
    stream, normed, project, mixture, resid_one, normed_two, upward, hidden = saved
    row_count = stream.shape[0]
    all_rows = normed.shape[0]
    clip_count = all_rows // SEQ
    back_mlp = gather_grads(grad_out.astype(jnp.bfloat16))
    grad_down = jnp.einsum("rd,jre->jde", back_mlp, hidden, preferred_element_type=jnp.float32)
    grad_hidden = jnp.einsum(
        "rd,jde->jre", back_mlp, weight[8:12], preferred_element_type=jnp.float32
    )
    gelu_out, gelu_back = jax.vjp(exact_gelu, upward)
    grad_upward = gelu_back(grad_hidden)[0].astype(jnp.bfloat16)
    grad_up = jnp.einsum("rd,jre->jde", normed_two, grad_upward, preferred_element_type=jnp.float32)

    def up_term(first_row, row_num):
        return jnp.einsum(
            "jre,jde->rd", grad_upward, weight[4:8], preferred_element_type=jnp.float32
        )

    grad_normed_two = input_total(up_term, row_count)
    norm_out, norm_back = jax.vjp(layer_norm, resid_one, gain_two)
    part_stream, grad_gain_two = norm_back(grad_normed_two)
    grad_resid = grad_out + part_stream
    back_attn = gather_grads(grad_resid.astype(jnp.bfloat16))
    grad_out_proj = lax.dot_general(
        back_attn, mixture, (((0,), (0,)), ((), ())), preferred_element_type=jnp.float32
    )
    grad_mixture = jnp.dot(back_attn, weight[3], preferred_element_type=jnp.float32).astype(
        jnp.bfloat16
    )
    grad_heads = lax.map(
        attend_back_clip,
        (
            heads_of(project[0], clip_count),
            heads_of(project[1], clip_count),
            heads_of(project[2], clip_count),
            heads_of(grad_mixture, clip_count),
        ),
    )
    grad_project = jnp.stack([piece.reshape(all_rows, -1) for piece in grad_heads])
    grad_qkv = jnp.einsum("rd,sre->sde", normed, grad_project, preferred_element_type=jnp.float32)

    def qkv_term(first_row, row_num):
        return jnp.einsum(
            "sre,sde->rd", grad_project, weight[0:3], preferred_element_type=jnp.float32
        )

    grad_normed = input_total(qkv_term, row_count)
    norm_out_one, norm_back_one = jax.vjp(layer_norm, stream, gain_one)
    part_in, grad_gain_one = norm_back_one(grad_normed)
    grad_matrix = jnp.concatenate([grad_qkv, grad_out_proj[None], grad_up, grad_down], axis=0)
    return (grad_resid + part_in, grad_matrix, grad_gain_one, grad_gain_two)


def masked_rows(mask_index, mask_count, row_count):
    positions = lax.iota(jnp.int32, SEQ)
    slots = lax.iota(jnp.int32, mask_index.shape[1])
    live = slots[None, :] < mask_count[:, None]
    hits = (mask_index[:, :, None] == positions[None, None, :]) & live[:, :, None]
    flag_all = jnp.any(hits, axis=1).astype(jnp.float32).reshape(-1)
    return lax.dynamic_slice_in_dim(flag_all, lax.axis_index("narrow") * row_count, row_count, 0)


def shards_general(
    patches,
    cotangent,
    mask_index,
    mask_count,
    weights,
    first_moment,
    second_moment,
    small_params,
    small_first,
    small_second,
):
    row_count = patches.shape[0]
    narrow_size = lax.axis_size("narrow")
    owned_rows = weights.shape[2]
    matrices, small_low = (
        lax.all_gather(weights.astype(jnp.bfloat16), "wide", axis=2, tiled=True),
        lax.all_gather(small_params.astype(jnp.bfloat16), "wide", axis=1, tiled=True),
    )
    gains = small_low.astype(jnp.float32)
    flags = masked_rows(mask_index, mask_count, row_count)[:, None]
    stream = patches.astype(jnp.float32) * (1.0 - flags) + flags * gains[2 * LAYERS][None, :]
    saved_all = []
    for layer_idx in range(LAYERS):
        stream, saved = forward_layer(
            stream, matrices[layer_idx], gains[2 * layer_idx], gains[2 * layer_idx + 1]
        )
        saved_all.append(saved)
    grad_stream = cotangent
    grad_mats = [None] * LAYERS
    grad_gains = [None] * (2 * LAYERS)
    for layer_idx in reversed(range(LAYERS)):
        (
            grad_stream,
            grad_mats[layer_idx],
            grad_gains[2 * layer_idx],
            grad_gains[2 * layer_idx + 1],
        ) = backward_layer(
            grad_stream,
            saved_all[layer_idx],
            matrices[layer_idx],
            gains[2 * layer_idx],
            gains[2 * layer_idx + 1],
        )
    input_grad = grad_stream * (1.0 - flags)
    grad_embed = jnp.sum(grad_stream * flags, axis=0)
    grad_small = jnp.stack(grad_gains + [grad_embed])
    grad_matrix = jnp.stack(grad_mats)
    first_col = lax.axis_index("wide") * owned_rows
    small_total = lax.psum(grad_small, ("wide", "narrow"))
    small_own = lax.dynamic_slice_in_dim(small_total, first_col, owned_rows, 1)
    matrix_total = lax.psum(grad_matrix, "wide")
    matrix_own = lax.dynamic_slice_in_dim(matrix_total, first_col, owned_rows, 2)
    local_square = jnp.sum(matrix_own * matrix_own) + jnp.sum(small_own * small_own) / narrow_size
    grad_norm = jnp.sqrt(lax.psum(local_square, ("wide", "narrow")))
    factor = jnp.minimum(1.0, CLIP_MAX / grad_norm)
    new_weights, new_first, new_second = adam_values(
        weights, first_moment, second_moment, matrix_own * factor, D ** (-0.5), DECAY_RATE
    )
    new_small, new_small_first, new_small_second = adam_values(
        small_params, small_first, small_second, small_own * factor, RATE_SMALL, 0.0
    )
    return (
        stream,
        input_grad,
        new_weights,
        new_first,
        new_second,
        new_small,
        new_small_first,
        new_small_second,
        grad_norm,
    )


def solution(mesh):
    in_specs = (
        P(("wide", "narrow"), None),
        P(("wide", "narrow"), None),
        P("wide", None),
        P("wide"),
        P(None, None, "wide", "narrow"),
        P(None, None, "wide", "narrow"),
        P(None, None, "wide", "narrow"),
        P(None, "wide"),
        P(None, "wide"),
        P(None, "wide"),
    )
    out_specs = (
        P(("wide", "narrow"), None),
        P(("wide", "narrow"), None),
        P(None, None, "wide", "narrow"),
        P(None, None, "wide", "narrow"),
        P(None, None, "wide", "narrow"),
        P(None, "wide"),
        P(None, "wide"),
        P(None, "wide"),
        P(),
    )
    fits = mesh.shape["wide"] == NZ * NX and mesh.shape["narrow"] == 4
    step = shards if fits else shards_general
    return jax.shard_map(step, mesh=mesh, in_specs=in_specs, out_specs=out_specs, check_vma=False)
```

```python
import functools

import jax
import jax.numpy as jnp
from jax import lax
from jax.experimental import pallas as pl
from jax.experimental.pallas import tpu as pltpu
from jax.sharding import PartitionSpec as P

D = 768
HD = 64
LAYERS = 2
SEQ = 512
STEP = 10

EPS_NORM = 1e-06
BETA_ONE = 0.9
BETA_TWO = 0.999
EPS_ADAM = 1e-08
DECAY_RATE = 0.05
RATE_SMALL = 0.6
CLIP_MAX = 1.0

MESH = pl.DeviceIdType.MESH
F32 = jnp.float32
BF16 = jnp.bfloat16

PAIRS = 12
ADAM_STEPS = 2
PER = 6
NZ, NX = 4, 2
ROWS = 96
PARTS = 3
EARLY = 2
PART = ROWS // PARTS
COL = 192
WIDE = 2 * COL
SCALE = HD ** (-0.5)
TM = 256
TR = 64
HEADS_Y = COL // HD

WSLOTS = 4
STEPS = 82
BEGUN = 3
PLAN_WORDS = (
    (
        8, 66, 520, 72, 8, 579, 1096, 4104, 8, 64, 4097, 1,
        576, 584, 8, 4097, 4672, 4105, 4096, 576, 0, 4096, 4688, 0,
        576, 0, 576, 4096, 4096, 512, 4096, 0, 0, 36864, 0, 0,
        32768, 0, 0, 0, 262144, 32768, 0, 2359296, 32768, 262144, 2097152, 0,
        0, 17039360, 32768, 4194304, 32768, 16777216, 134217728, 262144, 16809984, 2359296, 32768, 0,
        2097152, 0, 17039360, 32768, 2359296, 16809984, 16777216, 0, 16777216, 2359296, 262144, 2129920,
        0, 2129920, 262144, 150994944, 33554432, 134479872, 134217728, 18874368, 958398464, 134217728,
    ),
    (
        0, 0, 1, 0, 0, 2, 3, 0, 4, 0, 5, 6,
        70, 7, 8, 9, 73, 10, 11, 12, 35, 36, 37, 38,
        102, 39, 40, 41, 105, 45, 42, 46, 110, 43, 47, 111,
        44, 48, 49, 50, 51, 52, 53, 54, 55, 56, 118, 119,
        120, 57, 58, 59, 60, 13, 14, 78, 15, 79, 16, 17,
        18, 19, 20, 21, 22, 23, 24, 86, 87, 88, 25, 26,
        27, 28, 29, 0, 0, 30, 0, 0, 0, 0,
    ),
)


def mm(a, b):
    return lax.dot_general(a, b, (((1,), (0,)), ((), ())), preferred_element_type=F32)


def mm_nt(a, b):
    return lax.dot_general(a, b, (((1,), (1,)), ((), ())), preferred_element_type=F32)


def mm_tn(a, b):
    return lax.dot_general(a, b, (((0,), (0,)), ((), ())), preferred_element_type=F32)


def loop(count, body):
    def wrapped(i, carry):
        body(i)
        return carry

    lax.fori_loop(0, count, wrapped, 0)


def rows_at(i, size):
    return pl.ds(pl.multiple_of(i * size, size), size)


def step_kernel(
    weights, patch, cot, mask_index, mask_count, small,
    out_block, out_igrad, out_grad, out_small, out_norm,
    G, WF, S, R1, NRM, NRM2, QK, V, MIX, GP, HID, GR, ACC, XS, XR, BK, TA, TB, GU, GM, DQK, DV,
    FL, GAIN, GPIECE, SG, SR, NB, NZC, NXY, RB0Y, RB0X, RB1, RB2, RB2X, RBZ, RBM, RBMZ,
    wf_s, ag_s, ag_r, ex_s, ex_r, in_s, in_r, lc_s, gn_s, gn_r, fs_s, fs_r, nm_s, nm_r,
):
    wide = lax.axis_index("wide")
    narrow = lax.axis_index("narrow")
    z, x = wide // NX, wide % NX
    y, c = narrow // 2, narrow % 2

    dev_core = (wide, 2 * y + 1 - c)
    dev_x = (z * NX + 1 - x, narrow)
    dev_y = (wide, 2 * (1 - y) + c)

    def z_to(k):
        return (z + k) % NZ

    def z_from(k):
        return (z + NZ - k) % NZ

    def dev_z(k):
        return (z_to(k) * NX + x, narrow)

    dev_xy = (z * NX + 1 - x, 2 * (1 - y) + c)

    def dev_zc(k):
        return (z_to(k) * NX + x, 2 * y + 1 - c)

    def load_pair(p):
        return pltpu.make_async_copy(weights.at[pl.ds(2 * p, 2)], WF.at[p % WSLOTS], wf_s.at[p % WSLOTS])

    for p in range(WSLOTS):
        load_pair(p).start()

    greeted = [dev_core, dev_x, dev_y, dev_xy] + [dev(k) for k in range(1, NZ) for dev in (dev_z, dev_zc)]
    barrier = pltpu.get_barrier_semaphore()
    for dev in greeted:
        pl.semaphore_signal(barrier, inc=1, device_id=dev, device_id_type=MESH)

    def remote(src, dst, send, recv, dev):
        return pltpu.make_async_remote_copy(
            src_ref=src, dst_ref=dst, send_sem=send, recv_sem=recv, device_id=dev, device_id_type=MESH
        )

    def lazy(*what):
        return lambda: remote(*what)

    ALL = slice(None)
    own = {"x": x, "y": y, "z": z}
    far = NZ - 1
    inner = jnp.logical_and(z > 0, z < far)
    outer = jnp.logical_or(z == 0, z == far)

    def block(p, h, where):
        return G.at[p, where["y"], where["z"], where["x"], h]

    def holding(axes):
        return {q: (ALL if q in axes else own[q]) for q in own}

    def along(axis):
        return (3, dev_x, 1 - x) if axis == "x" else (4, dev_y, 1 - y)

    def along_z(action):
        @pl.when(z != far)
        def _():
            action(1)

        action(2)

        @pl.when(z != 0)
        def _():
            action(3)

    def each_part(p, action):
        for test, h, order in (
            (p % 2 == 0, 0, ("z", "x", "y")),
            (p % 2 == 1, 0, ("z", "y", "x")),
            (p < EARLY, 1, ("z", "y", "x")),
            (p >= EARLY, 1, ("x", "z", "y")),
            (p < EARLY, 2, ("z", "x", "y")),
            (p >= EARLY, 2, ("y", "z", "x")),
        ):

            @pl.when(test)
            def _():
                action(h, order)

    def gather_plain(p, h, order, axis):
        slot, dev, there = along(axis)
        have = holding(order[: order.index(axis)])
        src = block(p, h, have)
        got = block(p, h, {**have, axis: there})
        send, recv = ag_s.at[p, h, slot], ag_r.at[p, h, slot]
        return lazy(src, src, send, recv, dev), lazy(got, got, send, recv, dev)

    def gather_z(p, h, order, k):
        have = holding(order[: order.index("z")])
        src = block(p, h, have)
        got = block(p, h, {**have, "z": z_from(k)})
        send, recv = ag_s.at[p, h, k - 1], ag_r.at[p, h, k - 1]
        return lazy(src, src, send, recv, dev_z(k)), lazy(got, got, send, recv, dev_z(k))

    def gather_relay(p, h, order):
        have = holding(order[: order.index("z")])
        src = block(p, h, {**have, "z": z_from(2)})
        dev = (far * (z - 1) * NX + x, narrow)
        return lazy(src, src, ag_s.at[p, h, 5], ag_r.at[p, h, 2 * (z - 1)], dev)

    def gather_steps(order):
        at = order.index("z") + 1
        return order[:at] + ("relay",) + order[at:]

    def gather_issue(p, step):
        def action(h, order):
            steps = gather_steps(order)
            before = steps[step - 1] if step > 0 else None
            if before == "z":
                gather_z(p, h, order, 2)[1]().wait_recv()
            elif before == "relay":
                for k in (1, 3):
                    gather_z(p, h, order, k)[1]().wait_recv()
            elif before is not None:
                gather_plain(p, h, order, before)[1]().wait_recv()
            if step == len(steps):
                return
            if steps[step] == "z":
                along_z(lambda k: gather_z(p, h, order, k)[0]().start())
            elif steps[step] == "relay":

                @pl.when(inner)
                def _():
                    gather_relay(p, h, order)().start()

            else:
                gather_plain(p, h, order, steps[step])[0]().start()

        each_part(p, action)

    def gather_sent(p):
        def action(h, order):
            along_z(lambda k: gather_z(p, h, order, k)[0]().wait_send())

            @pl.when(inner)
            def _():
                gather_relay(p, h, order)().wait_send()

            for axis in ("x", "y"):
                gather_plain(p, h, order, axis)[0]().wait_send()

        each_part(p, action)

    def pack(p):
        load_pair(p).wait()
        slot = p % WSLOTS
        both = jnp.concatenate([WF[slot, 0].astype(BF16), WF[slot, 1].astype(BF16)], axis=1)
        G[p, y, z, x] = both.reshape(PARTS, PART, WIDE)

        @pl.when(p + WSLOTS < PAIRS)
        def _():
            load_pair(p + WSLOTS).start()

    half = TM * c
    BKh = BK.at[pl.ds(pl.multiple_of(half, TM), TM)]
    GRh = GR.at[pl.ds(pl.multiple_of(half, TM), TM)]
    other = TM * (1 - c)
    BKo = BK.at[pl.ds(pl.multiple_of(other, TM), TM)]
    GRo = GR.at[pl.ds(pl.multiple_of(other, TM), TM)]
    patch_out = remote(patch, BKh, in_s.at[0], in_r.at[0], dev_core)
    patch_in = remote(patch, BKo, in_s.at[0], in_r.at[0], dev_core)
    cot_out = remote(cot, GRh, in_s.at[1], in_r.at[1], dev_core)
    cot_in = remote(cot, GRo, in_s.at[1], in_r.at[1], dev_core)
    patch_own = pltpu.make_async_copy(patch, BKh, lc_s.at[0])
    cot_own = pltpu.make_async_copy(cot, GRh, lc_s.at[1])
    patch_own.start()
    cot_own.start()
    GPIECE[z, x] = jnp.zeros((8, 128), F32)
    GPIECE[z, x, 0:5, 0:ROWS] = small[...].astype(BF16).astype(F32)
    gain_z = [
        (
            remote(GPIECE.at[z, x], GPIECE.at[z, x], gn_s.at[k - 1], gn_r.at[k - 1], dev_z(k)),
            remote(GPIECE.at[z_from(k), x], GPIECE.at[z_from(k), x], gn_s.at[k - 1], gn_r.at[k - 1], dev_z(k)),
        )
        for k in range(1, NZ)
    ]
    gain_x = (
        remote(GPIECE.at[:, x], GPIECE.at[:, x], gn_s.at[3], gn_r.at[3], dev_x),
        remote(GPIECE.at[:, 1 - x], GPIECE.at[:, 1 - x], gn_s.at[3], gn_r.at[3], dev_x),
    )
    loop(BEGUN, pack)
    pl.semaphore_wait(barrier, len(greeted))
    for s, _ in gain_z:
        s.start()
    patch_out.start()
    loop(BEGUN, lambda p: gather_issue(p, 0))
    cot_out.start()

    def gains_across(l, yy):
        index_row = mask_index[pl.ds(y, 1), :]
        count = mask_count[y]
        spot = lax.broadcasted_iota(jnp.int32, (SEQ, index_row.shape[1]), 0)
        live = lax.broadcasted_iota(jnp.int32, (1, index_row.shape[1]), 1) < count
        hits = jnp.where(jnp.logical_and(spot == index_row, live), 1.0, 0.0)
        FL[...] = jnp.max(hits, axis=1, keepdims=True)
        for _, r in gain_z:
            r.wait_recv()
        gain_x[0].start()

    def first_rows(l, yy):
        gain_x[1].wait_recv()
        lane = lax.broadcasted_iota(jnp.int32, (128, D), 0)
        feature = lax.broadcasted_iota(jnp.int32, (128, D), 1)
        gains = jnp.zeros((8, D), F32)
        for zz in range(NZ):
            for xx in range(NX):
                place = jnp.logical_and(feature - ROWS * (zz * NX + xx) == lane, lane < ROWS)
                gains = gains + mm(GPIECE[zz, xx].astype(BF16), jnp.where(place, 1.0, 0.0).astype(BF16))
        GAIN[...] = gains
        patch_own.wait()
        patch_in.wait_recv()
        embed = GAIN[4:5, :]

        def mask_tile(i):
            rows = rows_at(i, TR)
            flag = FL[rows, :]
            S[0, rows, :] = BK[rows, :].astype(F32) * (1.0 - flag) + flag * embed

        loop(SEQ // TR, mask_tile)

    def norm_parts(values):
        centre = values - jnp.mean(values, axis=-1, keepdims=True)
        spread = jnp.mean(centre * centre, axis=-1, keepdims=True)
        return centre, lax.rsqrt(spread + EPS_NORM)

    def norm_into(dst, src, gain_row):
        gain = GAIN[pl.ds(gain_row, 1), :]

        def tile(i):
            rows = rows_at(i, TR)
            centre, inv = norm_parts(src[rows, :])
            dst[rows, :] = (centre * inv * gain).astype(BF16)

        loop(SEQ // TR, tile)

    def matrix(p, yy):
        return G[p, yy].reshape(D, WIDE)

    def exchange_copy(e, i):
        rows = rows_at(i, TM)
        return remote(XS.at[rows], XR.at[e, rows], ex_s.at[i], ex_r.at[e, i], dev_core)

    def give(e, value):
        XS[...] = value.astype(BF16)
        loop(SEQ // TM, lambda i: exchange_copy(e, i).start())

    def receive(e, take):
        def chunk(i):
            exchange_copy(e, i).wait_recv()

            def tile(j):
                rows = pl.ds(pl.multiple_of(i * TM + j * TR, TR), TR)
                take(rows, XS[rows, :].astype(F32) + XR[e, rows, :].astype(F32))

            loop(TM // TR, tile)

        loop(SEQ // TM, chunk)
        loop(SEQ // TM, lambda i: exchange_copy(e, i).wait_send())

    def attend(l, yy):
        def tile(i):
            rows = rows_at(i, TM)
            outs = []
            for hd in range(HEADS_Y):
                lo = hd * HD
                q = QK[l, yy, rows, lo : lo + HD]
                k = QK[l, yy, :, COL + lo : COL + lo + HD]
                v = V[l, yy, :, lo : lo + HD]
                s = mm_nt(q, k) * SCALE
                e = jnp.exp(s - jnp.max(s, axis=1, keepdims=True))
                probs = e / jnp.sum(e, axis=1, keepdims=True)
                outs.append(mm(probs.astype(BF16), v))
            MIX[l, yy, rows, :] = jnp.concatenate(outs, axis=1).astype(BF16)

        loop(SEQ // TM, tile)

    def attend_back(l, yy, hd):
        lo = hd * HD
        k = QK[l, yy, :, COL + lo : COL + lo + HD]
        v = V[l, yy, :, lo : lo + HD]

        def tile(i, carry):
            dk, dv = carry
            rows = rows_at(i, TM)
            q = QK[l, yy, rows, lo : lo + HD]
            dm = GM[yy, rows, lo : lo + HD]
            s = mm_nt(k, q) * SCALE
            e = jnp.exp(s - jnp.max(s, axis=0, keepdims=True))
            probs = e / jnp.sum(e, axis=0, keepdims=True)
            dp = mm_nt(v, dm)
            ds = probs * (dp - jnp.sum(probs * dp, axis=0, keepdims=True))
            ds = ds.astype(BF16)
            dv = dv + mm(probs.astype(BF16), dm)
            dk = dk + mm(ds, q)
            dq = mm_tn(ds, k) * SCALE
            DQK[yy, rows, lo : lo + HD] = dq.astype(BF16)
            return dk, dv

        zero = jnp.zeros((SEQ, HD), F32)
        dk, dv = lax.fori_loop(0, SEQ // TM, tile, (zero, zero))
        DQK[yy, :, COL + lo : COL + lo + HD] = (dk * SCALE).astype(BF16)
        DV[yy, :, lo : lo + HD] = dv.astype(BF16)

    def up_part(l, u, yy, p):
        ACC[:, 0:WIDE] = mm(NRM2[l], matrix(p, yy))

        def gelu(i):
            rows = rows_at(i, TR)
            v = ACC[rows, 0:WIDE]
            cdf = 0.5 * (1.0 + lax.erf(v * (2.0 ** -0.5)))
            HID[l, u, yy, rows, :] = (v * cdf).astype(BF16)
            pdf = jnp.exp(-0.5 * v * v) * 0.3989422804014327
            GP[l, u, yy, rows, :] = (cdf + v * pdf).astype(BF16)

        loop(SEQ // TR, gelu)

    def ln_one(l, yy):
        norm_into(NRM.at[l], S.at[l], 2 * l)

    def project_qk(l, yy):
        def one(side):
            QK[l, side] = mm(NRM[l], matrix(l * PER, side)).astype(BF16)

        loop(2, one)

    def project_v(l, yy):
        def one(side):
            V[l, side] = mm(NRM[l], matrix(l * PER + 1, side)[:, :COL]).astype(BF16)

        loop(2, one)

    def attn_out(l, yy):
        p = l * PER + 1
        total = mm_nt(MIX[l, 0], matrix(p, 0)[:, COL:])
        give(0, total + mm_nt(MIX[l, 1], matrix(p, 1)[:, COL:]))

    def attn_resid(l, yy):
        def take(rows, total):
            R1[l, rows, :] = S[l, rows, :] + total

        receive(0, take)
        norm_into(NRM2.at[l], R1.at[l], 2 * l + 1)

    def up(l, u):
        loop(2, lambda side: up_part(l, u, side, l * PER + 2 + u))

    def down_one(l, yy):
        p = l * PER + 4
        ACC[...] = mm_nt(HID[l, 0, 0], matrix(p, 0)) + mm_nt(HID[l, 0, 1], matrix(p, 1))

    def down_two(l, yy):
        p = l * PER + 5
        total = ACC[...] + mm_nt(HID[l, 1, 0], matrix(p, 0))
        give(1, total + mm_nt(HID[l, 1, 1], matrix(p, 1)))

    def layer_end(l, yy):
        def take(rows, total):
            value = R1[l, rows, :] + total

            @pl.when(l == 0)
            def _():
                S[1, rows, :] = value

            @pl.when(l == 1)
            def _():
                ACC[rows, :] = value

        receive(1, take)

        @pl.when(l == 1)
        def _():
            block_copy.start()

    block_copy = pltpu.make_async_copy(ACC.at[pl.ds(pl.multiple_of(half, TM), TM)], out_block, lc_s.at[2])

    def scatter_plain(p, h, order, axis):
        slot, dev, there = along(axis)
        place = order.index(axis)
        have = {q: (own[q] if q in order[:place] else ALL) for q in own}
        if place == 0:
            dst = (RB0Y if axis == "y" else RB0X).at[p if h > 0 else PAIRS + p // 2]
        else:
            dst = RB1.at[first_slot(p, h)] if z_last(order) else RB2X.at[p - EARLY, h - 1]
        send, recv = ag_s.at[p, h, slot], ag_r.at[late(p), h, slot]
        src = block(p, h, {**have, axis: there})
        return lazy(src, dst, send, recv, dev), lazy(dst, dst, send, recv, dev), dst

    def z_last(order):
        return order[2] == "z"

    def first_slot(p, h):
        return p if h == 0 else PAIRS + EARLY * (h - 1) + p

    def late(p):
        return (p + PER) % PAIRS

    def scatter_have(order):
        return {q: (own[q] if q in order[: order.index("z")] else ALL) for q in own}

    def scatter_z(p, h, order, k):
        dst = RB2.at[first_slot(p, h), k - 1] if z_last(order) else RBZ.at[p - EARLY, h - 1, k - 1]
        send, recv = ag_s.at[p, h, k - 1], ag_r.at[late(p), h, k - 1]
        src = block(p, h, {**scatter_have(order), "z": z_to(k)})
        return lazy(src, dst, send, recv, dev_z(k)), lazy(dst, dst, send, recv, dev_z(k)), dst

    def scatter_merge(p, h, order):
        dst = RBM.at[first_slot(p, h)] if z_last(order) else RBMZ.at[p - EARLY, h - 1]
        dev = ((1 + z // far) * NX + x, narrow)
        send, recv = ag_s.at[p, h, 5], ag_r.at[late(p), h, 5]
        src = block(p, h, {**scatter_have(order), "z": far - z})
        return lazy(src, dst, send, recv, dev), lazy(dst, dst, send, recv, dev), dst

    def scatter_steps(order):
        at = order.index("z")
        return order[:at] + ("merge",) + order[at:]

    def scatter_issue(p, step):
        def action(h, forward_order):
            order = forward_order[::-1]
            steps = scatter_steps(order)
            before = steps[step - 1] if step > 0 else None
            if before is not None and before != "merge":
                have = {q: (own[q] if q in order[: order.index(before) + 1] else ALL) for q in own}
                view = block(p, h, have)
                if before == "z":
                    scatter_z(p, h, order, 2)[1]().wait_recv()

                    @pl.when(z != 0)
                    def _():
                        scatter_z(p, h, order, 1)[1]().wait_recv()

                    @pl.when(z != far)
                    def _():
                        scatter_z(p, h, order, 3)[1]().wait_recv()

                    total = view[...].astype(F32) + scatter_z(p, h, order, 2)[2][...].astype(F32)
                    for k, there in ((1, z != 0), (3, z != far)):
                        total = total + jnp.where(there, scatter_z(p, h, order, k)[2][...].astype(F32), 0.0)
                else:
                    scatter_plain(p, h, order, before)[1]().wait_recv()
                    total = view[...].astype(F32) + scatter_plain(p, h, order, before)[2][...].astype(F32)
                if step < len(steps):
                    view[...] = total.astype(BF16)
                else:
                    out_grad[p, h] = total
                    NB[...] += fold(total * total)
            if step == len(steps):
                return
            if steps[step] == "merge":

                @pl.when(outer)
                def _():
                    scatter_merge(p, h, order)[0]().start()

            elif steps[step] == "z":

                @pl.when(inner)
                def _():
                    scatter_merge(p, h, order)[1]().wait_recv()
                    view = block(p, h, {**scatter_have(order), "z": z_to(2)})
                    term = scatter_merge(p, h, order)[2][...].astype(F32)
                    view[...] = (view[...].astype(F32) + term).astype(BF16)

                along_z(lambda k: scatter_z(p, h, order, k)[0]().start())
            else:
                scatter_plain(p, h, order, steps[step])[0]().start()

        each_part(p, action)

    def fold(sq):
        sq = jnp.sum(sq.reshape(PART // 8, 8, WIDE), axis=0)
        return sq[:, 0:128] + sq[:, 128:256] + sq[:, 256:384]

    def scatter_sent(p):
        def action(h, forward_order):
            order = forward_order[::-1]
            for axis in ("x", "y"):
                scatter_plain(p, h, order, axis)[0]().wait_send()

            @pl.when(outer)
            def _():
                scatter_merge(p, h, order)[0]().wait_send()

            along_z(lambda k: scatter_z(p, h, order, k)[0]().wait_send())

        each_part(p, action)

    NB[...] = jnp.zeros((8, 128), F32)
    SG[...] = jnp.zeros_like(SG)

    def transpose_into(dst, src):
        def tile(i):
            rows = rows_at(i, 128)
            dst[:, rows] = jnp.transpose(src[rows, :])

        loop(SEQ // 128, tile)

    def put_grad(p, yy, left, right):
        G[p, yy] = mm(left[...], right).astype(BF16).reshape(NZ, NX, PARTS, PART, WIDE)

    def norm_back(e, src, gain_row):
        gain = GAIN[pl.ds(gain_row, 1), :]
        def take(rows, dn):
            centre, inv = norm_parts(src[rows, :])
            xhat = centre * inv
            dh = dn * gain
            dv = inv * (
                dh
                - jnp.mean(dh, axis=-1, keepdims=True)
                - xhat * jnp.mean(dh * xhat, axis=-1, keepdims=True)
            )
            GR[rows, :] += dv
            SG[pl.ds(gain_row, 1), :] += jnp.sum(dn * xhat, axis=0, keepdims=True)

        receive(e, take)

    def cast_rows(dst, src):
        def tile(i):
            rows = rows_at(i, TR)
            dst[rows, :] = src[rows, :].astype(BF16)

        loop(SEQ // TR, tile)

    def both(action):
        loop(2, action)

    def back_prepare(l, yy):
        @pl.when(l == 1)
        def _():
            cot_own.wait()
            cot_in.wait_recv()
            cot_out.wait_send()

        cast_rows(BK, GR)
        transpose_into(TA, BK)
        transpose_into(TB, NRM2.at[l])

    def back_down(l, u, side):
        p = l * PER + 4 + u

        @pl.when(side == 0)
        def _():
            gather_sent(p)

        gh = mm(BK[...], matrix(p, side))
        GU[u, side] = (gh * GP[l, u, side].astype(F32)).astype(BF16)
        put_grad(p, side, TA, HID[l, u, side])

    def back_up_sum(l, yy):
        p = l * PER + 2

        @pl.when(l == 1)
        def _():
            block_copy.wait()

        ACC[...] = mm_nt(GU[0, 0], matrix(p, 0)) + mm_nt(GU[0, 1], matrix(p, 1))

    def back_up_give(l, yy):
        p = l * PER + 3
        total = ACC[...] + mm_nt(GU[1, 0], matrix(p, 0))
        give(0, total + mm_nt(GU[1, 1], matrix(p, 1)))

    def back_up(l, u):
        p = l * PER + 2 + u
        gather_sent(p)
        both(lambda side: put_grad(p, side, TB, GU[u, side]))

    def back_norm_two(l, yy):
        norm_back(0, R1.at[l], 2 * l + 1)

    def back_attn_prepare(l, yy):
        cast_rows(BK, GR)
        transpose_into(TA, BK)
        transpose_into(TB, NRM.at[l])

        def grad_mix(side):
            GM[side] = mm(BK[...], matrix(l * PER + 1, side)[:, COL:]).astype(BF16)

        both(grad_mix)

    def back_attn_grads(l, yy):
        p = l * PER + 1
        gather_sent(p)
        ACC[...] = mm_nt(DV[0], matrix(p, 0)[:, :COL]) + mm_nt(DV[1], matrix(p, 1)[:, :COL])

        def grads(side):
            gv = mm(TB[...], DV[side])
            go = mm(TA[...], MIX[l, side])
            pair = jnp.concatenate([gv, go], axis=1).astype(BF16)
            G[p, side] = pair.reshape(NZ, NX, PARTS, PART, WIDE)

        both(grads)

    def back_qk_give(l, yy):
        p = l * PER
        total = ACC[...] + mm_nt(DQK[0], matrix(p, 0))
        give(1, total + mm_nt(DQK[1], matrix(p, 1)))

    def back_qk(l, yy):
        p = l * PER
        gather_sent(p)
        both(lambda side: put_grad(p, side, TB, DQK[side]))

    def back_norm_one(l, yy):
        norm_back(1, S.at[l], 2 * l)

    def position(i):
        s = i % PER
        slot = jnp.where(s < 2, s + 4, jnp.where(s < 4, s, 5 - s))
        return (LAYERS - 1 - i // PER) * PER + slot

    def scatter_at(t, phase):
        scatter_issue(position(t), phase)

    igrad_copy = pltpu.make_async_copy(GRh, out_igrad, lc_s.at[3])
    place = 2 * y + x
    around = ((2 * y + 1 - x, dev_x), (2 * (1 - y) + x, dev_y), (2 * (1 - y) + 1 - x, dev_xy))

    def small_z(k):
        got = SR.at[z_from(k), 0]
        return (
            remote(SR.at[z, 0], SR.at[z, 0], fs_s.at[k - 1], fs_r.at[k - 1], dev_z(k)),
            remote(got, got, fs_s.at[k - 1], fs_r.at[k - 1], dev_z(k)),
        )

    def small_xy(k):
        there, dev = around[k]
        return (
            remote(SR.at[place, 1], SR.at[place, 1], fs_s.at[3 + k], fs_r.at[3 + k], dev),
            remote(SR.at[there, 1], SR.at[there, 1], fs_s.at[3 + k], fs_r.at[3 + k], dev),
        )

    def rows_done():
        def finish_tile(i):
            rows = rows_at(i, TR)
            flag = FL[rows, :]
            value = GR[rows, :]
            SG[4:5, :] += jnp.sum(value * flag, axis=0, keepdims=True)
            GR[rows, :] = value * (1.0 - flag)

        loop(SEQ // TR, finish_tile)
        igrad_copy.start()
        SR[z, 0] = SG[...]
        for k in range(1, NZ):
            small_z(k)[0].start()

    def small_sums():
        for k in range(1, NZ):
            small_z(k)[1].wait_recv()
        SR[place, 1] = SR[0, 0] + SR[1, 0] + SR[2, 0] + SR[3, 0]
        for k in range(3):
            small_xy(k)[0].start()

    pieces = {
        "g1": gains_across,
        "g2": first_rows,
        "ln1": ln_one,
        "qk": project_qk,
        "v": project_v,
        "at": attend,
        "out": attn_out,
        "res": attn_resid,
        "up": up,
        "dn0": down_one,
        "dn1": down_two,
        "fin": layer_end,
        "b4p": back_prepare,
        "b4": lambda l, side: back_down(l, 0, side),
        "b5": lambda l, side: back_down(l, 1, side),
        "b2a": back_up_sum,
        "b2b": lambda l, yy: back_up(l, 0),
        "b3a": back_up_give,
        "b3b": lambda l, yy: back_up(l, 1),
        "b3c": back_norm_two,
        "b1p": back_attn_prepare,
        "ab0": lambda l, side: attend_back(l, side, 0),
        "ab1": lambda l, side: attend_back(l, side, 1),
        "ab2": lambda l, side: attend_back(l, side, 2),
        "b1f": back_attn_grads,
        "b0a": back_qk_give,
        "b0b": back_qk,
        "b0c": back_norm_one,
        "rows": lambda l, yy: rows_done(),
        "small": lambda l, yy: small_sums(),
    }
    def digit(word, k, base):
        return lax.rem(lax.div(word, base**k), base)

    def plan_of(m, low, high):
        if high - low == 1:
            return tuple(jnp.int32(words[low]) for words in PLAN_WORDS)
        middle = (low + high) // 2
        return lax.cond(m < middle, lambda: plan_of(m, low, middle), lambda: plan_of(m, middle, high))

    def micro(m, firsts):
        counts, word = plan_of(m, 0, STEPS)
        count = tuple(digit(counts, kind, 8) for kind in range(10))

        @pl.when(counts > 0)
        def _():
            for kind in range(10):
                action = gather_issue if kind < 5 else scatter_at

                @pl.when(count[kind] > 0)
                def _():
                    def one(i, carry):
                        if kind == 0:
                            pack(firsts[kind] + i)
                        action(firsts[kind] + i, kind % 5)
                        return carry

                    lax.fori_loop(0, count[kind], one, 0)


        @pl.when(word > 0)
        def _():
            what, l, yy = lax.rem(word, 32), digit(lax.div(word, 32), 0, 2), lax.div(word, 64)
            for i, action in enumerate(pieces.values()):

                @pl.when(what == i + 1)
                def _():
                    action(l, yy)

        return tuple(f + n for f, n in zip(firsts, count))

    lax.fori_loop(0, STEPS, micro, (jnp.int32(BEGUN),) + (jnp.int32(0),) * 9)

    own_square = jnp.sum(jnp.sum(NB[...], axis=1, keepdims=True), axis=0, keepdims=True)
    NZC[z, c] = jnp.broadcast_to(own_square, (8, 128))
    nm_z = []
    for j, (zz, cc, frm, dev) in enumerate(
        [(z, 1 - c, z, dev_core)]
        + [(z_to(k), c, z_from(k), dev_z(k)) for k in range(1, NZ)]
        + [(z_to(k), 1 - c, z_from(k), dev_zc(k)) for k in range(1, NZ)]
    ):
        got = NZC.at[frm, cc]
        nm_z.append(
            (
                remote(NZC.at[z, c], NZC.at[z, c], nm_s.at[j], nm_r.at[j], dev),
                remote(got, got, nm_s.at[j], nm_r.at[j], dev),
            )
        )
    for s, _ in nm_z:
        s.start()
    for k in range(3):
        small_xy(k)[1].wait_recv()
    total_small = SR[0, 1] + SR[1, 1] + SR[2, 1] + SR[3, 1]
    out_small[...] = total_small
    small_square = jnp.sum(jnp.sum(total_small * total_small, axis=1, keepdims=True), axis=0, keepdims=True)
    for _, r in nm_z:
        r.wait_recv()
    square = NZC[0, 0] + NZC[0, 1]
    for zz in range(1, NZ):
        square = square + (NZC[zz, 0] + NZC[zz, 1])
    NXY[place] = square
    nm_xy = [
        (
            remote(NXY.at[place], NXY.at[place], nm_s.at[7 + k], nm_r.at[7 + k], dev),
            remote(NXY.at[there], NXY.at[there], nm_s.at[7 + k], nm_r.at[7 + k], dev),
        )
        for k, (there, dev) in enumerate(around)
    ]
    for s, _ in nm_xy:
        s.start()
    for _, r in nm_xy:
        r.wait_recv()
    out_norm[...] = jnp.sqrt(NXY[0] + NXY[1] + NXY[2] + NXY[3] + small_square)

    for s, _ in [small_z(k) for k in range(1, NZ)] + [small_xy(k) for k in range(3)] + nm_z + nm_xy + gain_z:
        s.wait_send()
    gain_x[0].wait_send()
    patch_out.wait_send()
    loop(PAIRS, scatter_sent)
    igrad_copy.wait()


def big_step(weights, patches, cotangent, mask_index, mask_count, small):
    vm = pl.BlockSpec(memory_space=pltpu.VMEM)
    hb = pl.BlockSpec(memory_space=pl.ANY)
    sm = pl.BlockSpec(memory_space=pltpu.SMEM)
    dma = pltpu.SemaphoreType.DMA
    V = pltpu.VMEM
    scratch = [
        V((PAIRS, 2, NZ, NX, PARTS, PART, WIDE), BF16),
        V((WSLOTS, 2, ROWS, COL), F32),
        V((2, SEQ, D), F32),
        V((2, SEQ, D), F32),
        V((2, SEQ, D), BF16),
        V((2, SEQ, D), BF16),
        V((2, 2, SEQ, WIDE), BF16),
        V((2, 2, SEQ, COL), BF16),
        V((2, 2, SEQ, COL), BF16),
        V((2, 2, 2, SEQ, WIDE), BF16),
        V((2, 2, 2, SEQ, WIDE), BF16),
        V((SEQ, D), F32),
        V((SEQ, D), F32),
        V((SEQ, D), BF16),
        V((2, SEQ, D), BF16),
        V((SEQ, D), BF16),
        V((D, SEQ), BF16),
        V((D, SEQ), BF16),
        V((2, 2, SEQ, WIDE), BF16),
        V((2, SEQ, COL), BF16),
        V((2, SEQ, WIDE), BF16),
        V((2, SEQ, COL), BF16),
        V((SEQ, 1), F32),
        V((8, D), F32),
        V((NZ, NX, 8, 128), F32),
        V((8, D), F32),
        V((4, 2, 8, D), F32),
        V((8, 128), F32),
        V((NZ, 2, 8, 128), F32),
        V((4, 8, 128), F32),
        V((PAIRS + PAIRS // 2, NZ, NX, PART, WIDE), BF16),
        V((PAIRS + PAIRS // 2, 2, NZ, PART, WIDE), BF16),
        V((PAIRS + 2 * EARLY, NZ, PART, WIDE), BF16),
        V((PAIRS + 2 * EARLY, NZ - 1, PART, WIDE), BF16),
        V((PAIRS - EARLY, 2, PART, WIDE), BF16),
        V((PAIRS - EARLY, 2, NZ - 1, 2, PART, WIDE), BF16),
        V((PAIRS + 2 * EARLY, PART, WIDE), BF16),
        V((PAIRS - EARLY, 2, 2, PART, WIDE), BF16),
        dma((WSLOTS,)),
        dma((PAIRS, PARTS, 6)), dma((PAIRS, PARTS, 6)),
        dma((2,)), dma((2, 2)),
        dma((2,)), dma((2,)), dma((4,)),
        dma((4,)), dma((4,)),
        dma((6,)), dma((6,)),
        dma((10,)), dma((10,)),
    ]
    return pl.pallas_call(
        step_kernel,
        out_shape=(
            jax.ShapeDtypeStruct((TM, D), F32),
            jax.ShapeDtypeStruct((TM, D), F32),
            jax.ShapeDtypeStruct((PAIRS, PARTS, PART, WIDE), F32),
            jax.ShapeDtypeStruct((8, D), F32),
            jax.ShapeDtypeStruct((8, 128), F32),
        ),
        in_specs=[hb, hb, hb, vm, sm, vm],
        out_specs=(hb, hb, vm, vm, vm),
        scratch_shapes=scratch,
        compiler_params=pltpu.CompilerParams(
            collective_id=0, has_side_effects=True, vmem_limit_bytes=62 << 20
        ),
        name="train_step",
    )(weights, patches, cotangent, mask_index, mask_count, small)


def adam_values(weight_in, moment_one, moment_two, gradient, step_rate, decay_rate):
    moment_one = BETA_ONE * moment_one + (1.0 - BETA_ONE) * gradient
    moment_two = BETA_TWO * moment_two + (1.0 - BETA_TWO) * gradient * gradient
    first_hat = moment_one / (1.0 - BETA_ONE**STEP)
    second_hat = moment_two / (1.0 - BETA_TWO**STEP)
    updated = weight_in - step_rate * (
        first_hat / (jnp.sqrt(second_hat) + EPS_ADAM) + decay_rate * weight_in
    )
    return (updated, moment_one, moment_two)


def adam_kernel(
    norm, grad, small_total, small, small_one, small_two, block, igrad, w, m, v,
    nw, nm, nv, ns, nsm, nsv, grad_norm, block_out, igrad_out,
):
    factor = jnp.minimum(1.0, CLIP_MAX / norm[0:1, 0:1])
    for i in range(PAIRS // ADAM_STEPS):
        g = grad[i].reshape(ROWS, WIDE) * factor
        for j in range(2):
            k = 2 * i + j
            nw[k], nm[k], nv[k] = adam_values(
                w[k], m[k], v[k], g[:, j * COL : (j + 1) * COL], D ** (-0.5), DECAY_RATE
            )
    block_out[...] = block[...]
    igrad_out[...] = igrad[...]

    @pl.when(pl.program_id(0) == 0)
    def _():
        first = ROWS * lax.axis_index("wide")
        row = lax.broadcasted_iota(jnp.int32, (D, ROWS), 0)
        column = lax.broadcasted_iota(jnp.int32, (D, ROWS), 1)
        pick = jnp.where(row == column + first, 1.0, 0.0)
        own = lax.dot_general(
            small_total[...], pick, (((1,), (0,)), ((), ())),
            precision=lax.Precision.HIGHEST, preferred_element_type=F32,
        )[0:5]
        ns[...], nsm[...], nsv[...] = adam_values(
            small[...], small_one[...], small_two[...], own * factor, RATE_SMALL, 0.0
        )
        grad_norm[...] = norm[0:1, 0:1]


def adam_all(norm, grad, small_total, smalls, rows, matrices):
    shape = matrices[0].shape
    flat = (LAYERS * 12, ROWS, COL)
    blk = pl.BlockSpec((2 * PAIRS // ADAM_STEPS, ROWS, COL), lambda i: (i, 0, 0))
    row_blk = pl.BlockSpec((TM // ADAM_STEPS, D), lambda i: (i, 0))

    def whole(*dims):
        return pl.BlockSpec(dims, lambda i: (0,) * len(dims))

    outs = pl.pallas_call(
        adam_kernel,
        grid=(ADAM_STEPS,),
        out_shape=(
            *(jax.ShapeDtypeStruct(flat, F32) for _ in range(3)),
            *(jax.ShapeDtypeStruct((5, ROWS), F32) for _ in range(3)),
            jax.ShapeDtypeStruct((1, 1), F32),
            *(jax.ShapeDtypeStruct((TM, D), F32) for _ in range(2)),
        ),
        in_specs=[
            whole(8, 128),
            pl.BlockSpec((PAIRS // ADAM_STEPS, PARTS, PART, WIDE), lambda i: (i, 0, 0, 0)),
            whole(8, D),
            *(whole(5, ROWS) for _ in range(3)),
            row_blk, row_blk,
            blk, blk, blk,
        ],
        out_specs=(
            blk, blk, blk, *(whole(5, ROWS) for _ in range(3)), whole(1, 1), row_blk, row_blk,
        ),
        compiler_params=pltpu.CompilerParams(vmem_limit_bytes=62 << 20),
        name="adam",
    )(norm, grad, small_total, *smalls, *rows, *(a.reshape(flat) for a in matrices))
    return tuple(o.reshape(shape) for o in outs[:3]), outs[3:6], outs[6].reshape(()), outs[7:]


def shards(patches, cotangent, mask_index, mask_count, weights, first_moment, second_moment,
           small_params, small_first, small_second):
    block_output, input_grad, grad_own, small_total, norm = big_step(
        weights.reshape(LAYERS * 12, ROWS, COL), patches, cotangent, mask_index, mask_count, small_params
    )
    new_matrices, new_smalls, grad_norm, rows = adam_all(
        norm, grad_own, small_total, (small_params, small_first, small_second),
        (block_output, input_grad), (weights, first_moment, second_moment),
    )
    return (*rows, *new_matrices, *new_smalls, grad_norm)


def layer_norm(values, gain):
    centre = values - jnp.mean(values, axis=-1, keepdims=True)
    spread = jnp.mean(centre * centre, axis=-1, keepdims=True)
    return centre * lax.rsqrt(spread + EPS_NORM) * gain


def exact_gelu(values):
    return jax.nn.gelu(values, approximate=False)


def gather_rows(share):
    return lax.all_gather(share, "narrow", axis=0, tiled=True)


def gather_grads(share):
    return lax.all_gather(share, "narrow", axis=0, tiled=True)


def branch_total(term, row_count):
    return lax.psum_scatter(
        term(jnp.int32(0), row_count * lax.axis_size("narrow")).astype(jnp.bfloat16),
        "narrow",
        scatter_dimension=0,
        tiled=True,
    ).astype(jnp.float32)


def input_total(term, row_count):
    return lax.psum_scatter(
        term(jnp.int32(0), row_count * lax.axis_size("narrow")).astype(jnp.bfloat16),
        "narrow",
        scatter_dimension=0,
        tiled=True,
    ).astype(jnp.float32)


def heads_of(values, clip_count):
    return values.reshape(clip_count, SEQ, values.shape[1] // HD, HD)


def attend_clip(parts):
    queries, key_rows, value_rows = parts
    scores = jnp.einsum(
        "qhd,khd->hqk", queries, key_rows, preferred_element_type=jnp.float32
    ) * HD ** (-0.5)
    probs = jax.nn.softmax(scores, axis=-1)
    return jnp.einsum(
        "hqk,khd->qhd", probs.astype(jnp.bfloat16), value_rows, preferred_element_type=jnp.float32
    ).astype(jnp.bfloat16)


def attend_back_clip(parts):
    queries, key_rows, value_rows, grad_mix = parts
    scale = HD ** (-0.5)
    scores = (
        jnp.einsum("qhd,khd->hqk", queries, key_rows, preferred_element_type=jnp.float32) * scale
    )
    probs = jax.nn.softmax(scores, axis=-1)
    grad_values = jnp.einsum(
        "hqk,qhd->khd", probs.astype(jnp.bfloat16), grad_mix, preferred_element_type=jnp.float32
    ).astype(jnp.bfloat16)
    grad_probs = jnp.einsum(
        "qhd,khd->hqk", grad_mix, value_rows, preferred_element_type=jnp.float32
    )
    grad_scores = probs * (grad_probs - jnp.sum(probs * grad_probs, axis=-1, keepdims=True))
    grad_scores = grad_scores.astype(jnp.bfloat16)
    grad_queries = (
        jnp.einsum("hqk,khd->qhd", grad_scores, key_rows, preferred_element_type=jnp.float32)
        * scale
    ).astype(jnp.bfloat16)
    grad_keys = (
        jnp.einsum("hqk,qhd->khd", grad_scores, queries, preferred_element_type=jnp.float32) * scale
    ).astype(jnp.bfloat16)
    return (grad_queries, grad_keys, grad_values)


def forward_layer(stream, weight, gain_one, gain_two):
    row_count = stream.shape[0]
    normed = gather_rows(layer_norm(stream, gain_one).astype(jnp.bfloat16))
    all_rows = normed.shape[0]
    clip_count = all_rows // SEQ
    project = jnp.einsum(
        "rd,sde->sre", normed, weight[0:3], preferred_element_type=jnp.float32
    ).astype(jnp.bfloat16)
    mixture = lax.map(
        attend_clip,
        (
            heads_of(project[0], clip_count),
            heads_of(project[1], clip_count),
            heads_of(project[2], clip_count),
        ),
    )
    mixture = mixture.reshape(all_rows, -1)

    def attn_term(first_row, row_num):
        return lax.dot_general(
            mixture, weight[3], (((1,), (1,)), ((), ())), preferred_element_type=jnp.float32
        )

    resid_one = stream + branch_total(attn_term, row_count)
    normed_two = gather_rows(layer_norm(resid_one, gain_two).astype(jnp.bfloat16))
    upward = jnp.einsum("rd,jde->jre", normed_two, weight[4:8], preferred_element_type=jnp.float32)
    hidden = exact_gelu(upward).astype(jnp.bfloat16)

    def mlp_term(first_row, row_num):
        return jnp.einsum("jre,jde->rd", hidden, weight[8:12], preferred_element_type=jnp.float32)

    result = resid_one + branch_total(mlp_term, row_count)
    return (result, (stream, normed, project, mixture, resid_one, normed_two, upward, hidden))


def backward_layer(grad_out, saved, weight, gain_one, gain_two):
    stream, normed, project, mixture, resid_one, normed_two, upward, hidden = saved
    row_count = stream.shape[0]
    all_rows = normed.shape[0]
    clip_count = all_rows // SEQ
    back_mlp = gather_grads(grad_out.astype(jnp.bfloat16))
    grad_down = jnp.einsum("rd,jre->jde", back_mlp, hidden, preferred_element_type=jnp.float32)
    grad_hidden = jnp.einsum(
        "rd,jde->jre", back_mlp, weight[8:12], preferred_element_type=jnp.float32
    )
    gelu_out, gelu_back = jax.vjp(exact_gelu, upward)
    grad_upward = gelu_back(grad_hidden)[0].astype(jnp.bfloat16)
    grad_up = jnp.einsum("rd,jre->jde", normed_two, grad_upward, preferred_element_type=jnp.float32)

    def up_term(first_row, row_num):
        return jnp.einsum(
            "jre,jde->rd", grad_upward, weight[4:8], preferred_element_type=jnp.float32
        )

    grad_normed_two = input_total(up_term, row_count)
    norm_out, norm_back = jax.vjp(layer_norm, resid_one, gain_two)
    part_stream, grad_gain_two = norm_back(grad_normed_two)
    grad_resid = grad_out + part_stream
    back_attn = gather_grads(grad_resid.astype(jnp.bfloat16))
    grad_out_proj = lax.dot_general(
        back_attn, mixture, (((0,), (0,)), ((), ())), preferred_element_type=jnp.float32
    )
    grad_mixture = jnp.dot(back_attn, weight[3], preferred_element_type=jnp.float32).astype(
        jnp.bfloat16
    )
    grad_heads = lax.map(
        attend_back_clip,
        (
            heads_of(project[0], clip_count),
            heads_of(project[1], clip_count),
            heads_of(project[2], clip_count),
            heads_of(grad_mixture, clip_count),
        ),
    )
    grad_project = jnp.stack([piece.reshape(all_rows, -1) for piece in grad_heads])
    grad_qkv = jnp.einsum("rd,sre->sde", normed, grad_project, preferred_element_type=jnp.float32)

    def qkv_term(first_row, row_num):
        return jnp.einsum(
            "sre,sde->rd", grad_project, weight[0:3], preferred_element_type=jnp.float32
        )

    grad_normed = input_total(qkv_term, row_count)
    norm_out_one, norm_back_one = jax.vjp(layer_norm, stream, gain_one)
    part_in, grad_gain_one = norm_back_one(grad_normed)
    grad_matrix = jnp.concatenate([grad_qkv, grad_out_proj[None], grad_up, grad_down], axis=0)
    return (grad_resid + part_in, grad_matrix, grad_gain_one, grad_gain_two)


def masked_rows(mask_index, mask_count, row_count):
    positions = lax.iota(jnp.int32, SEQ)
    slots = lax.iota(jnp.int32, mask_index.shape[1])
    live = slots[None, :] < mask_count[:, None]
    hits = (mask_index[:, :, None] == positions[None, None, :]) & live[:, :, None]
    flag_all = jnp.any(hits, axis=1).astype(jnp.float32).reshape(-1)
    return lax.dynamic_slice_in_dim(flag_all, lax.axis_index("narrow") * row_count, row_count, 0)


def shards_general(
    patches,
    cotangent,
    mask_index,
    mask_count,
    weights,
    first_moment,
    second_moment,
    small_params,
    small_first,
    small_second,
):
    row_count = patches.shape[0]
    narrow_size = lax.axis_size("narrow")
    owned_rows = weights.shape[2]
    matrices, small_low = (
        lax.all_gather(weights.astype(jnp.bfloat16), "wide", axis=2, tiled=True),
        lax.all_gather(small_params.astype(jnp.bfloat16), "wide", axis=1, tiled=True),
    )
    gains = small_low.astype(jnp.float32)
    flags = masked_rows(mask_index, mask_count, row_count)[:, None]
    stream = patches.astype(jnp.float32) * (1.0 - flags) + flags * gains[2 * LAYERS][None, :]
    saved_all = []
    for layer_idx in range(LAYERS):
        stream, saved = forward_layer(
            stream, matrices[layer_idx], gains[2 * layer_idx], gains[2 * layer_idx + 1]
        )
        saved_all.append(saved)
    grad_stream = cotangent
    grad_mats = [None] * LAYERS
    grad_gains = [None] * (2 * LAYERS)
    for layer_idx in reversed(range(LAYERS)):
        (
            grad_stream,
            grad_mats[layer_idx],
            grad_gains[2 * layer_idx],
            grad_gains[2 * layer_idx + 1],
        ) = backward_layer(
            grad_stream,
            saved_all[layer_idx],
            matrices[layer_idx],
            gains[2 * layer_idx],
            gains[2 * layer_idx + 1],
        )
    input_grad = grad_stream * (1.0 - flags)
    grad_embed = jnp.sum(grad_stream * flags, axis=0)
    grad_small = jnp.stack(grad_gains + [grad_embed])
    grad_matrix = jnp.stack(grad_mats)
    first_col = lax.axis_index("wide") * owned_rows
    small_total = lax.psum(grad_small, ("wide", "narrow"))
    small_own = lax.dynamic_slice_in_dim(small_total, first_col, owned_rows, 1)
    matrix_total = lax.psum(grad_matrix, "wide")
    matrix_own = lax.dynamic_slice_in_dim(matrix_total, first_col, owned_rows, 2)
    local_square = jnp.sum(matrix_own * matrix_own) + jnp.sum(small_own * small_own) / narrow_size
    grad_norm = jnp.sqrt(lax.psum(local_square, ("wide", "narrow")))
    factor = jnp.minimum(1.0, CLIP_MAX / grad_norm)
    new_weights, new_first, new_second = adam_values(
        weights, first_moment, second_moment, matrix_own * factor, D ** (-0.5), DECAY_RATE
    )
    new_small, new_small_first, new_small_second = adam_values(
        small_params, small_first, small_second, small_own * factor, RATE_SMALL, 0.0
    )
    return (
        stream,
        input_grad,
        new_weights,
        new_first,
        new_second,
        new_small,
        new_small_first,
        new_small_second,
        grad_norm,
    )


def solution(mesh):
    in_specs = (
        P(("wide", "narrow"), None),
        P(("wide", "narrow"), None),
        P("wide", None),
        P("wide"),
        P(None, None, "wide", "narrow"),
        P(None, None, "wide", "narrow"),
        P(None, None, "wide", "narrow"),
        P(None, "wide"),
        P(None, "wide"),
        P(None, "wide"),
    )
    out_specs = (
        P(("wide", "narrow"), None),
        P(("wide", "narrow"), None),
        P(None, None, "wide", "narrow"),
        P(None, None, "wide", "narrow"),
        P(None, None, "wide", "narrow"),
        P(None, "wide"),
        P(None, "wide"),
        P(None, "wide"),
        P(),
    )
    fits = mesh.shape["wide"] == NZ * NX and mesh.shape["narrow"] == 4
    step = shards if fits else shards_general
    return jax.shard_map(step, mesh=mesh, in_specs=in_specs, out_specs=out_specs, check_vma=False)
```

```python
import functools

import jax
import jax.numpy as jnp
from jax import lax
from jax.experimental import pallas as pl
from jax.experimental.pallas import tpu as pltpu
from jax.sharding import PartitionSpec as P

D = 768
HD = 64
LAYERS = 2
SEQ = 512
STEP = 10

EPS_NORM = 1e-06
BETA_ONE = 0.9
BETA_TWO = 0.999
EPS_ADAM = 1e-08
DECAY_RATE = 0.05
RATE_SMALL = 0.6
CLIP_MAX = 1.0

MESH = pl.DeviceIdType.MESH
F32 = jnp.float32
BF16 = jnp.bfloat16

PAIRS = 12
ADAM_STEPS = 2
PER = 6
NZ, NX = 4, 2
ROWS = 96
PARTS = 3
EARLY = 2
PART = ROWS // PARTS
COL = 192
WIDE = 2 * COL
SCALE = HD ** (-0.5)
TM = 256
TR = 64
HEADS_Y = COL // HD

WSLOTS = 4
STEPS = 82
BEGUN = 3
PLAN_WORDS = (
    (
        8, 66, 520, 72, 8, 579, 1096, 4104, 8, 64, 4097, 1,
        576, 584, 8, 4097, 4672, 4105, 4096, 576, 0, 4096, 4688, 0,
        576, 0, 576, 4096, 4096, 512, 4096, 0, 0, 36864, 0, 0,
        32768, 0, 0, 0, 262144, 32768, 0, 2359296, 32768, 262144, 2097152, 0,
        0, 17039360, 32768, 4194304, 32768, 16777216, 134217728, 262144, 16809984, 2359296, 32768, 0,
        2097152, 0, 17039360, 32768, 2359296, 16809984, 16777216, 0, 16777216, 2359296, 262144, 2129920,
        0, 2129920, 262144, 150994944, 33554432, 134479872, 134217728, 18874368, 958398464, 134217728,
    ),
    (
        0, 0, 1, 0, 0, 2, 3, 0, 4, 0, 5, 6,
        70, 7, 8, 9, 73, 10, 11, 12, 35, 36, 37, 38,
        102, 39, 40, 41, 105, 45, 42, 46, 110, 43, 47, 111,
        44, 48, 49, 50, 51, 52, 53, 54, 55, 56, 118, 119,
        120, 57, 58, 59, 60, 13, 14, 78, 15, 79, 16, 17,
        18, 19, 20, 21, 22, 23, 24, 86, 87, 88, 25, 26,
        27, 28, 29, 0, 0, 30, 0, 0, 0, 0,
    ),
)


def mm(a, b):
    return lax.dot_general(a, b, (((1,), (0,)), ((), ())), preferred_element_type=F32)


def mm_nt(a, b):
    return lax.dot_general(a, b, (((1,), (1,)), ((), ())), preferred_element_type=F32)


def mm_tn(a, b):
    return lax.dot_general(a, b, (((0,), (0,)), ((), ())), preferred_element_type=F32)


def loop(count, body):
    def wrapped(i, carry):
        body(i)
        return carry

    lax.fori_loop(0, count, wrapped, 0)


def rows_at(i, size):
    return pl.ds(pl.multiple_of(i * size, size), size)


def step_kernel(
    weights, patch, cot, mask_index, mask_count, small,
    out_block, out_igrad, out_grad, out_small, out_norm,
    G, WF, S, R1, NRM, NRM2, QK, V, MIX, GP, HID, GR, ACC, XS, XR, BK, TA, TB, GU, GM, DQK, DV,
    FL, GAIN, GPIECE, SG, SR, NB, NZC, NXY, RB0Y, RB0X, RB1, RB2, RB2X, RBZ, RBM, RBMZ,
    wf_s, ag_s, ag_r, ex_s, ex_r, in_s, in_r, lc_s, gn_s, gn_r, fs_s, fs_r, nm_s, nm_r,
):
    wide = lax.axis_index("wide")
    narrow = lax.axis_index("narrow")
    z, x = wide // NX, wide % NX
    y, c = narrow // 2, narrow % 2

    dev_core = (wide, 2 * y + 1 - c)
    dev_x = (z * NX + 1 - x, narrow)
    dev_y = (wide, 2 * (1 - y) + c)

    def z_to(k):
        return (z + k) % NZ

    def z_from(k):
        return (z + NZ - k) % NZ

    def dev_z(k):
        return (z_to(k) * NX + x, narrow)

    dev_xy = (z * NX + 1 - x, 2 * (1 - y) + c)

    def dev_zc(k):
        return (z_to(k) * NX + x, 2 * y + 1 - c)

    def load_pair(p):
        return pltpu.make_async_copy(weights.at[pl.ds(2 * p, 2)], WF.at[p % WSLOTS], wf_s.at[p % WSLOTS])

    for p in range(WSLOTS):
        load_pair(p).start()

    greeted = [dev_core, dev_x, dev_y, dev_xy] + [dev(k) for k in range(1, NZ) for dev in (dev_z, dev_zc)]
    barrier = pltpu.get_barrier_semaphore()
    for dev in greeted:
        pl.semaphore_signal(barrier, inc=1, device_id=dev, device_id_type=MESH)

    def remote(src, dst, send, recv, dev):
        return pltpu.make_async_remote_copy(
            src_ref=src, dst_ref=dst, send_sem=send, recv_sem=recv, device_id=dev, device_id_type=MESH
        )

    def lazy(*what):
        return lambda: remote(*what)

    ALL = slice(None)
    own = {"x": x, "y": y, "z": z}
    far = NZ - 1
    inner = jnp.logical_and(z > 0, z < far)
    outer = jnp.logical_or(z == 0, z == far)

    def block(p, h, where):
        return G.at[p, where["y"], where["z"], where["x"], h]

    def holding(axes):
        return {q: (ALL if q in axes else own[q]) for q in own}

    def along(axis):
        return (3, dev_x, 1 - x) if axis == "x" else (4, dev_y, 1 - y)

    def along_z(action):
        @pl.when(z != far)
        def _():
            action(1)

        action(2)

        @pl.when(z != 0)
        def _():
            action(3)

    def each_part(p, action):
        for test, h, order in (
            (p % 2 == 0, 0, ("z", "x", "y")),
            (p % 2 == 1, 0, ("z", "y", "x")),
            (p < EARLY, 1, ("z", "y", "x")),
            (p >= EARLY, 1, ("x", "z", "y")),
            (p < EARLY, 2, ("z", "x", "y")),
            (p >= EARLY, 2, ("y", "z", "x")),
        ):

            @pl.when(test)
            def _():
                action(h, order)

    def gather_plain(p, h, order, axis):
        slot, dev, there = along(axis)
        have = holding(order[: order.index(axis)])
        src = block(p, h, have)
        got = block(p, h, {**have, axis: there})
        send, recv = ag_s.at[p, h, slot], ag_r.at[p, h, slot]
        return lazy(src, src, send, recv, dev), lazy(got, got, send, recv, dev)

    def gather_z(p, h, order, k):
        have = holding(order[: order.index("z")])
        src = block(p, h, have)
        got = block(p, h, {**have, "z": z_from(k)})
        send, recv = ag_s.at[p, h, k - 1], ag_r.at[p, h, k - 1]
        return lazy(src, src, send, recv, dev_z(k)), lazy(got, got, send, recv, dev_z(k))

    def gather_relay(p, h, order):
        have = holding(order[: order.index("z")])
        src = block(p, h, {**have, "z": z_from(2)})
        dev = (far * (z - 1) * NX + x, narrow)
        return lazy(src, src, ag_s.at[p, h, 5], ag_r.at[p, h, 2 * (z - 1)], dev)

    def gather_steps(order):
        at = order.index("z") + 1
        return order[:at] + ("relay",) + order[at:]

    def gather_issue(p, step):
        def action(h, order):
            steps = gather_steps(order)
            before = steps[step - 1] if step > 0 else None
            if before == "z":
                gather_z(p, h, order, 2)[1]().wait_recv()
            elif before == "relay":
                for k in (1, 3):
                    gather_z(p, h, order, k)[1]().wait_recv()
            elif before is not None:
                gather_plain(p, h, order, before)[1]().wait_recv()
            if step == len(steps):
                return
            if steps[step] == "z":
                along_z(lambda k: gather_z(p, h, order, k)[0]().start())
            elif steps[step] == "relay":

                @pl.when(inner)
                def _():
                    gather_relay(p, h, order)().start()

            else:
                gather_plain(p, h, order, steps[step])[0]().start()

        each_part(p, action)

    def gather_sent(p):
        def action(h, order):
            along_z(lambda k: gather_z(p, h, order, k)[0]().wait_send())

            @pl.when(inner)
            def _():
                gather_relay(p, h, order)().wait_send()

            for axis in ("x", "y"):
                gather_plain(p, h, order, axis)[0]().wait_send()

        each_part(p, action)

    def pack(p):
        load_pair(p).wait()
        slot = p % WSLOTS
        both = jnp.concatenate([WF[slot, 0].astype(BF16), WF[slot, 1].astype(BF16)], axis=1)
        G[p, y, z, x] = both.reshape(PARTS, PART, WIDE)

        @pl.when(p + WSLOTS < PAIRS)
        def _():
            load_pair(p + WSLOTS).start()

    half = TM * c
    BKh = BK.at[pl.ds(pl.multiple_of(half, TM), TM)]
    GRh = GR.at[pl.ds(pl.multiple_of(half, TM), TM)]
    other = TM * (1 - c)
    BKo = BK.at[pl.ds(pl.multiple_of(other, TM), TM)]
    GRo = GR.at[pl.ds(pl.multiple_of(other, TM), TM)]
    patch_out = remote(patch, BKh, in_s.at[0], in_r.at[0], dev_core)
    patch_in = remote(patch, BKo, in_s.at[0], in_r.at[0], dev_core)
    cot_out = remote(cot, GRh, in_s.at[1], in_r.at[1], dev_core)
    cot_in = remote(cot, GRo, in_s.at[1], in_r.at[1], dev_core)
    patch_own = pltpu.make_async_copy(patch, BKh, lc_s.at[0])
    cot_own = pltpu.make_async_copy(cot, GRh, lc_s.at[1])
    patch_own.start()
    cot_own.start()
    GPIECE[z, x] = jnp.zeros((8, 128), F32)
    GPIECE[z, x, 0:5, 0:ROWS] = small[...].astype(BF16).astype(F32)
    gain_z = [
        (
            remote(GPIECE.at[z, x], GPIECE.at[z, x], gn_s.at[k - 1], gn_r.at[k - 1], dev_z(k)),
            remote(GPIECE.at[z_from(k), x], GPIECE.at[z_from(k), x], gn_s.at[k - 1], gn_r.at[k - 1], dev_z(k)),
        )
        for k in range(1, NZ)
    ]
    gain_x = (
        remote(GPIECE.at[:, x], GPIECE.at[:, x], gn_s.at[3], gn_r.at[3], dev_x),
        remote(GPIECE.at[:, 1 - x], GPIECE.at[:, 1 - x], gn_s.at[3], gn_r.at[3], dev_x),
    )
    loop(BEGUN, pack)
    pl.semaphore_wait(barrier, len(greeted))
    for s, _ in gain_z:
        s.start()
    patch_out.start()
    loop(BEGUN, lambda p: gather_issue(p, 0))
    cot_out.start()

    def gains_across(l, yy):
        index_row = mask_index[pl.ds(y, 1), :]
        count = mask_count[y]
        spot = lax.broadcasted_iota(jnp.int32, (SEQ, index_row.shape[1]), 0)
        live = lax.broadcasted_iota(jnp.int32, (1, index_row.shape[1]), 1) < count
        hits = jnp.where(jnp.logical_and(spot == index_row, live), 1.0, 0.0)
        FL[...] = jnp.max(hits, axis=1, keepdims=True)
        for _, r in gain_z:
            r.wait_recv()
        gain_x[0].start()

    def first_rows(l, yy):
        gain_x[1].wait_recv()
        lane = lax.broadcasted_iota(jnp.int32, (128, D), 0)
        feature = lax.broadcasted_iota(jnp.int32, (128, D), 1)
        gains = jnp.zeros((8, D), F32)
        for zz in range(NZ):
            for xx in range(NX):
                place = jnp.logical_and(feature - ROWS * (zz * NX + xx) == lane, lane < ROWS)
                gains = gains + mm(GPIECE[zz, xx].astype(BF16), jnp.where(place, 1.0, 0.0).astype(BF16))
        GAIN[...] = gains
        patch_own.wait()
        patch_in.wait_recv()
        embed = GAIN[4:5, :]

        def mask_tile(i):
            rows = rows_at(i, TR)
            flag = FL[rows, :]
            S[0, rows, :] = BK[rows, :].astype(F32) * (1.0 - flag) + flag * embed

        loop(SEQ // TR, mask_tile)

    def norm_parts(values):
        centre = values - jnp.mean(values, axis=-1, keepdims=True)
        spread = jnp.mean(centre * centre, axis=-1, keepdims=True)
        return centre, lax.rsqrt(spread + EPS_NORM)

    def norm_into(dst, src, gain_row):
        gain = GAIN[pl.ds(gain_row, 1), :]

        def tile(i):
            rows = rows_at(i, TR)
            centre, inv = norm_parts(src[rows, :])
            dst[rows, :] = (centre * inv * gain).astype(BF16)

        loop(SEQ // TR, tile)

    def matrix(p, yy):
        return G[p, yy].reshape(D, WIDE)

    def exchange_copy(e, i):
        rows = rows_at(i, TM)
        return remote(XS.at[rows], XR.at[e, rows], ex_s.at[i], ex_r.at[e, i], dev_core)

    def give(e, value):
        XS[...] = value.astype(BF16)
        loop(SEQ // TM, lambda i: exchange_copy(e, i).start())

    def receive(e, take):
        def chunk(i):
            exchange_copy(e, i).wait_recv()

            def tile(j):
                rows = pl.ds(pl.multiple_of(i * TM + j * TR, TR), TR)
                take(rows, XS[rows, :].astype(F32) + XR[e, rows, :].astype(F32))

            loop(TM // TR, tile)

        loop(SEQ // TM, chunk)
        loop(SEQ // TM, lambda i: exchange_copy(e, i).wait_send())

    def attend(l, yy):
        def tile(i):
            rows = rows_at(i, TM)
            outs = []
            for hd in range(HEADS_Y):
                lo = hd * HD
                q = QK[l, yy, rows, lo : lo + HD]
                k = QK[l, yy, :, COL + lo : COL + lo + HD]
                v = V[l, yy, :, lo : lo + HD]
                s = mm_nt(q, k) * SCALE
                e = jnp.exp(s - jnp.max(s, axis=1, keepdims=True))
                probs = e * (1.0 / jnp.sum(e, axis=1, keepdims=True))
                outs.append(mm(probs.astype(BF16), v))
            MIX[l, yy, rows, :] = jnp.concatenate(outs, axis=1).astype(BF16)

        loop(SEQ // TM, tile)

    def attend_back(l, yy, hd):
        lo = hd * HD
        k = QK[l, yy, :, COL + lo : COL + lo + HD]
        v = V[l, yy, :, lo : lo + HD]

        def tile(i, carry):
            dk, dv = carry
            rows = rows_at(i, TM)
            q = QK[l, yy, rows, lo : lo + HD]
            dm = GM[yy, rows, lo : lo + HD]
            s = mm_nt(k, q) * SCALE
            e = jnp.exp(s - jnp.max(s, axis=0, keepdims=True))
            probs = e * (1.0 / jnp.sum(e, axis=0, keepdims=True))
            dp = mm_nt(v, dm)
            ds = probs * (dp - jnp.sum(probs * dp, axis=0, keepdims=True))
            ds = ds.astype(BF16)
            dv = dv + mm(probs.astype(BF16), dm)
            dk = dk + mm(ds, q)
            dq = mm_tn(ds, k) * SCALE
            DQK[yy, rows, lo : lo + HD] = dq.astype(BF16)
            return dk, dv

        zero = jnp.zeros((SEQ, HD), F32)
        dk, dv = lax.fori_loop(0, SEQ // TM, tile, (zero, zero))
        DQK[yy, :, COL + lo : COL + lo + HD] = (dk * SCALE).astype(BF16)
        DV[yy, :, lo : lo + HD] = dv.astype(BF16)

    def up_part(l, u, yy, p):
        ACC[:, 0:WIDE] = mm(NRM2[l], matrix(p, yy))

        def gelu(i):
            rows = rows_at(i, TR)
            v = ACC[rows, 0:WIDE]
            cdf = 0.5 * (1.0 + lax.erf(v * (2.0 ** -0.5)))
            HID[l, u, yy, rows, :] = (v * cdf).astype(BF16)
            pdf = jnp.exp(-0.5 * v * v) * 0.3989422804014327
            GP[l, u, yy, rows, :] = (cdf + v * pdf).astype(BF16)

        loop(SEQ // TR, gelu)

    def ln_one(l, yy):
        norm_into(NRM.at[l], S.at[l], 2 * l)

    def project_qk(l, yy):
        def one(side):
            QK[l, side] = mm(NRM[l], matrix(l * PER, side)).astype(BF16)

        loop(2, one)

    def project_v(l, yy):
        def one(side):
            V[l, side] = mm(NRM[l], matrix(l * PER + 1, side)[:, :COL]).astype(BF16)

        loop(2, one)

    def attn_out(l, yy):
        p = l * PER + 1
        total = mm_nt(MIX[l, 0], matrix(p, 0)[:, COL:])
        give(0, total + mm_nt(MIX[l, 1], matrix(p, 1)[:, COL:]))

    def attn_resid(l, yy):
        def take(rows, total):
            R1[l, rows, :] = S[l, rows, :] + total

        receive(0, take)
        norm_into(NRM2.at[l], R1.at[l], 2 * l + 1)

    def up(l, u):
        loop(2, lambda side: up_part(l, u, side, l * PER + 2 + u))

    def down_one(l, yy):
        p = l * PER + 4
        ACC[...] = mm_nt(HID[l, 0, 0], matrix(p, 0)) + mm_nt(HID[l, 0, 1], matrix(p, 1))

    def down_two(l, yy):
        p = l * PER + 5
        total = ACC[...] + mm_nt(HID[l, 1, 0], matrix(p, 0))
        give(1, total + mm_nt(HID[l, 1, 1], matrix(p, 1)))

    def layer_end(l, yy):
        def take(rows, total):
            value = R1[l, rows, :] + total

            @pl.when(l == 0)
            def _():
                S[1, rows, :] = value

            @pl.when(l == 1)
            def _():
                ACC[rows, :] = value

        receive(1, take)

        @pl.when(l == 1)
        def _():
            block_copy.start()

    block_copy = pltpu.make_async_copy(ACC.at[pl.ds(pl.multiple_of(half, TM), TM)], out_block, lc_s.at[2])

    def scatter_plain(p, h, order, axis):
        slot, dev, there = along(axis)
        place = order.index(axis)
        have = {q: (own[q] if q in order[:place] else ALL) for q in own}
        if place == 0:
            dst = (RB0Y if axis == "y" else RB0X).at[p if h > 0 else PAIRS + p // 2]
        else:
            dst = RB1.at[first_slot(p, h)] if z_last(order) else RB2X.at[p - EARLY, h - 1]
        send, recv = ag_s.at[p, h, slot], ag_r.at[late(p), h, slot]
        src = block(p, h, {**have, axis: there})
        return lazy(src, dst, send, recv, dev), lazy(dst, dst, send, recv, dev), dst

    def z_last(order):
        return order[2] == "z"

    def first_slot(p, h):
        return p if h == 0 else PAIRS + EARLY * (h - 1) + p

    def late(p):
        return (p + PER) % PAIRS

    def scatter_have(order):
        return {q: (own[q] if q in order[: order.index("z")] else ALL) for q in own}

    def scatter_z(p, h, order, k):
        dst = RB2.at[first_slot(p, h), k - 1] if z_last(order) else RBZ.at[p - EARLY, h - 1, k - 1]
        send, recv = ag_s.at[p, h, k - 1], ag_r.at[late(p), h, k - 1]
        src = block(p, h, {**scatter_have(order), "z": z_to(k)})
        return lazy(src, dst, send, recv, dev_z(k)), lazy(dst, dst, send, recv, dev_z(k)), dst

    def scatter_merge(p, h, order):
        dst = RBM.at[first_slot(p, h)] if z_last(order) else RBMZ.at[p - EARLY, h - 1]
        dev = ((1 + z // far) * NX + x, narrow)
        send, recv = ag_s.at[p, h, 5], ag_r.at[late(p), h, 5]
        src = block(p, h, {**scatter_have(order), "z": far - z})
        return lazy(src, dst, send, recv, dev), lazy(dst, dst, send, recv, dev), dst

    def scatter_steps(order):
        at = order.index("z")
        return order[:at] + ("merge",) + order[at:]

    def scatter_issue(p, step):
        def action(h, forward_order):
            order = forward_order[::-1]
            steps = scatter_steps(order)
            before = steps[step - 1] if step > 0 else None
            if before is not None and before != "merge":
                have = {q: (own[q] if q in order[: order.index(before) + 1] else ALL) for q in own}
                view = block(p, h, have)
                if before == "z":
                    scatter_z(p, h, order, 2)[1]().wait_recv()

                    @pl.when(z != 0)
                    def _():
                        scatter_z(p, h, order, 1)[1]().wait_recv()

                    @pl.when(z != far)
                    def _():
                        scatter_z(p, h, order, 3)[1]().wait_recv()

                    total = view[...].astype(F32) + scatter_z(p, h, order, 2)[2][...].astype(F32)
                    for k, there in ((1, z != 0), (3, z != far)):
                        total = total + jnp.where(there, scatter_z(p, h, order, k)[2][...].astype(F32), 0.0)
                else:
                    scatter_plain(p, h, order, before)[1]().wait_recv()
                    total = view[...].astype(F32) + scatter_plain(p, h, order, before)[2][...].astype(F32)
                if step < len(steps):
                    view[...] = total.astype(BF16)
                else:
                    out_grad[p, h] = total
                    NB[...] += fold(total * total)
            if step == len(steps):
                return
            if steps[step] == "merge":

                @pl.when(outer)
                def _():
                    scatter_merge(p, h, order)[0]().start()

            elif steps[step] == "z":

                @pl.when(inner)
                def _():
                    scatter_merge(p, h, order)[1]().wait_recv()
                    view = block(p, h, {**scatter_have(order), "z": z_to(2)})
                    term = scatter_merge(p, h, order)[2][...].astype(F32)
                    view[...] = (view[...].astype(F32) + term).astype(BF16)

                along_z(lambda k: scatter_z(p, h, order, k)[0]().start())
            else:
                scatter_plain(p, h, order, steps[step])[0]().start()

        each_part(p, action)

    def fold(sq):
        sq = jnp.sum(sq.reshape(PART // 8, 8, WIDE), axis=0)
        return sq[:, 0:128] + sq[:, 128:256] + sq[:, 256:384]

    def scatter_sent(p):
        def action(h, forward_order):
            order = forward_order[::-1]
            for axis in ("x", "y"):
                scatter_plain(p, h, order, axis)[0]().wait_send()

            @pl.when(outer)
            def _():
                scatter_merge(p, h, order)[0]().wait_send()

            along_z(lambda k: scatter_z(p, h, order, k)[0]().wait_send())

        each_part(p, action)

    NB[...] = jnp.zeros((8, 128), F32)
    SG[...] = jnp.zeros_like(SG)

    def transpose_into(dst, src):
        def tile(i):
            rows = rows_at(i, 128)
            dst[:, rows] = jnp.transpose(src[rows, :])

        loop(SEQ // 128, tile)

    def put_grad(p, yy, left, right):
        G[p, yy] = mm(left[...], right).astype(BF16).reshape(NZ, NX, PARTS, PART, WIDE)

    def norm_back(e, src, gain_row):
        gain = GAIN[pl.ds(gain_row, 1), :]
        def take(rows, dn):
            centre, inv = norm_parts(src[rows, :])
            xhat = centre * inv
            dh = dn * gain
            dv = inv * (
                dh
                - jnp.mean(dh, axis=-1, keepdims=True)
                - xhat * jnp.mean(dh * xhat, axis=-1, keepdims=True)
            )
            GR[rows, :] += dv
            SG[pl.ds(gain_row, 1), :] += jnp.sum(dn * xhat, axis=0, keepdims=True)

        receive(e, take)

    def cast_rows(dst, src):
        def tile(i):
            rows = rows_at(i, TR)
            dst[rows, :] = src[rows, :].astype(BF16)

        loop(SEQ // TR, tile)

    def both(action):
        loop(2, action)

    def back_prepare(l, yy):
        @pl.when(l == 1)
        def _():
            cot_own.wait()
            cot_in.wait_recv()
            cot_out.wait_send()

        cast_rows(BK, GR)
        transpose_into(TA, BK)
        transpose_into(TB, NRM2.at[l])

    def back_down(l, u, side):
        p = l * PER + 4 + u

        @pl.when(side == 0)
        def _():
            gather_sent(p)

        gh = mm(BK[...], matrix(p, side))
        GU[u, side] = (gh * GP[l, u, side].astype(F32)).astype(BF16)
        put_grad(p, side, TA, HID[l, u, side])

    def back_up_sum(l, yy):
        p = l * PER + 2

        @pl.when(l == 1)
        def _():
            block_copy.wait()

        ACC[...] = mm_nt(GU[0, 0], matrix(p, 0)) + mm_nt(GU[0, 1], matrix(p, 1))

    def back_up_give(l, yy):
        p = l * PER + 3
        total = ACC[...] + mm_nt(GU[1, 0], matrix(p, 0))
        give(0, total + mm_nt(GU[1, 1], matrix(p, 1)))

    def back_up(l, u):
        p = l * PER + 2 + u
        gather_sent(p)
        both(lambda side: put_grad(p, side, TB, GU[u, side]))

    def back_norm_two(l, yy):
        norm_back(0, R1.at[l], 2 * l + 1)

    def back_attn_prepare(l, yy):
        cast_rows(BK, GR)
        transpose_into(TA, BK)
        transpose_into(TB, NRM.at[l])

        def grad_mix(side):
            GM[side] = mm(BK[...], matrix(l * PER + 1, side)[:, COL:]).astype(BF16)

        both(grad_mix)

    def back_attn_grads(l, yy):
        p = l * PER + 1
        gather_sent(p)
        ACC[...] = mm_nt(DV[0], matrix(p, 0)[:, :COL]) + mm_nt(DV[1], matrix(p, 1)[:, :COL])

        def grads(side):
            gv = mm(TB[...], DV[side])
            go = mm(TA[...], MIX[l, side])
            pair = jnp.concatenate([gv, go], axis=1).astype(BF16)
            G[p, side] = pair.reshape(NZ, NX, PARTS, PART, WIDE)

        both(grads)

    def back_qk_give(l, yy):
        p = l * PER
        total = ACC[...] + mm_nt(DQK[0], matrix(p, 0))
        give(1, total + mm_nt(DQK[1], matrix(p, 1)))

    def back_qk(l, yy):
        p = l * PER
        gather_sent(p)
        both(lambda side: put_grad(p, side, TB, DQK[side]))

    def back_norm_one(l, yy):
        norm_back(1, S.at[l], 2 * l)

    def position(i):
        s = i % PER
        slot = jnp.where(s < 2, s + 4, jnp.where(s < 4, s, 5 - s))
        return (LAYERS - 1 - i // PER) * PER + slot

    def scatter_at(t, phase):
        scatter_issue(position(t), phase)

    igrad_copy = pltpu.make_async_copy(GRh, out_igrad, lc_s.at[3])
    place = 2 * y + x
    around = ((2 * y + 1 - x, dev_x), (2 * (1 - y) + x, dev_y), (2 * (1 - y) + 1 - x, dev_xy))

    def small_z(k):
        got = SR.at[z_from(k), 0]
        return (
            remote(SR.at[z, 0], SR.at[z, 0], fs_s.at[k - 1], fs_r.at[k - 1], dev_z(k)),
            remote(got, got, fs_s.at[k - 1], fs_r.at[k - 1], dev_z(k)),
        )

    def small_xy(k):
        there, dev = around[k]
        return (
            remote(SR.at[place, 1], SR.at[place, 1], fs_s.at[3 + k], fs_r.at[3 + k], dev),
            remote(SR.at[there, 1], SR.at[there, 1], fs_s.at[3 + k], fs_r.at[3 + k], dev),
        )

    def rows_done():
        def finish_tile(i):
            rows = rows_at(i, TR)
            flag = FL[rows, :]
            value = GR[rows, :]
            SG[4:5, :] += jnp.sum(value * flag, axis=0, keepdims=True)
            GR[rows, :] = value * (1.0 - flag)

        loop(SEQ // TR, finish_tile)
        igrad_copy.start()
        SR[z, 0] = SG[...]
        for k in range(1, NZ):
            small_z(k)[0].start()

    def small_sums():
        for k in range(1, NZ):
            small_z(k)[1].wait_recv()
        SR[place, 1] = SR[0, 0] + SR[1, 0] + SR[2, 0] + SR[3, 0]
        for k in range(3):
            small_xy(k)[0].start()

    pieces = {
        "g1": gains_across,
        "g2": first_rows,
        "ln1": ln_one,
        "qk": project_qk,
        "v": project_v,
        "at": attend,
        "out": attn_out,
        "res": attn_resid,
        "up": up,
        "dn0": down_one,
        "dn1": down_two,
        "fin": layer_end,
        "b4p": back_prepare,
        "b4": lambda l, side: back_down(l, 0, side),
        "b5": lambda l, side: back_down(l, 1, side),
        "b2a": back_up_sum,
        "b2b": lambda l, yy: back_up(l, 0),
        "b3a": back_up_give,
        "b3b": lambda l, yy: back_up(l, 1),
        "b3c": back_norm_two,
        "b1p": back_attn_prepare,
        "ab0": lambda l, side: attend_back(l, side, 0),
        "ab1": lambda l, side: attend_back(l, side, 1),
        "ab2": lambda l, side: attend_back(l, side, 2),
        "b1f": back_attn_grads,
        "b0a": back_qk_give,
        "b0b": back_qk,
        "b0c": back_norm_one,
        "rows": lambda l, yy: rows_done(),
        "small": lambda l, yy: small_sums(),
    }
    def digit(word, k, base):
        return lax.rem(lax.div(word, base**k), base)

    def plan_of(m, low, high):
        if high - low == 1:
            return tuple(jnp.int32(words[low]) for words in PLAN_WORDS)
        middle = (low + high) // 2
        return lax.cond(m < middle, lambda: plan_of(m, low, middle), lambda: plan_of(m, middle, high))

    def micro(m, firsts):
        counts, word = plan_of(m, 0, STEPS)
        count = tuple(digit(counts, kind, 8) for kind in range(10))

        @pl.when(counts > 0)
        def _():
            for kind in range(10):
                action = gather_issue if kind < 5 else scatter_at

                @pl.when(count[kind] > 0)
                def _():
                    def one(i, carry):
                        if kind == 0:
                            pack(firsts[kind] + i)
                        action(firsts[kind] + i, kind % 5)
                        return carry

                    lax.fori_loop(0, count[kind], one, 0)


        @pl.when(word > 0)
        def _():
            what, l, yy = lax.rem(word, 32), digit(lax.div(word, 32), 0, 2), lax.div(word, 64)
            for i, action in enumerate(pieces.values()):

                @pl.when(what == i + 1)
                def _():
                    action(l, yy)

        return tuple(f + n for f, n in zip(firsts, count))

    lax.fori_loop(0, STEPS, micro, (jnp.int32(BEGUN),) + (jnp.int32(0),) * 9)

    own_square = jnp.sum(jnp.sum(NB[...], axis=1, keepdims=True), axis=0, keepdims=True)
    NZC[z, c] = jnp.broadcast_to(own_square, (8, 128))
    nm_z = []
    for j, (zz, cc, frm, dev) in enumerate(
        [(z, 1 - c, z, dev_core)]
        + [(z_to(k), c, z_from(k), dev_z(k)) for k in range(1, NZ)]
        + [(z_to(k), 1 - c, z_from(k), dev_zc(k)) for k in range(1, NZ)]
    ):
        got = NZC.at[frm, cc]
        nm_z.append(
            (
                remote(NZC.at[z, c], NZC.at[z, c], nm_s.at[j], nm_r.at[j], dev),
                remote(got, got, nm_s.at[j], nm_r.at[j], dev),
            )
        )
    for s, _ in nm_z:
        s.start()
    for k in range(3):
        small_xy(k)[1].wait_recv()
    total_small = SR[0, 1] + SR[1, 1] + SR[2, 1] + SR[3, 1]
    out_small[...] = total_small
    small_square = jnp.sum(jnp.sum(total_small * total_small, axis=1, keepdims=True), axis=0, keepdims=True)
    for _, r in nm_z:
        r.wait_recv()
    square = NZC[0, 0] + NZC[0, 1]
    for zz in range(1, NZ):
        square = square + (NZC[zz, 0] + NZC[zz, 1])
    NXY[place] = square
    nm_xy = [
        (
            remote(NXY.at[place], NXY.at[place], nm_s.at[7 + k], nm_r.at[7 + k], dev),
            remote(NXY.at[there], NXY.at[there], nm_s.at[7 + k], nm_r.at[7 + k], dev),
        )
        for k, (there, dev) in enumerate(around)
    ]
    for s, _ in nm_xy:
        s.start()
    for _, r in nm_xy:
        r.wait_recv()
    out_norm[...] = jnp.sqrt(NXY[0] + NXY[1] + NXY[2] + NXY[3] + small_square)

    for s, _ in [small_z(k) for k in range(1, NZ)] + [small_xy(k) for k in range(3)] + nm_z + nm_xy + gain_z:
        s.wait_send()
    gain_x[0].wait_send()
    patch_out.wait_send()
    loop(PAIRS, scatter_sent)
    igrad_copy.wait()


def big_step(weights, patches, cotangent, mask_index, mask_count, small):
    vm = pl.BlockSpec(memory_space=pltpu.VMEM)
    hb = pl.BlockSpec(memory_space=pl.ANY)
    sm = pl.BlockSpec(memory_space=pltpu.SMEM)
    dma = pltpu.SemaphoreType.DMA
    V = pltpu.VMEM
    scratch = [
        V((PAIRS, 2, NZ, NX, PARTS, PART, WIDE), BF16),
        V((WSLOTS, 2, ROWS, COL), F32),
        V((2, SEQ, D), F32),
        V((2, SEQ, D), F32),
        V((2, SEQ, D), BF16),
        V((2, SEQ, D), BF16),
        V((2, 2, SEQ, WIDE), BF16),
        V((2, 2, SEQ, COL), BF16),
        V((2, 2, SEQ, COL), BF16),
        V((2, 2, 2, SEQ, WIDE), BF16),
        V((2, 2, 2, SEQ, WIDE), BF16),
        V((SEQ, D), F32),
        V((SEQ, D), F32),
        V((SEQ, D), BF16),
        V((2, SEQ, D), BF16),
        V((SEQ, D), BF16),
        V((D, SEQ), BF16),
        V((D, SEQ), BF16),
        V((2, 2, SEQ, WIDE), BF16),
        V((2, SEQ, COL), BF16),
        V((2, SEQ, WIDE), BF16),
        V((2, SEQ, COL), BF16),
        V((SEQ, 1), F32),
        V((8, D), F32),
        V((NZ, NX, 8, 128), F32),
        V((8, D), F32),
        V((4, 2, 8, D), F32),
        V((8, 128), F32),
        V((NZ, 2, 8, 128), F32),
        V((4, 8, 128), F32),
        V((PAIRS + PAIRS // 2, NZ, NX, PART, WIDE), BF16),
        V((PAIRS + PAIRS // 2, 2, NZ, PART, WIDE), BF16),
        V((PAIRS + 2 * EARLY, NZ, PART, WIDE), BF16),
        V((PAIRS + 2 * EARLY, NZ - 1, PART, WIDE), BF16),
        V((PAIRS - EARLY, 2, PART, WIDE), BF16),
        V((PAIRS - EARLY, 2, NZ - 1, 2, PART, WIDE), BF16),
        V((PAIRS + 2 * EARLY, PART, WIDE), BF16),
        V((PAIRS - EARLY, 2, 2, PART, WIDE), BF16),
        dma((WSLOTS,)),
        dma((PAIRS, PARTS, 6)), dma((PAIRS, PARTS, 6)),
        dma((2,)), dma((2, 2)),
        dma((2,)), dma((2,)), dma((4,)),
        dma((4,)), dma((4,)),
        dma((6,)), dma((6,)),
        dma((10,)), dma((10,)),
    ]
    return pl.pallas_call(
        step_kernel,
        out_shape=(
            jax.ShapeDtypeStruct((TM, D), F32),
            jax.ShapeDtypeStruct((TM, D), F32),
            jax.ShapeDtypeStruct((PAIRS, PARTS, PART, WIDE), F32),
            jax.ShapeDtypeStruct((8, D), F32),
            jax.ShapeDtypeStruct((8, 128), F32),
        ),
        in_specs=[hb, hb, hb, vm, sm, vm],
        out_specs=(hb, hb, vm, vm, vm),
        scratch_shapes=scratch,
        compiler_params=pltpu.CompilerParams(
            collective_id=0, has_side_effects=True, vmem_limit_bytes=62 << 20
        ),
        name="train_step",
    )(weights, patches, cotangent, mask_index, mask_count, small)


def adam_values(weight_in, moment_one, moment_two, gradient, step_rate, decay_rate):
    moment_one = BETA_ONE * moment_one + (1.0 - BETA_ONE) * gradient
    moment_two = BETA_TWO * moment_two + (1.0 - BETA_TWO) * gradient * gradient
    first_hat = moment_one / (1.0 - BETA_ONE**STEP)
    second_hat = moment_two / (1.0 - BETA_TWO**STEP)
    updated = weight_in - step_rate * (
        first_hat / (jnp.sqrt(second_hat) + EPS_ADAM) + decay_rate * weight_in
    )
    return (updated, moment_one, moment_two)


def adam_kernel(
    norm, grad, small_total, small, small_one, small_two, block, igrad, w, m, v,
    nw, nm, nv, ns, nsm, nsv, grad_norm, block_out, igrad_out,
):
    factor = jnp.minimum(1.0, CLIP_MAX / norm[0:1, 0:1])
    for i in range(PAIRS // ADAM_STEPS):
        g = grad[i].reshape(ROWS, WIDE) * factor
        for j in range(2):
            k = 2 * i + j
            nw[k], nm[k], nv[k] = adam_values(
                w[k], m[k], v[k], g[:, j * COL : (j + 1) * COL], D ** (-0.5), DECAY_RATE
            )
    block_out[...] = block[...]
    igrad_out[...] = igrad[...]

    @pl.when(pl.program_id(0) == 0)
    def _():
        first = ROWS * lax.axis_index("wide")
        row = lax.broadcasted_iota(jnp.int32, (D, ROWS), 0)
        column = lax.broadcasted_iota(jnp.int32, (D, ROWS), 1)
        pick = jnp.where(row == column + first, 1.0, 0.0)
        own = lax.dot_general(
            small_total[...], pick, (((1,), (0,)), ((), ())),
            precision=lax.Precision.HIGHEST, preferred_element_type=F32,
        )[0:5]
        ns[...], nsm[...], nsv[...] = adam_values(
            small[...], small_one[...], small_two[...], own * factor, RATE_SMALL, 0.0
        )
        grad_norm[...] = norm[0:1, 0:1]


def adam_all(norm, grad, small_total, smalls, rows, matrices):
    shape = matrices[0].shape
    flat = (LAYERS * 12, ROWS, COL)
    blk = pl.BlockSpec((2 * PAIRS // ADAM_STEPS, ROWS, COL), lambda i: (i, 0, 0))
    row_blk = pl.BlockSpec((TM // ADAM_STEPS, D), lambda i: (i, 0))

    def whole(*dims):
        return pl.BlockSpec(dims, lambda i: (0,) * len(dims))

    outs = pl.pallas_call(
        adam_kernel,
        grid=(ADAM_STEPS,),
        out_shape=(
            *(jax.ShapeDtypeStruct(flat, F32) for _ in range(3)),
            *(jax.ShapeDtypeStruct((5, ROWS), F32) for _ in range(3)),
            jax.ShapeDtypeStruct((1, 1), F32),
            *(jax.ShapeDtypeStruct((TM, D), F32) for _ in range(2)),
        ),
        in_specs=[
            whole(8, 128),
            pl.BlockSpec((PAIRS // ADAM_STEPS, PARTS, PART, WIDE), lambda i: (i, 0, 0, 0)),
            whole(8, D),
            *(whole(5, ROWS) for _ in range(3)),
            row_blk, row_blk,
            blk, blk, blk,
        ],
        out_specs=(
            blk, blk, blk, *(whole(5, ROWS) for _ in range(3)), whole(1, 1), row_blk, row_blk,
        ),
        compiler_params=pltpu.CompilerParams(vmem_limit_bytes=62 << 20),
        name="adam",
    )(norm, grad, small_total, *smalls, *rows, *(a.reshape(flat) for a in matrices))
    return tuple(o.reshape(shape) for o in outs[:3]), outs[3:6], outs[6].reshape(()), outs[7:]


def shards(patches, cotangent, mask_index, mask_count, weights, first_moment, second_moment,
           small_params, small_first, small_second):
    block_output, input_grad, grad_own, small_total, norm = big_step(
        weights.reshape(LAYERS * 12, ROWS, COL), patches, cotangent, mask_index, mask_count, small_params
    )
    new_matrices, new_smalls, grad_norm, rows = adam_all(
        norm, grad_own, small_total, (small_params, small_first, small_second),
        (block_output, input_grad), (weights, first_moment, second_moment),
    )
    return (*rows, *new_matrices, *new_smalls, grad_norm)


def layer_norm(values, gain):
    centre = values - jnp.mean(values, axis=-1, keepdims=True)
    spread = jnp.mean(centre * centre, axis=-1, keepdims=True)
    return centre * lax.rsqrt(spread + EPS_NORM) * gain


def exact_gelu(values):
    return jax.nn.gelu(values, approximate=False)


def gather_rows(share):
    return lax.all_gather(share, "narrow", axis=0, tiled=True)


def gather_grads(share):
    return lax.all_gather(share, "narrow", axis=0, tiled=True)


def branch_total(term, row_count):
    return lax.psum_scatter(
        term(jnp.int32(0), row_count * lax.axis_size("narrow")).astype(jnp.bfloat16),
        "narrow",
        scatter_dimension=0,
        tiled=True,
    ).astype(jnp.float32)


def input_total(term, row_count):
    return lax.psum_scatter(
        term(jnp.int32(0), row_count * lax.axis_size("narrow")).astype(jnp.bfloat16),
        "narrow",
        scatter_dimension=0,
        tiled=True,
    ).astype(jnp.float32)


def heads_of(values, clip_count):
    return values.reshape(clip_count, SEQ, values.shape[1] // HD, HD)


def attend_clip(parts):
    queries, key_rows, value_rows = parts
    scores = jnp.einsum(
        "qhd,khd->hqk", queries, key_rows, preferred_element_type=jnp.float32
    ) * HD ** (-0.5)
    probs = jax.nn.softmax(scores, axis=-1)
    return jnp.einsum(
        "hqk,khd->qhd", probs.astype(jnp.bfloat16), value_rows, preferred_element_type=jnp.float32
    ).astype(jnp.bfloat16)


def attend_back_clip(parts):
    queries, key_rows, value_rows, grad_mix = parts
    scale = HD ** (-0.5)
    scores = (
        jnp.einsum("qhd,khd->hqk", queries, key_rows, preferred_element_type=jnp.float32) * scale
    )
    probs = jax.nn.softmax(scores, axis=-1)
    grad_values = jnp.einsum(
        "hqk,qhd->khd", probs.astype(jnp.bfloat16), grad_mix, preferred_element_type=jnp.float32
    ).astype(jnp.bfloat16)
    grad_probs = jnp.einsum(
        "qhd,khd->hqk", grad_mix, value_rows, preferred_element_type=jnp.float32
    )
    grad_scores = probs * (grad_probs - jnp.sum(probs * grad_probs, axis=-1, keepdims=True))
    grad_scores = grad_scores.astype(jnp.bfloat16)
    grad_queries = (
        jnp.einsum("hqk,khd->qhd", grad_scores, key_rows, preferred_element_type=jnp.float32)
        * scale
    ).astype(jnp.bfloat16)
    grad_keys = (
        jnp.einsum("hqk,qhd->khd", grad_scores, queries, preferred_element_type=jnp.float32) * scale
    ).astype(jnp.bfloat16)
    return (grad_queries, grad_keys, grad_values)


def forward_layer(stream, weight, gain_one, gain_two):
    row_count = stream.shape[0]
    normed = gather_rows(layer_norm(stream, gain_one).astype(jnp.bfloat16))
    all_rows = normed.shape[0]
    clip_count = all_rows // SEQ
    project = jnp.einsum(
        "rd,sde->sre", normed, weight[0:3], preferred_element_type=jnp.float32
    ).astype(jnp.bfloat16)
    mixture = lax.map(
        attend_clip,
        (
            heads_of(project[0], clip_count),
            heads_of(project[1], clip_count),
            heads_of(project[2], clip_count),
        ),
    )
    mixture = mixture.reshape(all_rows, -1)

    def attn_term(first_row, row_num):
        return lax.dot_general(
            mixture, weight[3], (((1,), (1,)), ((), ())), preferred_element_type=jnp.float32
        )

    resid_one = stream + branch_total(attn_term, row_count)
    normed_two = gather_rows(layer_norm(resid_one, gain_two).astype(jnp.bfloat16))
    upward = jnp.einsum("rd,jde->jre", normed_two, weight[4:8], preferred_element_type=jnp.float32)
    hidden = exact_gelu(upward).astype(jnp.bfloat16)

    def mlp_term(first_row, row_num):
        return jnp.einsum("jre,jde->rd", hidden, weight[8:12], preferred_element_type=jnp.float32)

    result = resid_one + branch_total(mlp_term, row_count)
    return (result, (stream, normed, project, mixture, resid_one, normed_two, upward, hidden))


def backward_layer(grad_out, saved, weight, gain_one, gain_two):
    stream, normed, project, mixture, resid_one, normed_two, upward, hidden = saved
    row_count = stream.shape[0]
    all_rows = normed.shape[0]
    clip_count = all_rows // SEQ
    back_mlp = gather_grads(grad_out.astype(jnp.bfloat16))
    grad_down = jnp.einsum("rd,jre->jde", back_mlp, hidden, preferred_element_type=jnp.float32)
    grad_hidden = jnp.einsum(
        "rd,jde->jre", back_mlp, weight[8:12], preferred_element_type=jnp.float32
    )
    gelu_out, gelu_back = jax.vjp(exact_gelu, upward)
    grad_upward = gelu_back(grad_hidden)[0].astype(jnp.bfloat16)
    grad_up = jnp.einsum("rd,jre->jde", normed_two, grad_upward, preferred_element_type=jnp.float32)

    def up_term(first_row, row_num):
        return jnp.einsum(
            "jre,jde->rd", grad_upward, weight[4:8], preferred_element_type=jnp.float32
        )

    grad_normed_two = input_total(up_term, row_count)
    norm_out, norm_back = jax.vjp(layer_norm, resid_one, gain_two)
    part_stream, grad_gain_two = norm_back(grad_normed_two)
    grad_resid = grad_out + part_stream
    back_attn = gather_grads(grad_resid.astype(jnp.bfloat16))
    grad_out_proj = lax.dot_general(
        back_attn, mixture, (((0,), (0,)), ((), ())), preferred_element_type=jnp.float32
    )
    grad_mixture = jnp.dot(back_attn, weight[3], preferred_element_type=jnp.float32).astype(
        jnp.bfloat16
    )
    grad_heads = lax.map(
        attend_back_clip,
        (
            heads_of(project[0], clip_count),
            heads_of(project[1], clip_count),
            heads_of(project[2], clip_count),
            heads_of(grad_mixture, clip_count),
        ),
    )
    grad_project = jnp.stack([piece.reshape(all_rows, -1) for piece in grad_heads])
    grad_qkv = jnp.einsum("rd,sre->sde", normed, grad_project, preferred_element_type=jnp.float32)

    def qkv_term(first_row, row_num):
        return jnp.einsum(
            "sre,sde->rd", grad_project, weight[0:3], preferred_element_type=jnp.float32
        )

    grad_normed = input_total(qkv_term, row_count)
    norm_out_one, norm_back_one = jax.vjp(layer_norm, stream, gain_one)
    part_in, grad_gain_one = norm_back_one(grad_normed)
    grad_matrix = jnp.concatenate([grad_qkv, grad_out_proj[None], grad_up, grad_down], axis=0)
    return (grad_resid + part_in, grad_matrix, grad_gain_one, grad_gain_two)


def masked_rows(mask_index, mask_count, row_count):
    positions = lax.iota(jnp.int32, SEQ)
    slots = lax.iota(jnp.int32, mask_index.shape[1])
    live = slots[None, :] < mask_count[:, None]
    hits = (mask_index[:, :, None] == positions[None, None, :]) & live[:, :, None]
    flag_all = jnp.any(hits, axis=1).astype(jnp.float32).reshape(-1)
    return lax.dynamic_slice_in_dim(flag_all, lax.axis_index("narrow") * row_count, row_count, 0)


def shards_general(
    patches,
    cotangent,
    mask_index,
    mask_count,
    weights,
    first_moment,
    second_moment,
    small_params,
    small_first,
    small_second,
):
    row_count = patches.shape[0]
    narrow_size = lax.axis_size("narrow")
    owned_rows = weights.shape[2]
    matrices, small_low = (
        lax.all_gather(weights.astype(jnp.bfloat16), "wide", axis=2, tiled=True),
        lax.all_gather(small_params.astype(jnp.bfloat16), "wide", axis=1, tiled=True),
    )
    gains = small_low.astype(jnp.float32)
    flags = masked_rows(mask_index, mask_count, row_count)[:, None]
    stream = patches.astype(jnp.float32) * (1.0 - flags) + flags * gains[2 * LAYERS][None, :]
    saved_all = []
    for layer_idx in range(LAYERS):
        stream, saved = forward_layer(
            stream, matrices[layer_idx], gains[2 * layer_idx], gains[2 * layer_idx + 1]
        )
        saved_all.append(saved)
    grad_stream = cotangent
    grad_mats = [None] * LAYERS
    grad_gains = [None] * (2 * LAYERS)
    for layer_idx in reversed(range(LAYERS)):
        (
            grad_stream,
            grad_mats[layer_idx],
            grad_gains[2 * layer_idx],
            grad_gains[2 * layer_idx + 1],
        ) = backward_layer(
            grad_stream,
            saved_all[layer_idx],
            matrices[layer_idx],
            gains[2 * layer_idx],
            gains[2 * layer_idx + 1],
        )
    input_grad = grad_stream * (1.0 - flags)
    grad_embed = jnp.sum(grad_stream * flags, axis=0)
    grad_small = jnp.stack(grad_gains + [grad_embed])
    grad_matrix = jnp.stack(grad_mats)
    first_col = lax.axis_index("wide") * owned_rows
    small_total = lax.psum(grad_small, ("wide", "narrow"))
    small_own = lax.dynamic_slice_in_dim(small_total, first_col, owned_rows, 1)
    matrix_total = lax.psum(grad_matrix, "wide")
    matrix_own = lax.dynamic_slice_in_dim(matrix_total, first_col, owned_rows, 2)
    local_square = jnp.sum(matrix_own * matrix_own) + jnp.sum(small_own * small_own) / narrow_size
    grad_norm = jnp.sqrt(lax.psum(local_square, ("wide", "narrow")))
    factor = jnp.minimum(1.0, CLIP_MAX / grad_norm)
    new_weights, new_first, new_second = adam_values(
        weights, first_moment, second_moment, matrix_own * factor, D ** (-0.5), DECAY_RATE
    )
    new_small, new_small_first, new_small_second = adam_values(
        small_params, small_first, small_second, small_own * factor, RATE_SMALL, 0.0
    )
    return (
        stream,
        input_grad,
        new_weights,
        new_first,
        new_second,
        new_small,
        new_small_first,
        new_small_second,
        grad_norm,
    )


def solution(mesh):
    in_specs = (
        P(("wide", "narrow"), None),
        P(("wide", "narrow"), None),
        P("wide", None),
        P("wide"),
        P(None, None, "wide", "narrow"),
        P(None, None, "wide", "narrow"),
        P(None, None, "wide", "narrow"),
        P(None, "wide"),
        P(None, "wide"),
        P(None, "wide"),
    )
    out_specs = (
        P(("wide", "narrow"), None),
        P(("wide", "narrow"), None),
        P(None, None, "wide", "narrow"),
        P(None, None, "wide", "narrow"),
        P(None, None, "wide", "narrow"),
        P(None, "wide"),
        P(None, "wide"),
        P(None, "wide"),
        P(),
    )
    fits = mesh.shape["wide"] == NZ * NX and mesh.shape["narrow"] == 4
    step = shards if fits else shards_general
    return jax.shard_map(step, mesh=mesh, in_specs=in_specs, out_specs=out_specs, check_vma=False)
```
